32 devices in a mesh: groups: 2 (over x), space: 16 (over z, y, core).
Axes of the slice: x: 2, y: 2, z: 4, core: 2. Of those that a mesh axis runs over, the one named last changes fastest.
Arguments:
- eigvecs: bfloat16 [2, 384, 3, 12288], P(None, None, None, ('groups', 'space')), parts along dimension 3, may hold values from -1.5 to 1.5
- momenta: int32 [4, 3], replicated, may hold values from -2 to 2
- peram: bfloat16 [32, 2, 384, 384], P(('groups', 'space')), parts along dimension 0, may hold values from -0.21875 to 0.21875
- graph: int32 [3072, 8], P(('groups', 'space')), parts along dimension 0, may hold values from 0 to 15, all different within a row; in each aligned block of 96 rows (0 to 95, 96 to 191, ...) at most 96 rows name the same one
Outputs:
- contracted: bfloat16 [3072, 8, 768], P(('groups', 'space')), parts along dimension 0
The draws below stay inside these ranges and needn't reach their ends.
There are 2 independent parts, one for each index of `groups`. The reference program is written for one: setup_inputs(seed, part) draws one part's arguments, and reference() takes and returns one part's arrays. A program takes and returns all parts, laid end to end along the dimension named above; an argument that names none is the same for every part. Nothing has to cross between parts.
Inputs may be any that keep to these rules, and one draw needn't show every extreme that they name: `graph`: each row names 8 different owners; among the rows of one device no owner is named more than 96 times, a bound that some block reaches.
All inputs are finite; a program needn't handle non-finite values.
Results may differ from the reference program's by a relative error of at most 0.0064.
Values may be sent and summed in bfloat16 or wider, within the bound.
A program may use at most 64 MiB of HBM per device.

```python
import math
import jax
import jax.numpy as jnp
import numpy as np
from jax import lax

N = 384
MOMENTA = 4
EXTENT = 128
SITES = 6144
ROWS = 1536
ROWS_DEV = 96
OWNERS = 16
FANOUT = 8
CAP = 96


def plant(entries, key, least, high):
    place = [jax.random.randint(jax.random.fold_in(key, axis), (), 0, length) for axis, length in enumerate(entries.shape)]
    widest = entries.shape.index(max(entries.shape))
    beside = place[:widest] + [(place[widest] + 1) % entries.shape[widest]] + place[widest + 1:]
    return entries.at[tuple(place)].set(least).at[tuple(beside)].set(high)


def with_spikes(values, rng, source, target, shards_of, factor):
    def block_of(position):
        return (jnp.arange(values.shape[position]) // (values.shape[position] // shards_of)).reshape((-1,) + (1,) * (values.ndim - 1 - position))

    near = jax.random.permutation(rng, shards_of)[block_of(target)]
    far = (block_of(target) + shards_of // 2) % shards_of
    return jnp.where((block_of(source) == near) | (block_of(source) == far), factor * values, values)


def block_scale(stream_key, shape, shards, least, high):
    gain = 1.0
    for axis_at, shards_of in shards:
        heights = jax.random.uniform(jax.random.fold_in(jax.random.fold_in(stream_key, 6), axis_at), (shards_of,), jnp.float32, least / len(shards), high / len(shards))
        gain = gain * jnp.repeat(jnp.exp(heights), shape[axis_at] // shards_of).reshape((-1,) + (1,) * (len(shape) - 1 - axis_at))
    return gain


def assign_block(rng, own, number, rows, number_of, top, most, skew):
    sequence = jax.random.permutation(rng, number_of)
    packed, ordinary = load_shares(number_of, rows * top, most, skew, True), load_shares(number_of, rows * top, most, skew, False)
    places = jnp.arange(number_of)

    def named(tallies, turn):
        used = int((tallies > 0).sum())
        fixed = max(1, used // 4)
        moved = fixed + (places - fixed + turn * (used - fixed)) % max(1, number_of - fixed)
        return jnp.zeros((number_of,), jnp.int32).at[sequence[jnp.where(places < fixed, places, moved)]].set(jnp.asarray(tallies, jnp.int32))

    tallies = jnp.where(number % 4 == 0, named(packed, number // 4), named(ordinary, number - number // 4 - 1))
    mixed = jax.random.permutation(jax.random.fold_in(own, 3), number_of)
    donor, sink = mixed[0:number_of // 2 * 2:2], mixed[1:number_of // 2 * 2:2]
    slack = jnp.minimum(tallies[donor] - 1, most - tallies[sink]) // 2
    slack = jnp.where((donor == sequence[0]) | (sink == sequence[0]) | (tallies[sink] == 0), 0, jnp.maximum(slack, 0))
    moved = jax.random.randint(jax.random.fold_in(own, 4), (number_of // 2,), 0, 1 << 20) % (slack + 1)
    tallies = tallies.at[donor].add(-moved).at[sink].add(moved)
    labels = jnp.searchsorted(jnp.cumsum(tallies), jnp.arange(rows * top), side="right").astype(jnp.int32)
    table = labels.reshape(top, rows).T
    table = table[jax.random.permutation(jax.random.fold_in(own, 1), rows)]
    turn = jax.random.randint(jax.random.fold_in(own, 2), (rows, 1), 0, top)
    return jnp.take_along_axis(table, (jnp.arange(top)[None, :] + turn) % top, axis=1)


def load_shares(count, total, bound, slope, full):
    weights = [(1 << 20) // math.isqrt(rank ** slope) + 1 for rank in range(1, count + 1)]
    largest = bound if full else min(bound, max(-(-total // count), total * weights[0] // sum(weights)))
    least = 1 if total - largest >= count - 1 else 0
    counts, spare = [largest] + [least] * (count - 1), total - largest - least * (count - 1)
    while spare > 0:
        movable = [i for i in range(1, count) if counts[i] < largest] or [i for i in range(1, count) if counts[i] < bound]
        mass, budget = sum([weights[i] for i in movable]), spare
        for i in movable:
            more = min(bound - counts[i], max(1, budget * weights[i] // mass), spare)
            counts[i] = counts[i] + more
            spare = spare - more
    return np.array(counts)


def gaussian(stream_key, shape, width, reach, pieces=(), kind=jnp.bfloat16):
    gain = block_scale(stream_key, shape, pieces, -0.22, 0.18) if pieces else 1.0
    drawn = jax.random.normal(stream_key, shape, jnp.float32) * width * gain
    return jnp.minimum(jnp.maximum(drawn, -reach), reach).astype(kind)


def noise_with(own_key, dims, width, reach, split, heavy, held_as=jnp.bfloat16):
    values = width * jax.random.normal(own_key, dims, jnp.float32)
    if split:
        values = values * block_scale(own_key, dims, split, -0.22, 0.18)
    return jnp.clip(with_spikes(values, jax.random.fold_in(own_key, 3), *heavy), -reach, reach).astype(held_as)


def setup_inputs(seed: int = 0, part: int = 0) -> dict:
    splits = jax.random.split(jax.random.key(seed), 5)
    part_splits = jax.random.split(jax.random.fold_in(splits[4], part), 5)
    eigvecs = noise_with(part_splits[0], (2, N, 3, SITES), ((6 * SITES) ** -0.25), 1.5, ((3, 16),), (3, 1, 16, 2.0))
    momenta = plant(jax.random.randint(splits[1], (MOMENTA, 3), -2, 3), jax.random.fold_in(splits[1], 1), -2, 2).astype(jnp.int32)
    peram = gaussian(part_splits[2], (OWNERS, 2, N, N), (2 * N) ** -0.5, 0.21875, ((0, 16),))
    graph_keys = jax.random.split(jax.random.fold_in(part_splits[3], 1), ROWS // ROWS_DEV)
    graph_turns = jax.random.permutation(jax.random.fold_in(part_splits[3], 3), ROWS // ROWS_DEV)
    graph = jax.vmap(lambda own, number: assign_block(jax.random.fold_in(part_splits[3], 2), own, number, ROWS_DEV, OWNERS, FANOUT, CAP, 2))(graph_keys, graph_turns).reshape((ROWS, FANOUT))
    return dict(eigvecs=eigvecs, momenta=momenta, peram=peram, graph=graph)


def phase_tables(momenta, site_index, extent):
    coord_x = site_index % extent
    coord_y = (site_index // extent) % extent
    coord_z = site_index // (extent * extent)
    wave_number = momenta[:, 0:1] * coord_x[None, :] + momenta[:, 1:2] * coord_y[None, :] + momenta[:, 2:3] * coord_z[None, :]
    wave_number = jnp.mod(wave_number, extent)
    phase_angle = wave_number.astype(jnp.float32) * (2.0 * math.pi / extent)
    return jnp.cos(phase_angle), jnp.sin(phase_angle)


def block_form(peram_pair):
    peram_re = peram_pair[0]
    peram_im = peram_pair[1]
    top_half = jnp.concatenate([peram_re, peram_im], axis=1)
    bottom_half = jnp.concatenate([-peram_im, peram_re], axis=1)
    return jnp.concatenate([top_half, bottom_half], axis=0)


def reference(eigvecs, momenta, peram, graph):
    num_vec = eigvecs.shape[1]
    num_sites = eigvecs.shape[3]
    site_index = jnp.arange(num_sites, dtype=jnp.int32)
    cosine, sine = phase_tables(momenta, site_index, EXTENT)
    vec_re = eigvecs[0].astype(jnp.float32)
    vec_im = eigvecs[1].astype(jnp.float32)
    right_side = jnp.concatenate([
        jnp.concatenate([eigvecs[0], -eigvecs[1]], axis=1),
        jnp.concatenate([eigvecs[1], eigvecs[0]], axis=1)], axis=0).reshape(2 * num_vec, 6 * num_sites)

    def one_momentum(tables):
        cos_row, sin_row = tables
        left_re = vec_re * cos_row - vec_im * sin_row
        left_im = -(vec_re * sin_row + vec_im * cos_row)
        left_cat = jnp.concatenate([left_re, left_im], axis=1).astype(jnp.bfloat16).reshape(num_vec, 6 * num_sites)
        return lax.dot_general(left_cat, right_side, (((1,), (1,)), ((), ())), preferred_element_type=jnp.float32)

    elementals = lax.map(one_momentum, (cosine, sine))
    elemental = elementals.reshape(-1, 2 * num_vec).astype(jnp.bfloat16)
    blocks = jax.vmap(block_form)(peram)
    fanout = graph.shape[1]
    row_blocks = elemental.reshape(-1, 16, 2 * num_vec)
    owner_blocks = graph.reshape(-1, 16, fanout)

    def contract(pair):
        row_group, owners = pair
        first_blocks = blocks[owners].astype(jnp.float32)
        second_blocks = blocks[jnp.bitwise_xor(owners, 1)].astype(jnp.float32)
        sinks = jnp.einsum('ra,rkab->rkb', row_group.astype(jnp.float32), first_blocks).astype(jnp.bfloat16)
        return jnp.einsum('rka,rkba->rkb', sinks.astype(jnp.float32), second_blocks).astype(jnp.bfloat16)

    result = lax.map(contract, (row_blocks, owner_blocks))
    return result.reshape(-1, fanout, 2 * num_vec)
```

```python
import functools
import math

import jax
import jax.numpy as jnp
from jax import lax
from jax.experimental import pallas as pl
from jax.experimental.pallas import tpu as pltpu
from jax.sharding import PartitionSpec as P

EXTENT = 128
VMEM_ROOM = 40 << 20
BF16 = jnp.bfloat16
F32 = jnp.float32


def partner(block, axis, bit):
    count = lax.axis_size(axis)
    route = []
    for low in range(count):
        high = low | 1 << bit
        if high != low and high < count:
            route += [(low, high), (high, low)]
    return lax.ppermute(block, axis, route)


def phase_tables(momenta, site_index, extent):
    coord_x = site_index % extent
    coord_y = site_index // extent % extent
    coord_z = site_index // (extent * extent)
    wave_number = (
        momenta[:, 0:1] * coord_x[None, :]
        + momenta[:, 1:2] * coord_y[None, :]
        + momenta[:, 2:3] * coord_z[None, :]
    )
    wave_number = jnp.mod(wave_number, extent)
    phase_angle = wave_number.astype(jnp.float32) * (2.0 * math.pi / extent)
    return (jnp.cos(phase_angle), jnp.sin(phase_angle))


def block_form(peram_pair):
    peram_re = peram_pair[0]
    peram_im = peram_pair[1]
    top_half = jnp.concatenate([peram_re, peram_im], axis=1)
    bottom_half = jnp.concatenate([-peram_im, peram_re], axis=1)
    return jnp.concatenate([top_half, bottom_half], axis=0)


def sink_product(arrived, block):
    return lax.dot_general(
        arrived, block, (((2,), (0,)), ((), ())), preferred_element_type=jnp.float32
    ).astype(jnp.bfloat16)


def adjoint_product(sinks, block):
    return lax.dot_general(
        sinks, block, (((2,), (1,)), ((), ())), preferred_element_type=jnp.float32
    ).astype(jnp.bfloat16)


def on_device(eigvecs, momenta, peram, graph):
    num_vec = eigvecs.shape[1]
    local_sites = eigvecs.shape[3]
    spaces = lax.axis_size("space")
    position = lax.axis_index("space")
    site_index = position * local_sites + jnp.arange(local_sites, dtype=jnp.int32)
    cosine, sine = phase_tables(momenta, site_index, EXTENT)
    total_rows = cosine.shape[0] * num_vec
    rows_here = total_rows // spaces
    right_side = jnp.concatenate(
        [
            jnp.concatenate([eigvecs[0], -eigvecs[1]], axis=1),
            jnp.concatenate([eigvecs[1], eigvecs[0]], axis=1),
        ],
        axis=0,
    ).reshape(2 * num_vec, 6 * local_sites)
    row_index = jnp.arange(rows_here * lax.axis_size("space"), dtype=jnp.int32)
    vector_index = row_index % num_vec
    momentum_index = row_index // num_vec
    vec_re = jnp.take(eigvecs[0], vector_index, axis=0).astype(jnp.float32)
    vec_im = jnp.take(eigvecs[1], vector_index, axis=0).astype(jnp.float32)
    cos_rows = jnp.take(cosine, momentum_index, axis=0)[:, None, :]
    sin_rows = jnp.take(sine, momentum_index, axis=0)[:, None, :]
    left_re = vec_re * cos_rows - vec_im * sin_rows
    left_im = -(vec_re * sin_rows + vec_im * cos_rows)
    left_cat = (
        jnp.concatenate([left_re, left_im], axis=1)
        .astype(jnp.bfloat16)
        .reshape(rows_here * lax.axis_size("space"), 6 * local_sites)
    )
    summed = lax.psum_scatter(
        lax.dot_general(
            left_cat, right_side, (((1,), (1,)), ((), ())), preferred_element_type=jnp.float32
        ),
        "space",
        scatter_dimension=0,
        tiled=True,
    )
    elemental = summed.astype(jnp.bfloat16)
    fanout = graph.shape[1]
    capacity = max(2, 2 * rows_here * fanout // spaces)
    flat_owner = graph.reshape(-1)
    entries = flat_owner.shape[0]
    onehot = (flat_owner[:, None] == jnp.arange(spaces, dtype=jnp.int32)[None, :]).astype(jnp.int32)
    earlier = jnp.cumsum(onehot, axis=0) - onehot
    slot = jnp.sum(earlier * onehot, axis=1)
    source_row = jnp.arange(entries, dtype=jnp.int32) // fanout
    payload = jnp.take(elemental, source_row, axis=0)
    outgoing = (
        jnp.zeros((spaces, capacity, 2 * num_vec), jnp.bfloat16).at[flat_owner, slot].set(payload)
    )
    own_block = block_form(peram[0])
    partner_block = partner(own_block, "space", 0)
    sinks = sink_product(
        lax.all_to_all(outgoing, "space", split_axis=0, concat_axis=0, tiled=True), own_block
    )
    finished = adjoint_product(sinks, partner_block)
    returned = lax.all_to_all(finished, "space", split_axis=0, concat_axis=0, tiled=True)
    collected = returned[flat_owner, slot]
    return collected.reshape(rows_here, fanout, 2 * num_vec)


NT = (((1,), (1,)), ((), ()))
NN = (((1,), (0,)), ((), ()))


def dot(a, b, dims):
    return lax.dot_general(a, b, dims, preferred_element_type=F32)


def fill_phases(mom_ref, cos_ref, sin_ref, first_site):
    count = cos_ref.shape[0]
    shape = (1, cos_ref.shape[1])
    bits = EXTENT.bit_length() - 1
    site = first_site + lax.broadcasted_iota(jnp.int32, shape, 1)
    coord_x = site & (EXTENT - 1)
    coord_y = (site >> bits) & (EXTENT - 1)
    coord_z = site >> (2 * bits)
    for q in range(count):
        wave = (mom_ref[q, 0] * coord_x + mom_ref[q, 1] * coord_y + mom_ref[q, 2] * coord_z) & (EXTENT - 1)
        angle = wave.astype(F32) * (2.0 * math.pi / EXTENT)
        cos_ref[q : q + 1, :] = jnp.cos(angle)
        sin_ref[q : q + 1, :] = jnp.sin(angle)


def fused_kernel(
    lines, wide, mom_ref, vec_hbm, peram_hbm, owner_ref, out_ref,
    vec_ref, cos_ref, sin_ref, pair, gath, prod, own, core_out, core_in, z_out, z_in, total, y_out, y_in, elem, results, picks,
    load_sem, pair_sem, core_sem, z_sem, y_sem, gath_send, gath_recv,
):
    colours, num_vec, local_sites = vec_ref.shape[1:]
    rows = own.shape[1]
    half = num_vec // 2
    me = lax.axis_index("space")
    core = me % 2
    chip = me // 2
    line = chip // wide
    column = chip % wide
    mate = chip * 2 + 1 - core
    other = 1 - column
    across = (line * wide + other) * 2 + core
    above = me + 2 * wide
    below = me - 2 * wide
    has_above = line < lines - 1
    has_below = line > 0

    def copy(src, dst, send, recv, to):
        return pltpu.make_async_remote_copy(
            src_ref=src, dst_ref=dst, send_sem=send, recv_sem=recv,
            device_id={"space": to}, device_id_type=pl.DeviceIdType.MESH,
        )

    barrier = pltpu.get_barrier_semaphore()

    def greet(to):
        pl.semaphore_signal(barrier, inc=1, device_id={"space": to}, device_id_type=pl.DeviceIdType.MESH)

    greet(mate)
    greet(across)
    load_own = pltpu.make_async_copy(peram_hbm, pair.at[core], load_sem.at[0])
    load_own.start()
    load_vec = pltpu.make_async_copy(vec_hbm, vec_ref, load_sem.at[1])
    load_vec.start()

    @pl.when(has_above)
    def _():
        greet(above)

    @pl.when(has_below)
    def _():
        greet(below)

    def core_copy(unit):
        return copy(core_out.at[unit], core_in.at[unit], core_sem.at[0, unit], core_sem.at[1, unit], mate)

    def unit_product(unit):
        first = unit * (2 * rows)
        momentum = first // num_vec
        start = pl.multiple_of(first % num_vec, 2 * rows)
        cosine = cos_ref[pl.ds(momentum, 1), :]
        sine = sin_ref[pl.ds(momentum, 1), :]
        left = []
        for colour in range(colours):
            v_re = vec_ref[0, colour, pl.ds(start, 2 * rows), :].astype(F32)
            v_im = vec_ref[1, colour, pl.ds(start, 2 * rows), :].astype(F32)
            left_re = (v_re * cosine - v_im * sine).astype(BF16)
            left_im = (-(v_re * sine + v_im * cosine)).astype(BF16)
            left.append(jnp.concatenate([left_re, left_im], axis=0))
        left = jnp.concatenate(left, axis=1)
        by_re = dot(left, jnp.concatenate([vec_ref[0, colour] for colour in range(colours)], axis=1), NT)
        by_im = dot(left, jnp.concatenate([vec_ref[1, colour] for colour in range(colours)], axis=1), NT)
        prod[:, :num_vec] = by_re[: 2 * rows] - by_im[2 * rows :]
        prod[:, num_vec:] = by_im[: 2 * rows] + by_re[2 * rows :]
        own[unit] = prod[pl.ds(pl.multiple_of(core * rows, rows), rows), :]
        core_out[unit] = prod[pl.ds(pl.multiple_of((1 - core) * rows, rows), rows), :].astype(BF16)

    def line_product(to_line):
        @pl.loop(0, wide)
        def _(col):
            unit_product(to_line * wide + col)
            core_copy(to_line * wide + col).start()

    lower = line < lines // 2

    def line_at(step):
        if step == lines - 1:
            return line
        down = lines - 1 - step
        down = jnp.where(down <= line, down - 1, down)
        up = jnp.where(step >= line, step + 1, step)
        return jnp.where(lower, down, up)

    def z_copy(to_line, col, to):
        way = jnp.where(to_line > line, 0, 1)
        return z_arrival(way, to_line, col, to)

    def z_arrival(way, to_line, col, to):
        return copy(
            z_out.at[to_line, col], z_in.at[way, to_line, col],
            z_sem.at[0, to_line, col], z_sem.at[1 + way, to_line, col], to,
        )

    def chip_sum(to_line, col):
        unit = to_line * wide + col
        core_copy(unit).wait_recv()
        return own[unit] + core_in[unit].astype(F32)

    def begin_line(step):
        to_line = line_at(step)
        upward = to_line > line
        first = jnp.where(upward, line == 0, line == lines - 1)

        @pl.when(first)
        def _():
            for col in range(wide):
                z_out[to_line, col] = chip_sum(to_line, col).astype(BF16)
                z_copy(to_line, col, jnp.where(upward, above, below)).start()

    def pass_on(step):
        to_line = line_at(step)
        upward = to_line > line
        way = jnp.where(upward, 0, 1)
        behind = jnp.where(upward, line > 0, line < lines - 1)

        @pl.when(behind)
        def _():
            for col in range(wide):
                z_arrival(way, to_line, col, mate).wait_recv()
                z_out[to_line, col] = (chip_sum(to_line, col) + z_in[way, to_line, col].astype(F32)).astype(BF16)
                z_copy(to_line, col, jnp.where(upward, above, below)).start()

    parts = gath.shape[2]

    def gather_copy(block, which, part, way, to):
        return copy(
            gath.at[block, which, part], gath.at[block, which, part],
            gath_send.at[way, block, part], gath_recv.at[block, which, part], to,
        )

    def gather_arrived(block, which, part):
        gather_copy(block, which, part, 0, mate).wait_recv()

    def forward(distance, part):
        low = line - distance
        high = line + distance

        @pl.when(low >= 0)
        def _():
            block = low * wide + column
            gather_arrived(block, core, part)

            @pl.when(has_above)
            def _():
                gather_copy(block, core, part, 0, above).start()

            gather_copy(block, core, part, 1, across).start()
            gather_copy(block, core, part, 2, mate).start()

        @pl.when(high < lines)
        def _():
            block = high * wide + column
            gather_arrived(block, core, part)

            @pl.when(has_below)
            def _():
                gather_copy(block, core, part, 0, below).start()

            gather_copy(block, core, part, 1, across).start()
            gather_copy(block, core, part, 2, mate).start()

    def relay(at):
        for part in range(parts):
            gather_arrived(at * wide + other, core, part)
            gather_copy(at * wide + other, core, part, 2, mate).start()

    def from_mate(block):
        for part in range(parts):
            gather_arrived(block, 1 - core, part)

    toward = 1 - 2 * (line // (lines // 2))

    def line_on(turn):
        return (line + toward * turn + lines) % lines

    group = results.shape[2]
    fanout = out_ref.shape[1]
    owners = results.shape[1]

    def make_picks():
        spread = lax.broadcasted_iota(jnp.int32, (rows * fanout, fanout), 0) % fanout
        spread = jnp.where(spread == lax.broadcasted_iota(jnp.int32, (rows * fanout, fanout), 1), 1.0, 0.0)
        named = dot(spread.astype(BF16), owner_ref[...].astype(F32).astype(BF16), NN)
        own_row = lax.broadcasted_iota(jnp.int32, named.shape, 0) // fanout
        at_row = own_row == lax.broadcasted_iota(jnp.int32, named.shape, 1)
        named = jnp.sum(jnp.where(at_row, named, 0.0), axis=1, keepdims=True)
        shape = (group * fanout, owners * group)
        of_row = lax.broadcasted_iota(jnp.int32, shape, 0) // fanout
        of_col = lax.broadcasted_iota(jnp.int32, shape, 1)
        same = of_row == of_col % group
        col_owner = (of_col // group).astype(F32)
        for g in range(rows // group):
            chosen = named[g * group * fanout : (g + 1) * group * fanout, :] == col_owner
            picks[g] = jnp.where(same & chosen, 1.0, 0.0).astype(BF16)

    fill_phases(mom_ref, cos_ref, sin_ref, me * local_sites)
    peers = 2 + jnp.where(has_above, 1, 0) + jnp.where(has_below, 1, 0)
    pl.semaphore_wait(barrier, peers)
    pair_copy = copy(peram_hbm, pair.at[core], pair_sem.at[0], pair_sem.at[1], mate)
    pair_copy.start()
    load_vec.wait()
    unit_product(line_at(0) * wide)
    core_copy(line_at(0) * wide).start()

    @pl.loop(1, wide)
    def _(col):
        unit_product(line_at(0) * wide + col)
        core_copy(line_at(0) * wide + col).start()

    load_own.wait()
    pair_copy.wait_recv()
    mine_rows = pl.ds(pl.multiple_of(core * half, half), half)
    lefts = jnp.concatenate([pair[0, 0, mine_rows, :], pair[0, 1, mine_rows, :]], axis=0)
    by_re = dot(lefts, pair[1, 0], NT)
    by_im = dot(lefts, pair[1, 1], NT)
    gath[chip, core, 0] = (by_re[:half] + by_im[half:]).astype(BF16)
    gath[chip, core, 1] = (by_re[half:] - by_im[:half]).astype(BF16)
    for part in range(parts):

        @pl.when(has_above)
        def _():
            gather_copy(chip, core, part, 0, above).start()

        @pl.when(has_below)
        def _():
            gather_copy(chip, core, part, 3, below).start()

        gather_copy(chip, core, part, 1, across).start()
        gather_copy(chip, core, part, 2, mate).start()

    for step in range(1, lines):
        if step == lines - 1:
            forward(1, 0)
        line_product(line_at(step))
        begin_line(step - 1)
    for part in range(1, parts):
        forward(1, part)
    relay(line)
    for step in range(1, lines):
        if step < lines - 1:
            for part in range(parts):
                forward(step + 1, part)
            pass_on(step - 1)
    for turn in range(1, lines - 2):
        relay(line_on(turn))
    pass_on(lines - 2)
    for col in range(wide):
        total[col] = chip_sum(line, col)

    @pl.when(has_below)
    def _():
        for col in range(wide):
            z_arrival(0, line, col, mate).wait_recv()
            total[col] += z_in[0, line, col].astype(F32)

    @pl.when(has_above)
    def _():
        for col in range(wide):
            z_arrival(1, line, col, mate).wait_recv()
            total[col] += z_in[1, line, col].astype(F32)

    y_out[...] = total[other].astype(BF16)
    y_copy = copy(y_out, y_in, y_sem.at[0], y_sem.at[1], across)
    y_copy.start()
    make_picks()
    for turn in range(max(1, lines - 2), lines - 1):
        relay(line_on(turn))
    y_copy.wait_recv()
    row = (total[column] + y_in[...].astype(F32)).astype(BF16)
    elem[:rows] = row[:, :num_vec]
    elem[rows:] = row[:, num_vec:]

    def put(owner, re, im):
        sixteen = results.shape[2]
        results[:, owner, :, :num_vec] = re.astype(BF16).reshape(rows // sixteen, sixteen, num_vec)
        results[:, owner, :, num_vec:] = im.astype(BF16).reshape(rows // sixteen, sixteen, num_vec)

    def contract(block):
        m_re = jnp.concatenate([gath[block, 0, 0], gath[block, 1, 0]], axis=0)
        m_im = jnp.concatenate([gath[block, 0, 1], gath[block, 1, 1]], axis=0)
        e = elem[...]
        by_re = dot(e, m_re, NN)
        by_im = dot(e, m_im, NN)
        put(2 * block, by_re[:rows] - by_im[rows:], by_im[:rows] + by_re[rows:])
        by_re = dot(e, m_re, NT)
        by_im = dot(e, m_im, NT)
        put(2 * block + 1, by_re[:rows] + by_im[rows:], by_re[rows:] - by_im[:rows])

    @pl.loop(0, lines)
    def _(turn):
        at = line_on(turn)
        mine = at * wide + column
        theirs = at * wide + other

        @pl.when(turn == 1)
        def _():
            relay(line_on(lines - 1))

        from_mate(mine)
        contract(mine)
        from_mate(theirs)
        contract(theirs)

    for g in range(rows // group):
        rows_out = dot(picks[g], results[g].reshape(owners * group, 2 * num_vec), NN)
        out_ref[g * group : (g + 1) * group] = rows_out.reshape(group, fanout, 2 * num_vec).astype(BF16)

    pair_copy.wait_send()
    y_copy.wait_send()

    @pl.loop(0, lines * wide)
    def _(unit):
        core_copy(unit).wait_send()
        for part in range(parts):
            gather_copy(unit, core, part, 2, mate).wait_send()

    @pl.loop(0, lines)
    def _(at):
        @pl.when(at != line)
        def _():
            for col in range(wide):
                z_copy(at, col, mate).wait_send()

        for part in range(parts):
            gather_copy(at * wide + column, core, part, 1, across).wait_send()

        @pl.when(((at <= line) & has_above) | ((at > line) & has_below))
        def _():
            for part in range(parts):
                gather_copy(at * wide + column, core, part, 0, above).wait_send()

    @pl.when(has_below)
    def _():
        for part in range(parts):
            gather_copy(chip, core, part, 3, below).wait_send()


def fused_on_device(eigvecs, momenta, peram, graph):
    num_vec, colours, local_sites = eigvecs.shape[1:]
    spaces = lax.axis_size("space")
    wide = 2
    lines = spaces // (2 * wide)
    chips = lines * wide
    rows, fanout = graph.shape
    group = 16
    vectors = jnp.transpose(eigvecs, (0, 2, 1, 3))
    half = num_vec // 2
    dma = pltpu.SemaphoreType.DMA
    return pl.pallas_call(
        functools.partial(fused_kernel, lines, wide),
        out_shape=pltpu.VMEM((rows, fanout, 2 * num_vec), BF16),
        in_specs=[
            pl.BlockSpec(memory_space=pltpu.SMEM),
            pl.BlockSpec(memory_space=pltpu.HBM),
            pl.BlockSpec(memory_space=pltpu.HBM),
            pl.BlockSpec(memory_space=pltpu.VMEM),
        ],
        out_specs=pl.BlockSpec(memory_space=pltpu.VMEM),
        scratch_shapes=[
            pltpu.VMEM((2, colours, num_vec, local_sites), BF16),
            pltpu.VMEM((momenta.shape[0], local_sites), F32),
            pltpu.VMEM((momenta.shape[0], local_sites), F32),
            pltpu.VMEM((2, 2, num_vec, num_vec), BF16),
            pltpu.VMEM((chips, 2, 2, half, num_vec), BF16),
            pltpu.VMEM((2 * rows, 2 * num_vec), F32),
            pltpu.VMEM((chips, rows, 2 * num_vec), F32),
            pltpu.VMEM((chips, rows, 2 * num_vec), BF16),
            pltpu.VMEM((chips, rows, 2 * num_vec), BF16),
            pltpu.VMEM((lines, wide, rows, 2 * num_vec), BF16),
            pltpu.VMEM((2, lines, wide, rows, 2 * num_vec), BF16),
            pltpu.VMEM((wide, rows, 2 * num_vec), F32),
            pltpu.VMEM((rows, 2 * num_vec), BF16),
            pltpu.VMEM((rows, 2 * num_vec), BF16),
            pltpu.VMEM((2 * rows, num_vec), BF16),
            pltpu.VMEM((rows // group, spaces, group, 2 * num_vec), BF16),
            pltpu.VMEM((rows // group, group * fanout, spaces * group), BF16),
            dma((2,)),
            dma((2,)),
            dma((2, chips)),
            dma((3, lines, wide)),
            dma((2,)),
            dma((4, chips, 2)),
            dma((chips, 2, 2)),
        ],
        compiler_params=pltpu.CompilerParams(
            collective_id=0, has_side_effects=True, vmem_limit_bytes=VMEM_ROOM + (16 << 20)
        ),
    )(momenta, vectors, peram[0], graph.T)


def fits(mesh, eigvecs, momenta, graph):
    num_vec = eigvecs.shape[1]
    spaces = mesh.shape["space"]
    rows = momenta.shape[0] * num_vec // spaces
    return (
        spaces % 8 == 0
        and spaces <= 256
        and rows % 16 == 0
        and num_vec % (2 * rows) == 0
        and num_vec % 128 == 0
        and spaces * 2 * num_vec * num_vec + 14 * spaces * rows * 2 * num_vec <= VMEM_ROOM
    )


def solution(mesh):
    placed = (
        P(None, None, None, ("groups", "space")),
        P(),
        P(("groups", "space"), None, None, None),
        P(("groups", "space"), None),
    )

    def whole(eigvecs, momenta, peram, graph):
        body = fused_on_device if fits(mesh, eigvecs, momenta, graph) else on_device
        return jax.shard_map(
            body,
            mesh=mesh,
            in_specs=placed,
            out_specs=P(("groups", "space"), None, None),
            check_vma=False,
        )(eigvecs, momenta, peram, graph)

    return whole
```

```python
import functools
import math

import jax
import jax.numpy as jnp
from jax import lax
from jax.experimental import pallas as pl
from jax.experimental.pallas import tpu as pltpu
from jax.sharding import PartitionSpec as P

EXTENT = 128
VMEM_ROOM = 40 << 20
BF16 = jnp.bfloat16
F32 = jnp.float32


def partner(block, axis, bit):
    count = lax.axis_size(axis)
    route = []
    for low in range(count):
        high = low | 1 << bit
        if high != low and high < count:
            route += [(low, high), (high, low)]
    return lax.ppermute(block, axis, route)


def phase_tables(momenta, site_index, extent):
    coord_x = site_index % extent
    coord_y = site_index // extent % extent
    coord_z = site_index // (extent * extent)
    wave_number = (
        momenta[:, 0:1] * coord_x[None, :]
        + momenta[:, 1:2] * coord_y[None, :]
        + momenta[:, 2:3] * coord_z[None, :]
    )
    wave_number = jnp.mod(wave_number, extent)
    phase_angle = wave_number.astype(jnp.float32) * (2.0 * math.pi / extent)
    return (jnp.cos(phase_angle), jnp.sin(phase_angle))


def block_form(peram_pair):
    peram_re = peram_pair[0]
    peram_im = peram_pair[1]
    top_half = jnp.concatenate([peram_re, peram_im], axis=1)
    bottom_half = jnp.concatenate([-peram_im, peram_re], axis=1)
    return jnp.concatenate([top_half, bottom_half], axis=0)


def sink_product(arrived, block):
    return lax.dot_general(
        arrived, block, (((2,), (0,)), ((), ())), preferred_element_type=jnp.float32
    ).astype(jnp.bfloat16)


def adjoint_product(sinks, block):
    return lax.dot_general(
        sinks, block, (((2,), (1,)), ((), ())), preferred_element_type=jnp.float32
    ).astype(jnp.bfloat16)


def on_device(eigvecs, momenta, peram, graph):
    num_vec = eigvecs.shape[1]
    local_sites = eigvecs.shape[3]
    spaces = lax.axis_size("space")
    position = lax.axis_index("space")
    site_index = position * local_sites + jnp.arange(local_sites, dtype=jnp.int32)
    cosine, sine = phase_tables(momenta, site_index, EXTENT)
    total_rows = cosine.shape[0] * num_vec
    rows_here = total_rows // spaces
    right_side = jnp.concatenate(
        [
            jnp.concatenate([eigvecs[0], -eigvecs[1]], axis=1),
            jnp.concatenate([eigvecs[1], eigvecs[0]], axis=1),
        ],
        axis=0,
    ).reshape(2 * num_vec, 6 * local_sites)
    row_index = jnp.arange(rows_here * lax.axis_size("space"), dtype=jnp.int32)
    vector_index = row_index % num_vec
    momentum_index = row_index // num_vec
    vec_re = jnp.take(eigvecs[0], vector_index, axis=0).astype(jnp.float32)
    vec_im = jnp.take(eigvecs[1], vector_index, axis=0).astype(jnp.float32)
    cos_rows = jnp.take(cosine, momentum_index, axis=0)[:, None, :]
    sin_rows = jnp.take(sine, momentum_index, axis=0)[:, None, :]
    left_re = vec_re * cos_rows - vec_im * sin_rows
    left_im = -(vec_re * sin_rows + vec_im * cos_rows)
    left_cat = (
        jnp.concatenate([left_re, left_im], axis=1)
        .astype(jnp.bfloat16)
        .reshape(rows_here * lax.axis_size("space"), 6 * local_sites)
    )
    summed = lax.psum_scatter(
        lax.dot_general(
            left_cat, right_side, (((1,), (1,)), ((), ())), preferred_element_type=jnp.float32
        ),
        "space",
        scatter_dimension=0,
        tiled=True,
    )
    elemental = summed.astype(jnp.bfloat16)
    fanout = graph.shape[1]
    capacity = max(2, 2 * rows_here * fanout // spaces)
    flat_owner = graph.reshape(-1)
    entries = flat_owner.shape[0]
    onehot = (flat_owner[:, None] == jnp.arange(spaces, dtype=jnp.int32)[None, :]).astype(jnp.int32)
    earlier = jnp.cumsum(onehot, axis=0) - onehot
    slot = jnp.sum(earlier * onehot, axis=1)
    source_row = jnp.arange(entries, dtype=jnp.int32) // fanout
    payload = jnp.take(elemental, source_row, axis=0)
    outgoing = (
        jnp.zeros((spaces, capacity, 2 * num_vec), jnp.bfloat16).at[flat_owner, slot].set(payload)
    )
    own_block = block_form(peram[0])
    partner_block = partner(own_block, "space", 0)
    sinks = sink_product(
        lax.all_to_all(outgoing, "space", split_axis=0, concat_axis=0, tiled=True), own_block
    )
    finished = adjoint_product(sinks, partner_block)
    returned = lax.all_to_all(finished, "space", split_axis=0, concat_axis=0, tiled=True)
    collected = returned[flat_owner, slot]
    return collected.reshape(rows_here, fanout, 2 * num_vec)


NT = (((1,), (1,)), ((), ()))
NN = (((1,), (0,)), ((), ()))


def dot(a, b, dims):
    return lax.dot_general(a, b, dims, preferred_element_type=F32)


def fill_phases(mom_ref, cos_ref, sin_ref, first_site):
    count = cos_ref.shape[0]
    shape = (1, cos_ref.shape[1])
    bits = EXTENT.bit_length() - 1
    site = first_site + lax.broadcasted_iota(jnp.int32, shape, 1)
    coord_x = site & (EXTENT - 1)
    coord_y = (site >> bits) & (EXTENT - 1)
    coord_z = site >> (2 * bits)
    for q in range(count):
        wave = (mom_ref[q, 0] * coord_x + mom_ref[q, 1] * coord_y + mom_ref[q, 2] * coord_z) & (EXTENT - 1)
        angle = wave.astype(F32) * (2.0 * math.pi / EXTENT)
        cos_ref[q : q + 1, :] = jnp.cos(angle)
        sin_ref[q : q + 1, :] = jnp.sin(angle)


def fused_kernel(
    lines, wide, mom_hbm, vec_hbm, peram_hbm, owner_hbm, out_ref,
    mom_ref, vec_ref, owner_ref, cos_ref, sin_ref, pair, gath, prod, own, core_out, core_in, z_out, z_in, total, y_out, y_in,
    lhs, results, picks, load_sem, send_sem, pair_recv, core_recv, z_recv, y_recv, gath_recv, mate_recv,
):
    colours, num_vec, local_sites = vec_ref.shape[1:]
    rows = own.shape[1]
    half = num_vec // 2
    me = lax.axis_index("space")
    core = me % 2
    chip = me // 2
    line = chip // wide
    column = chip % wide
    mate = chip * 2 + 1 - core
    other = 1 - column
    across = (line * wide + other) * 2 + core
    above = me + 2 * wide
    below = me - 2 * wide
    has_above = line < lines - 1
    has_below = line > 0

    def copy(src, dst, send, recv, to):
        return pltpu.make_async_remote_copy(
            src_ref=src, dst_ref=dst, send_sem=send, recv_sem=recv,
            device_id={"space": to}, device_id_type=pl.DeviceIdType.MESH,
        )

    barrier = pltpu.get_barrier_semaphore()

    def greet(to):
        pl.semaphore_signal(barrier, inc=1, device_id={"space": to}, device_id_type=pl.DeviceIdType.MESH)

    greet(mate)
    greet(across)

    @pl.when(has_above)
    def _():
        greet(above)

    @pl.when(has_below)
    def _():
        greet(below)

    loads = [
        pltpu.make_async_copy(src, dst, load_sem.at[place])
        for place, (src, dst) in enumerate(
            [(mom_hbm, mom_ref), (peram_hbm, pair.at[core]), (vec_hbm, vec_ref), (owner_hbm, owner_ref)]
        )
    ]
    for load in loads:
        load.start()
    load_mom, load_own, load_vec, load_owner = loads
    UP, ACROSS, MATE, DOWN, CORES, LINES, TOTALS, PAIR = range(8)

    def core_copy(unit):
        return copy(core_out.at[unit], core_in.at[unit], send_sem.at[CORES], core_recv.at[unit], mate)

    def unit_product(unit):
        first = unit * (2 * rows)
        momentum = first // num_vec
        start = pl.multiple_of(first % num_vec, 2 * rows)
        cosine = cos_ref[pl.ds(momentum, 1), :]
        sine = sin_ref[pl.ds(momentum, 1), :]
        left = []
        for colour in range(colours):
            v_re = vec_ref[0, colour, pl.ds(start, 2 * rows), :].astype(F32)
            v_im = vec_ref[1, colour, pl.ds(start, 2 * rows), :].astype(F32)
            left_re = (v_re * cosine - v_im * sine).astype(BF16)
            left_im = (-(v_re * sine + v_im * cosine)).astype(BF16)
            left.append(jnp.concatenate([left_re, left_im], axis=0))
        left = jnp.concatenate(left, axis=1)
        by_re = dot(left, jnp.concatenate([vec_ref[0, colour] for colour in range(colours)], axis=1), NT)
        by_im = dot(left, jnp.concatenate([vec_ref[1, colour] for colour in range(colours)], axis=1), NT)
        prod[:, :num_vec] = by_re[: 2 * rows] - by_im[2 * rows :]
        prod[:, num_vec:] = by_im[: 2 * rows] + by_re[2 * rows :]
        own[unit] = prod[pl.ds(pl.multiple_of(core * rows, rows), rows), :]
        core_out[unit] = prod[pl.ds(pl.multiple_of((1 - core) * rows, rows), rows), :].astype(BF16)

    lower = line < lines // 2
    below_count = line
    above_count = lines - 1 - line
    at_end = (line == 0) | (line == lines - 1)
    toward = jnp.where(lower, 1, -1)

    def line_at(step):
        if step == lines - 1:
            return line
        down = lines - 1 - step
        down = jnp.where(down <= line, down - 1, down)
        up = jnp.where(step >= line, step + 1, step)
        return jnp.where(lower, down, up)

    def column_at(piece):
        return jnp.where(piece == 0, other, column)

    def product_at(step, piece):
        unit = line_at(step) * wide + column_at(piece)
        unit_product(unit)
        core_copy(unit).start()

    share = rows // 2

    def z_copy(way, to_line, col, piece, to):
        span = pl.ds(piece * share, share)
        return copy(
            z_out.at[to_line, col, span], z_in.at[way, to_line, col, span],
            send_sem.at[LINES], z_recv.at[z_place(way, to_line, line + (1 - 2 * way)), col, piece], to,
        )

    def z_place(way, to_line, at):
        return jnp.where(to_line == at, lines, to_line) if way else to_line

    def z_arrived(way, to_line, col, piece):
        span = pl.ds(piece * share, share)
        copy(
            z_out.at[to_line, col, span], z_in.at[way, to_line, col, span],
            send_sem.at[LINES], z_recv.at[z_place(way, to_line, line), col, piece], mate,
        ).wait_recv()

    def chip_sum(to_line, col, span):
        unit = to_line * wide + col
        return own[unit, span] + core_in[unit, span].astype(F32)

    def mate_sent(to_line, col):
        core_copy(to_line * wide + col).wait_recv()

    def spans():
        return [(piece, pl.ds(piece * share, share)) for piece in range(2)]

    def begin(step, piece):
        to_line = line_at(step)
        col = column_at(piece)

        def send(way, to):
            mate_sent(to_line, col)
            for part, span in spans():
                z_out[to_line, col, span] = chip_sum(to_line, col, span).astype(BF16)
                z_copy(way, to_line, col, part, to).start()

        @pl.when(line == 0)
        def _():
            send(0, above)

        @pl.when(line == lines - 1)
        def _():
            send(1, below)

    def pass_on(way, to_line, piece, to):
        col = column_at(piece)
        mate_sent(to_line, col)
        for part, span in spans():
            z_arrived(way, to_line, col, part)
            before = z_in[way, to_line, col, span].astype(F32)
            z_out[to_line, col, span] = (chip_sum(to_line, col, span) + before).astype(BF16)
            z_copy(way, to_line, col, part, to).start()

    parts = gath.shape[2]

    def gather_copy(block, part, way, to):
        there = gath.at[block, core, part]
        recv = mate_recv.at[block] if way == MATE else gath_recv.at[block, part]
        return copy(there, there, send_sem.at[way], recv, to)

    def gather_arrived(block, part):
        gather_copy(block, part, ACROSS, across).wait_recv()

    def from_mate(block):
        there = gath.at[block, 1 - core]
        copy(there, there, send_sem.at[MATE], mate_recv.at[block], mate).wait_recv()

    def spread(at, part, onward, way, to, hold):
        block = at * wide + column
        gather_arrived(block, part)

        @pl.when(onward)
        def _():
            gather_copy(block, part, way, to).start()

        @pl.when(jnp.logical_not(hold))
        def _():
            gather_copy(block, part, ACROSS, across).start()

        gather_copy(block, part, MATE, mate).start()

    def nth_line(turn):
        inner = jnp.where(turn == 2, -1, jnp.where(turn == 3, 2, turn))
        return line + toward * jnp.where(at_end, turn, inner)

    def relay(nth):
        ends = toward * (nth // 2)
        inner = [0, 0, -1, 1, toward, 2 * toward, -toward, 2 * toward][nth]
        part = jnp.where(at_end, nth % 2, [0, 1, 0, 0, 1, 0, 1, 1][nth])
        block = (line + jnp.where(at_end, ends, inner)) * wide + other
        gather_arrived(block, part)
        gather_copy(block, part, MATE, mate).start()

    def arrivals(turn, count):
        tail = 2 * count - 1
        first = (turn == tail + 1) | (turn == tail + 2)
        is_block = (count > 0) & ((turn <= tail) | (turn == tail + 3))
        back = jnp.where(turn < tail, (turn + 1) // 2, count)
        ahead = jnp.where(first, lines - 1 - count, lines - (turn + 1) // 2)
        part = jnp.where(turn <= tail, (turn - 1) % 2, jnp.where(first, turn - tail - 1, jnp.where(turn == tail + 3, 1, (turn - 1) % 2)))
        is_sum = (count > 0) & jnp.logical_not(is_block) & (ahead > 0)
        return is_block, is_sum, back, ahead, part

    def held(at, part):
        return (at == line + toward * jnp.where(at_end, lines - 1, 2)) & (part == jnp.where(at_end, 0, 1))

    def slot(turn):
        is_block, is_sum, back, ahead, part = arrivals(turn, below_count)

        @pl.when(is_block)
        def _():
            spread(line - back, part, has_above, UP, above, held(line - back, part))

        @pl.when(is_sum)
        def _():
            pass_on(0, line + ahead, part, above)

        is_block_, is_sum_, back_, ahead_, part_ = arrivals(turn, above_count)

        @pl.when(is_block_)
        def _():
            spread(line + back_, part_, has_below, DOWN, below, held(line + back_, part_))

        @pl.when(is_sum_)
        def _():
            pass_on(1, line - ahead_, part_, below)

    def line_total(piece, after=None):
        col = column_at(piece)
        mate_sent(line, col)
        for part, span in spans():
            total[col, span] = chip_sum(line, col, span)

            @pl.when(has_below)
            def _():
                z_arrived(0, line, col, part)
                total[col, span] += z_in[0, line, col, span].astype(F32)

            @pl.when(has_above)
            def _():
                z_arrived(1, line, col, part)
                total[col, span] += z_in[1, line, col, span].astype(F32)

            if after is not None:
                after(part, span)

    def y_copy(part, span):
        return copy(y_out.at[span], y_in.at[span], send_sem.at[TOTALS], y_recv.at[part], across)

    def send_across(part, span):
        y_out[span] = total[other, span].astype(BF16)
        y_copy(part, span).start()

    group = results.shape[2]
    fanout = out_ref.shape[1]
    owners = results.shape[1]

    def make_picks():
        spread = lax.broadcasted_iota(jnp.int32, (rows * fanout, fanout), 0) % fanout
        spread = jnp.where(spread == lax.broadcasted_iota(jnp.int32, (rows * fanout, fanout), 1), 1.0, 0.0)
        named = dot(spread.astype(BF16), owner_ref[...].astype(F32).astype(BF16), NN)
        own_row = lax.broadcasted_iota(jnp.int32, named.shape, 0) // fanout
        at_row = own_row == lax.broadcasted_iota(jnp.int32, named.shape, 1)
        named = jnp.sum(jnp.where(at_row, named, 0.0), axis=1, keepdims=True)
        shape = (group * fanout, owners * group)
        of_row = lax.broadcasted_iota(jnp.int32, shape, 0) // fanout
        of_col = lax.broadcasted_iota(jnp.int32, shape, 1)
        same = of_row == of_col % group
        col_owner = (of_col // group).astype(F32)
        for g in range(rows // group):
            chosen = named[g * group * fanout : (g + 1) * group * fanout, :] == col_owner
            picks[g] = jnp.where(same & chosen, 1.0, 0.0).astype(BF16)

    peers = 2 + jnp.where(has_above, 1, 0) + jnp.where(has_below, 1, 0)
    with jax.named_scope("greet"):
        pl.semaphore_wait(barrier, peers)
    pair_copy = copy(peram_hbm, pair.at[core], send_sem.at[PAIR], pair_recv.at[0], mate)
    pair_copy.start()
    load_mom.wait()
    fill_phases(mom_ref, cos_ref, sin_ref, me * local_sites)
    load_own.wait()
    with jax.named_scope("pair"):
        pair_copy.wait_recv()
    mine_rows = pl.ds(pl.multiple_of(core * half, half), half)
    with jax.named_scope("block"):
        lefts = jnp.concatenate([pair[0, 0, mine_rows, :], pair[0, 1, mine_rows, :]], axis=0)
        by_re = dot(lefts, pair[1, 0], NT)
        by_im = dot(lefts, pair[1, 1], NT)
        gath[chip, core, 0] = (by_re[:half] + by_im[half:]).astype(BF16)
        gath[chip, core, 1] = (by_re[half:] - by_im[:half]).astype(BF16)
    def send_own(part):
        @pl.when(has_above)
        def _():
            gather_copy(chip, part, UP, above).start()

        @pl.when(has_below)
        def _():
            gather_copy(chip, part, DOWN, below).start()

    for part in range(parts):
        gather_copy(chip, part, ACROSS, across).start()
    send_own(0)

    @pl.when(jnp.logical_not(at_end))
    def _():
        send_own(1)

    for part in range(parts):
        gather_copy(chip, part, MATE, mate).start()

    def named_product(step, piece):
        with jax.named_scope(f"unit{step}{piece}"):
            product_at(step, piece)

    def named_slot(turn):
        with jax.named_scope(f"slot{turn}"):
            slot(turn)
            relay(turn - 1)

    with jax.named_scope("load"):
        load_vec.wait()
    named_product(0, 0)
    named_product(0, 1)
    begin(0, 0)
    named_product(1, 0)
    begin(0, 1)

    @pl.when(at_end)
    def _():
        send_own(1)

    named_slot(1)
    named_product(1, 1)
    named_product(2, 0)
    begin(1, 0)
    begin(1, 1)
    named_slot(2)
    named_product(2, 1)
    named_product(3, 0)
    begin(2, 0)
    begin(2, 1)
    named_slot(3)
    named_product(3, 1)
    load_owner.wait()
    with jax.named_scope("picks"):
        make_picks()
    named_slot(4)
    named_slot(5)
    named_slot(6)
    farthest = nth_line(lines - 1) * wide + column

    @pl.when(at_end)
    def _():
        with jax.named_scope("total0"):
            line_total(0, send_across)

    with jax.named_scope("slot7"):
        slot(7)

    @pl.when(at_end)
    def _():
        with jax.named_scope("total1"):
            line_total(1)
        gather_copy(farthest, 0, ACROSS, across).start()

    @pl.when(jnp.logical_not(at_end))
    def _():
        with jax.named_scope("total0"):
            relay(6)
            line_total(0, send_across)
        with jax.named_scope("total1"):
            line_total(1)
        gather_copy(farthest, 1, ACROSS, across).start()

    with jax.named_scope("across"):
        for part, span in spans():
            y_copy(part, span).wait_recv()
    row = (total[column] + y_in[...].astype(F32)).astype(BF16)
    row_re = row[:, :num_vec]
    row_im = row[:, num_vec:]
    lhs[0, :rows] = jnp.concatenate([row_re, -row_im], axis=1)
    lhs[0, rows:] = jnp.concatenate([row_im, row_re], axis=1)
    lhs[1, :rows] = row
    lhs[1, rows:] = jnp.concatenate([row_im, -row_re], axis=1)

    def put(owner, re, im):
        sixteen = results.shape[2]
        results[:, owner, :, :num_vec] = re.astype(BF16).reshape(rows // sixteen, sixteen, num_vec)
        results[:, owner, :, num_vec:] = im.astype(BF16).reshape(rows // sixteen, sixteen, num_vec)

    def contract(block):
        high = jnp.concatenate([gath[block, 0, 0], gath[block, 1, 0], gath[block, 0, 1], gath[block, 1, 1]], axis=0)
        by = dot(lhs[0], high, NN)
        put(2 * block, by[:rows], by[rows:])
        broad = [jnp.concatenate([gath[block, which, 0], gath[block, which, 1]], axis=1) for which in range(2)]
        by = dot(lhs[1], jnp.concatenate(broad, axis=0), NT)
        put(2 * block + 1, by[:rows], by[rows:])

    @pl.loop(0, 2 * lines)
    def _(turn):
        @pl.when(at_end & (turn == 2 * lines - 3))
        def _():
            with jax.named_scope("slot8"):
                slot(2 * lines)
                relay(2 * lines - 2)

        @pl.when(turn == jnp.where(at_end, 2 * lines - 1, 2 * lines - 2))
        def _():
            with jax.named_scope("last"):
                relay(2 * lines - 1)

        late = turn >= 2 * lines - 2
        near = jnp.where(late, turn % 2 == 0, turn < lines - 1)
        nth = jnp.where(late, lines - 1, turn % (lines - 1))
        block = nth_line(nth) * wide + jnp.where(near, column, other)
        with jax.named_scope("mate"):
            from_mate(block)
        with jax.named_scope("contract"):
            contract(block)

    for g in range(rows // group):
        rows_out = dot(picks[g], results[g].reshape(owners * group, 2 * num_vec), NN)
        out_ref[g * group : (g + 1) * group] = rows_out.reshape(group, fanout, 2 * num_vec).astype(BF16)

    def all_sent(what, way):
        copy(what, what, send_sem.at[way], core_recv.at[0], mate).wait_send()

    pair_copy.wait_send()
    all_sent(core_out, CORES)
    all_sent(z_out.at[pl.ds(0, lines - 1)], LINES)
    all_sent(y_out, TOTALS)
    all_sent(gath.at[pl.ds(0, lines), core], ACROSS)
    all_sent(gath.at[:, core], MATE)
    for count in range(1, lines):

        @pl.when(line == count - 1)
        def _():
            all_sent(gath.at[pl.ds(0, count), core], UP)

        @pl.when(line == lines - count)
        def _():
            all_sent(gath.at[pl.ds(0, count), core], DOWN)


def fused_on_device(eigvecs, momenta, peram, graph):
    num_vec, colours, local_sites = eigvecs.shape[1:]
    spaces = lax.axis_size("space")
    wide = 2
    lines = spaces // (2 * wide)
    chips = lines * wide
    rows, fanout = graph.shape
    group = 16
    vectors = jnp.transpose(eigvecs, (0, 2, 1, 3))
    half = num_vec // 2
    dma = pltpu.SemaphoreType.DMA
    return pl.pallas_call(
        functools.partial(fused_kernel, lines, wide),
        out_shape=pltpu.VMEM((rows, fanout, 2 * num_vec), BF16),
        in_specs=[pl.BlockSpec(memory_space=pltpu.HBM)] * 4,
        out_specs=pl.BlockSpec(memory_space=pltpu.VMEM),
        scratch_shapes=[
            pltpu.SMEM(momenta.shape, jnp.int32),
            pltpu.VMEM((2, colours, num_vec, local_sites), BF16),
            pltpu.VMEM((fanout, rows), jnp.int32),
            pltpu.VMEM((momenta.shape[0], local_sites), F32),
            pltpu.VMEM((momenta.shape[0], local_sites), F32),
            pltpu.VMEM((2, 2, num_vec, num_vec), BF16),
            pltpu.VMEM((chips, 2, 2, half, num_vec), BF16),
            pltpu.VMEM((2 * rows, 2 * num_vec), F32),
            pltpu.VMEM((chips, rows, 2 * num_vec), F32),
            pltpu.VMEM((chips, rows, 2 * num_vec), BF16),
            pltpu.VMEM((chips, rows, 2 * num_vec), BF16),
            pltpu.VMEM((lines, wide, rows, 2 * num_vec), BF16),
            pltpu.VMEM((2, lines, wide, rows, 2 * num_vec), BF16),
            pltpu.VMEM((wide, rows, 2 * num_vec), F32),
            pltpu.VMEM((rows, 2 * num_vec), BF16),
            pltpu.VMEM((rows, 2 * num_vec), BF16),
            pltpu.VMEM((2, 2 * rows, 2 * num_vec), BF16),
            pltpu.VMEM((rows // group, spaces, group, 2 * num_vec), BF16),
            pltpu.VMEM((rows // group, group * fanout, spaces * group), BF16),
            dma((4,)),
            dma((8,)),
            dma((1,)),
            dma((chips,)),
            dma((lines + 1, wide, 2)),
            dma((2,)),
            dma((chips, 2)),
            dma((chips,)),
        ],
        compiler_params=pltpu.CompilerParams(
            collective_id=0, has_side_effects=True, vmem_limit_bytes=VMEM_ROOM + (16 << 20)
        ),
    )(momenta, vectors, peram[0], graph.T)


def fits(mesh, eigvecs, momenta, graph):
    num_vec = eigvecs.shape[1]
    spaces = mesh.shape["space"]
    rows = momenta.shape[0] * num_vec // spaces
    return (
        spaces == 16
        and rows % 16 == 0
        and num_vec % (2 * rows) == 0
        and num_vec % 128 == 0
        and spaces * 2 * num_vec * num_vec + 14 * spaces * rows * 2 * num_vec <= VMEM_ROOM
    )


def solution(mesh):
    placed = (
        P(None, None, None, ("groups", "space")),
        P(),
        P(("groups", "space"), None, None, None),
        P(("groups", "space"), None),
    )

    def whole(eigvecs, momenta, peram, graph):
        body = fused_on_device if fits(mesh, eigvecs, momenta, graph) else on_device
        return jax.shard_map(
            body,
            mesh=mesh,
            in_specs=placed,
            out_specs=P(("groups", "space"), None, None),
            check_vma=False,
        )(eigvecs, momenta, peram, graph)

    return whole
```

```python
import functools
import math

import jax
import jax.numpy as jnp
from jax import lax
from jax.experimental import pallas as pl
from jax.experimental.pallas import tpu as pltpu
from jax.sharding import PartitionSpec as P

EXTENT = 128
VMEM_ROOM = 40 << 20
BF16 = jnp.bfloat16
F32 = jnp.float32


def partner(block, axis, bit):
    count = lax.axis_size(axis)
    route = []
    for low in range(count):
        high = low | 1 << bit
        if high != low and high < count:
            route += [(low, high), (high, low)]
    return lax.ppermute(block, axis, route)


def phase_tables(momenta, site_index, extent):
    coord_x = site_index % extent
    coord_y = site_index // extent % extent
    coord_z = site_index // (extent * extent)
    wave_number = (
        momenta[:, 0:1] * coord_x[None, :]
        + momenta[:, 1:2] * coord_y[None, :]
        + momenta[:, 2:3] * coord_z[None, :]
    )
    wave_number = jnp.mod(wave_number, extent)
    phase_angle = wave_number.astype(jnp.float32) * (2.0 * math.pi / extent)
    return (jnp.cos(phase_angle), jnp.sin(phase_angle))


def block_form(peram_pair):
    peram_re = peram_pair[0]
    peram_im = peram_pair[1]
    top_half = jnp.concatenate([peram_re, peram_im], axis=1)
    bottom_half = jnp.concatenate([-peram_im, peram_re], axis=1)
    return jnp.concatenate([top_half, bottom_half], axis=0)


def sink_product(arrived, block):
    return lax.dot_general(
        arrived, block, (((2,), (0,)), ((), ())), preferred_element_type=jnp.float32
    ).astype(jnp.bfloat16)


def adjoint_product(sinks, block):
    return lax.dot_general(
        sinks, block, (((2,), (1,)), ((), ())), preferred_element_type=jnp.float32
    ).astype(jnp.bfloat16)


def on_device(eigvecs, momenta, peram, graph):
    num_vec = eigvecs.shape[1]
    local_sites = eigvecs.shape[3]
    spaces = lax.axis_size("space")
    position = lax.axis_index("space")
    site_index = position * local_sites + jnp.arange(local_sites, dtype=jnp.int32)
    cosine, sine = phase_tables(momenta, site_index, EXTENT)
    total_rows = cosine.shape[0] * num_vec
    rows_here = total_rows // spaces
    right_side = jnp.concatenate(
        [
            jnp.concatenate([eigvecs[0], -eigvecs[1]], axis=1),
            jnp.concatenate([eigvecs[1], eigvecs[0]], axis=1),
        ],
        axis=0,
    ).reshape(2 * num_vec, 6 * local_sites)
    row_index = jnp.arange(rows_here * lax.axis_size("space"), dtype=jnp.int32)
    vector_index = row_index % num_vec
    momentum_index = row_index // num_vec
    vec_re = jnp.take(eigvecs[0], vector_index, axis=0).astype(jnp.float32)
    vec_im = jnp.take(eigvecs[1], vector_index, axis=0).astype(jnp.float32)
    cos_rows = jnp.take(cosine, momentum_index, axis=0)[:, None, :]
    sin_rows = jnp.take(sine, momentum_index, axis=0)[:, None, :]
    left_re = vec_re * cos_rows - vec_im * sin_rows
    left_im = -(vec_re * sin_rows + vec_im * cos_rows)
    left_cat = (
        jnp.concatenate([left_re, left_im], axis=1)
        .astype(jnp.bfloat16)
        .reshape(rows_here * lax.axis_size("space"), 6 * local_sites)
    )
    summed = lax.psum_scatter(
        lax.dot_general(
            left_cat, right_side, (((1,), (1,)), ((), ())), preferred_element_type=jnp.float32
        ),
        "space",
        scatter_dimension=0,
        tiled=True,
    )
    elemental = summed.astype(jnp.bfloat16)
    fanout = graph.shape[1]
    capacity = max(2, 2 * rows_here * fanout // spaces)
    flat_owner = graph.reshape(-1)
    entries = flat_owner.shape[0]
    onehot = (flat_owner[:, None] == jnp.arange(spaces, dtype=jnp.int32)[None, :]).astype(jnp.int32)
    earlier = jnp.cumsum(onehot, axis=0) - onehot
    slot = jnp.sum(earlier * onehot, axis=1)
    source_row = jnp.arange(entries, dtype=jnp.int32) // fanout
    payload = jnp.take(elemental, source_row, axis=0)
    outgoing = (
        jnp.zeros((spaces, capacity, 2 * num_vec), jnp.bfloat16).at[flat_owner, slot].set(payload)
    )
    own_block = block_form(peram[0])
    partner_block = partner(own_block, "space", 0)
    sinks = sink_product(
        lax.all_to_all(outgoing, "space", split_axis=0, concat_axis=0, tiled=True), own_block
    )
    finished = adjoint_product(sinks, partner_block)
    returned = lax.all_to_all(finished, "space", split_axis=0, concat_axis=0, tiled=True)
    collected = returned[flat_owner, slot]
    return collected.reshape(rows_here, fanout, 2 * num_vec)


NT = (((1,), (1,)), ((), ()))
NN = (((1,), (0,)), ((), ()))


def dot(a, b, dims):
    return lax.dot_general(a, b, dims, preferred_element_type=F32)


def fill_phases(mom_ref, cos_ref, sin_ref, first_site):
    count = cos_ref.shape[0]
    shape = (1, cos_ref.shape[1])
    bits = EXTENT.bit_length() - 1
    site = first_site + lax.broadcasted_iota(jnp.int32, shape, 1)
    coord_x = site & (EXTENT - 1)
    coord_y = (site >> bits) & (EXTENT - 1)
    coord_z = site >> (2 * bits)
    for q in range(count):
        wave = (mom_ref[q, 0] * coord_x + mom_ref[q, 1] * coord_y + mom_ref[q, 2] * coord_z) & (EXTENT - 1)
        angle = wave.astype(F32) * (2.0 * math.pi / EXTENT)
        cos_ref[q : q + 1, :] = jnp.cos(angle)
        sin_ref[q : q + 1, :] = jnp.sin(angle)


def fused_kernel(
    lines, wide, mom_hbm, vec_hbm, peram_hbm, owner_hbm, out_ref,
    mom_ref, vec_ref, owner_ref, cos_ref, sin_ref, pair, gath, prod, own, core_out, core_in, z_out, z_in, total, y_out, y_in,
    lhs, results, picks, load_sem, send_sem, pair_recv, core_recv, z_recv, y_recv, gath_recv, mate_recv,
):
    colours, num_vec, local_sites = vec_ref.shape[1:]
    rows = own.shape[1]
    half = num_vec // 2
    me = lax.axis_index("space")
    core = me % 2
    chip = me // 2
    line = chip // wide
    column = chip % wide
    mate = chip * 2 + 1 - core
    other = 1 - column
    across = (line * wide + other) * 2 + core
    above = me + 2 * wide
    below = me - 2 * wide
    has_above = line < lines - 1
    has_below = line > 0

    def copy(src, dst, send, recv, to):
        return pltpu.make_async_remote_copy(
            src_ref=src, dst_ref=dst, send_sem=send, recv_sem=recv,
            device_id={"space": to}, device_id_type=pl.DeviceIdType.MESH,
        )

    barrier = pltpu.get_barrier_semaphore()

    def greet(to):
        pl.semaphore_signal(barrier, inc=1, device_id={"space": to}, device_id_type=pl.DeviceIdType.MESH)

    greet(mate)
    greet(across)

    @pl.when(has_above)
    def _():
        greet(above)

    @pl.when(has_below)
    def _():
        greet(below)

    loads = [
        pltpu.make_async_copy(src, dst, load_sem.at[place])
        for place, (src, dst) in enumerate(
            [(mom_hbm, mom_ref), (peram_hbm, pair.at[core]), (vec_hbm, vec_ref), (owner_hbm, owner_ref)]
        )
    ]
    for load in loads:
        load.start()
    load_mom, load_own, load_vec, load_owner = loads
    UP, ACROSS, MATE, DOWN, CORES, LINES, TOTALS, PAIR = range(8)

    def core_copy(unit):
        return copy(core_out.at[unit], core_in.at[unit], send_sem.at[CORES], core_recv.at[unit], mate)

    def unit_product(unit):
        first = unit * (2 * rows)
        momentum = first // num_vec
        start = pl.multiple_of(first % num_vec, 2 * rows)
        cosine = cos_ref[pl.ds(momentum, 1), :]
        sine = sin_ref[pl.ds(momentum, 1), :]
        left = []
        for colour in range(colours):
            v_re = vec_ref[0, colour, pl.ds(start, 2 * rows), :].astype(F32)
            v_im = vec_ref[1, colour, pl.ds(start, 2 * rows), :].astype(F32)
            left_re = (v_re * cosine - v_im * sine).astype(BF16)
            left_im = (-(v_re * sine + v_im * cosine)).astype(BF16)
            left.append(jnp.concatenate([left_re, left_im], axis=0))
        left = jnp.concatenate(left, axis=1)
        by_re = dot(left, jnp.concatenate([vec_ref[0, colour] for colour in range(colours)], axis=1), NT)
        by_im = dot(left, jnp.concatenate([vec_ref[1, colour] for colour in range(colours)], axis=1), NT)
        prod[:, :num_vec] = by_re[: 2 * rows] - by_im[2 * rows :]
        prod[:, num_vec:] = by_im[: 2 * rows] + by_re[2 * rows :]
        own[unit] = prod[pl.ds(pl.multiple_of(core * rows, rows), rows), :]
        core_out[unit] = prod[pl.ds(pl.multiple_of((1 - core) * rows, rows), rows), :].astype(BF16)

    lower = line < lines // 2
    below_count = line
    above_count = lines - 1 - line
    at_end = (line == 0) | (line == lines - 1)
    toward = jnp.where(lower, 1, -1)

    def line_at(step):
        if step == lines - 1:
            return line
        down = lines - 1 - step
        down = jnp.where(down <= line, down - 1, down)
        up = jnp.where(step >= line, step + 1, step)
        return jnp.where(lower, down, up)

    def column_at(piece):
        return jnp.where(piece == 0, other, column)

    def product_at(step, piece):
        unit = line_at(step) * wide + column_at(piece)
        unit_product(unit)
        core_copy(unit).start()

    share = rows // 2

    def z_copy(way, to_line, col, piece, to):
        span = pl.ds(piece * share, share)
        return copy(
            z_out.at[to_line, col, span], z_in.at[way, to_line, col, span],
            send_sem.at[LINES], z_recv.at[z_place(way, to_line, line + (1 - 2 * way)), col, piece], to,
        )

    def z_place(way, to_line, at):
        return jnp.where(to_line == at, lines, to_line) if way else to_line

    def z_arrived(way, to_line, col, piece):
        span = pl.ds(piece * share, share)
        copy(
            z_out.at[to_line, col, span], z_in.at[way, to_line, col, span],
            send_sem.at[LINES], z_recv.at[z_place(way, to_line, line), col, piece], mate,
        ).wait_recv()

    def chip_sum(to_line, col, span):
        unit = to_line * wide + col
        return own[unit, span] + core_in[unit, span].astype(F32)

    def mate_sent(to_line, col):
        core_copy(to_line * wide + col).wait_recv()

    def spans():
        return [(piece, pl.ds(piece * share, share)) for piece in range(2)]

    def begin(step, piece):
        to_line = line_at(step)
        col = column_at(piece)

        def send(way, to):
            mate_sent(to_line, col)
            for part, span in spans():
                z_out[to_line, col, span] = chip_sum(to_line, col, span).astype(BF16)
                z_copy(way, to_line, col, part, to).start()

        @pl.when(line == 0)
        def _():
            send(0, above)

        @pl.when(line == lines - 1)
        def _():
            send(1, below)

    def pass_on(way, to_line, piece, part, to, wait):
        col = column_at(piece)
        if part == 0:
            mate_sent(to_line, col)
        span = pl.ds(part * share, share)
        z_arrived(way, to_line, col, part)
        before = z_in[way, to_line, col, span].astype(F32)
        z_out[to_line, col, span] = (chip_sum(to_line, col, span) + before).astype(BF16)

        @pl.when(jnp.logical_not(wait))
        def _():
            z_copy(way, to_line, col, part, to).start()

    parts = gath.shape[2]

    def gather_copy(block, part, piece, way, to):
        there = gath.at[block, core, part, pl.ds(piece * (half // 2), half // 2)]
        recv = mate_recv.at[block] if way == MATE else gath_recv.at[block, part, piece]
        return copy(there, there, send_sem.at[way], recv, to)

    def gather_arrived(block, part, piece):
        gather_copy(block, part, piece, ACROSS, across).wait_recv()

    def from_mate(block):
        there = gath.at[block, 1 - core]
        copy(there, there, send_sem.at[MATE], mate_recv.at[block], mate).wait_recv()

    def spread(at, part, piece, onward, way, to):
        block = at * wide + column
        gather_arrived(block, part, piece)

        @pl.when(onward)
        def _():
            gather_copy(block, part, piece, way, to).start()

        @pl.when(jnp.logical_not(held(at, part)))
        def _():
            gather_copy(block, part, piece, ACROSS, across).start()

        gather_copy(block, part, piece, MATE, mate).start()

    def nth_line(turn):
        inner = jnp.where(turn == 2, -1, jnp.where(turn == 3, 2, turn))
        return line + toward * jnp.where(at_end, turn, inner)

    def relay(nth, piece):
        ends = toward * (nth // 2)
        inner = [0, 0, -1, 1, toward, 2 * toward, -toward, 2 * toward][nth]
        part = jnp.where(at_end, nth % 2, [0, 1, 0, 0, 1, 0, 1, 1][nth])
        block = (line + jnp.where(at_end, ends, inner)) * wide + other
        gather_arrived(block, part, piece)
        gather_copy(block, part, piece, MATE, mate).start()

    def arrivals(turn, count):
        tail = 2 * count - 1
        first = (turn == tail + 1) | (turn == tail + 2)
        last_piece = jnp.where(count == lines - 1, 2, 3)
        is_block = (count > 0) & ((turn <= tail) | (turn == tail + last_piece))
        back = jnp.where(turn < tail, (turn + 1) // 2, count)
        ahead = jnp.where(first, lines - 1 - count, lines - (turn + 1) // 2)
        part = jnp.where(turn <= tail, (turn - 1) % 2, jnp.where(first, turn - tail - 1, jnp.where(turn == tail + 3, 1, (turn - 1) % 2)))
        is_sum = (count > 0) & jnp.logical_not(is_block) & (ahead > 0)
        return is_block, is_sum, back, ahead, part

    def held(at, part):
        return jnp.logical_not(at_end) & (at == line + 2 * toward) & (part == 1)

    def late_sum(turn, count):
        return (count == lines - 2) & (turn == 2 * lines - 3)

    def send_late(way, count, to_line, to):
        @pl.when(count == lines - 2)
        def _():
            for part in range(2):
                z_copy(way, to_line, column, part, to).start()

    def slot(turn, piece):
        is_block, is_sum, back, ahead, part = arrivals(turn, below_count)

        @pl.when(is_block)
        def _():
            spread(line - back, part, piece, has_above, UP, above)

        @pl.when(is_sum)
        def _():
            pass_on(0, line + ahead, part, piece, above, late_sum(turn, below_count))

        is_block_, is_sum_, back_, ahead_, part_ = arrivals(turn, above_count)

        @pl.when(is_block_)
        def _():
            spread(line + back_, part_, piece, has_below, DOWN, below)

        @pl.when(is_sum_)
        def _():
            pass_on(1, line - ahead_, part_, piece, below, late_sum(turn, above_count))

        if turn == 2 * lines - 2 and piece == 1:
            send_late(0, below_count, lines - 1, above)
            send_late(1, above_count, 0, below)

    def line_total(piece, after=None):
        col = column_at(piece)
        mate_sent(line, col)
        for part, span in spans():
            total[col, span] = chip_sum(line, col, span)

            @pl.when(has_below)
            def _():
                z_arrived(0, line, col, part)
                total[col, span] += z_in[0, line, col, span].astype(F32)

            @pl.when(has_above)
            def _():
                z_arrived(1, line, col, part)
                total[col, span] += z_in[1, line, col, span].astype(F32)

            if after is not None:
                after(part, span)

    def y_copy(part, span):
        return copy(y_out.at[span], y_in.at[span], send_sem.at[TOTALS], y_recv.at[part], across)

    def send_across(part, span):
        y_out[span] = total[other, span].astype(BF16)
        y_copy(part, span).start()

    group = results.shape[2]
    fanout = out_ref.shape[1]
    owners = results.shape[1]

    def make_picks():
        spread = lax.broadcasted_iota(jnp.int32, (rows * fanout, fanout), 0) % fanout
        spread = jnp.where(spread == lax.broadcasted_iota(jnp.int32, (rows * fanout, fanout), 1), 1.0, 0.0)
        named = dot(spread.astype(BF16), owner_ref[...].astype(F32).astype(BF16), NN)
        own_row = lax.broadcasted_iota(jnp.int32, named.shape, 0) // fanout
        at_row = own_row == lax.broadcasted_iota(jnp.int32, named.shape, 1)
        named = jnp.sum(jnp.where(at_row, named, 0.0), axis=1, keepdims=True)
        shape = (group * fanout, owners * group)
        of_row = lax.broadcasted_iota(jnp.int32, shape, 0) // fanout
        of_col = lax.broadcasted_iota(jnp.int32, shape, 1)
        same = of_row == of_col % group
        col_owner = (of_col // group).astype(F32)
        for g in range(rows // group):
            chosen = named[g * group * fanout : (g + 1) * group * fanout, :] == col_owner
            picks[g] = jnp.where(same & chosen, 1.0, 0.0).astype(BF16)

    peers = 2 + jnp.where(has_above, 1, 0) + jnp.where(has_below, 1, 0)
    with jax.named_scope("greet"):
        pl.semaphore_wait(barrier, peers)

    def pair_copy(part, rows_from):
        span = pl.ds(rows_from, num_vec - rows_from)
        return copy(
            peram_hbm.at[part, span], pair.at[core, part, span], send_sem.at[PAIR], pair_recv.at[part], mate
        )

    def pair_arrived(part, rows_from):
        span = pl.ds(rows_from, num_vec - rows_from)
        there = pair.at[1 - core, part, span]
        copy(there, there, send_sem.at[PAIR], pair_recv.at[part], mate).wait_recv()

    def each_part(act, first, second):
        @pl.when(core == 0)
        def _():
            for part in range(2):
                act(part, first)

        @pl.when(core == 1)
        def _():
            for part in range(2):
                act(part, second)

    each_part(lambda part, rows_from: pair_copy(part, rows_from).start(), half, 0)
    load_mom.wait()
    fill_phases(mom_ref, cos_ref, sin_ref, me * local_sites)
    load_own.wait()
    with jax.named_scope("pair"):

        @pl.when(core == 1)
        def _():
            pair_arrived(0, half)
            pair_arrived(1, half)

        @pl.when(core == 0)
        def _():
            pair_arrived(0, 0)

    mine_rows = pl.ds(pl.multiple_of(core * half, half), half)
    with jax.named_scope("block"):
        lefts = jnp.concatenate([pair[0, 0, mine_rows, :], pair[0, 1, mine_rows, :]], axis=0)
        by_re = dot(lefts, pair[1, 0], NT)

        @pl.when(core == 0)
        def _():
            pair_arrived(1, 0)

        by_im = dot(lefts, pair[1, 1], NT)
        gath[chip, core, 0] = (by_re[:half] + by_im[half:]).astype(BF16)
        gath[chip, core, 1] = (by_re[half:] - by_im[:half]).astype(BF16)
    def send_own(part):
        for piece in range(2):

            @pl.when(has_above)
            def _():
                gather_copy(chip, part, piece, UP, above).start()

            @pl.when(has_below)
            def _():
                gather_copy(chip, part, piece, DOWN, below).start()

    def send_both(block, part, way, to):
        for piece in range(2):
            gather_copy(block, part, piece, way, to).start()

    send_both(chip, 0, ACROSS, across)
    send_own(0)
    send_both(chip, 1, ACROSS, across)

    @pl.when(jnp.logical_not(at_end))
    def _():
        send_own(1)

    for part in range(parts):
        send_both(chip, part, MATE, mate)

    def named_product(step, piece):
        with jax.named_scope(f"unit{step}{piece}"):
            product_at(step, piece)

    def named_slot(turn, piece):
        with jax.named_scope(f"slot{turn}{piece}"):
            slot(turn, piece)
            relay(turn - 1, piece)

    with jax.named_scope("load"):
        load_vec.wait()
    named_product(0, 0)
    named_product(0, 1)
    begin(0, 0)
    named_product(1, 0)
    begin(0, 1)

    @pl.when(at_end)
    def _():
        send_own(1)

    named_slot(1, 0)
    named_product(1, 1)
    named_slot(1, 1)
    named_product(2, 0)
    begin(1, 0)
    begin(1, 1)
    named_slot(2, 0)
    named_product(2, 1)
    named_slot(2, 1)
    named_product(3, 0)
    begin(2, 0)
    begin(2, 1)
    named_slot(3, 0)
    named_product(3, 1)
    named_slot(3, 1)
    load_owner.wait()
    with jax.named_scope("picks"):
        make_picks()
    for turn in range(4, 7):
        for piece in range(2):
            named_slot(turn, piece)
    farthest = nth_line(lines - 1) * wide + column

    @pl.when(at_end)
    def _():
        with jax.named_scope("total0"):
            line_total(0, send_across)

    with jax.named_scope("slot7"):
        for piece in range(2):
            slot(2 * lines - 1, piece)

            @pl.when(at_end)
            def _():
                relay(2 * lines - 2, piece)

    @pl.when(at_end)
    def _():
        with jax.named_scope("total1"):
            line_total(1)

    @pl.when(jnp.logical_not(at_end))
    def _():
        with jax.named_scope("total0"):
            line_total(0, send_across)
        send_both(farthest, 1, ACROSS, across)
        with jax.named_scope("rel6"):
            for piece in range(2):
                relay(2 * lines - 2, piece)
        with jax.named_scope("total1"):
            line_total(1)

    with jax.named_scope("across"):
        for part, span in spans():
            y_copy(part, span).wait_recv()
    row = (total[column] + y_in[...].astype(F32)).astype(BF16)
    row_re = row[:, :num_vec]
    row_im = row[:, num_vec:]
    lhs[0, :rows] = jnp.concatenate([row_re, -row_im], axis=1)
    lhs[0, rows:] = jnp.concatenate([row_im, row_re], axis=1)
    lhs[1, :rows] = row
    lhs[1, rows:] = jnp.concatenate([row_im, -row_re], axis=1)

    def put(owner, re, im):
        sixteen = results.shape[2]
        results[:, owner, :, :num_vec] = re.astype(BF16).reshape(rows // sixteen, sixteen, num_vec)
        results[:, owner, :, num_vec:] = im.astype(BF16).reshape(rows // sixteen, sixteen, num_vec)

    def contract(block):
        high = jnp.concatenate([gath[block, 0, 0], gath[block, 1, 0], gath[block, 0, 1], gath[block, 1, 1]], axis=0)
        by = dot(lhs[0], high, NN)
        put(2 * block, by[:rows], by[rows:])
        broad = [jnp.concatenate([gath[block, which, 0], gath[block, which, 1]], axis=1) for which in range(2)]
        by = dot(lhs[1], jnp.concatenate(broad, axis=0), NT)
        put(2 * block + 1, by[:rows], by[rows:])

    def block_at(turn):
        return nth_line(turn // 2) * wide + jnp.where(turn % 2 == 0, column, other)

    def relay_last():
        with jax.named_scope("last"):
            for piece in range(2):
                relay(2 * lines - 1, piece)

    @pl.loop(0, lines - 1)
    def _(pair_turn):
        @pl.when(at_end & (pair_turn == lines - 2))
        def _():
            relay_last()

        first, second = block_at(2 * pair_turn), block_at(2 * pair_turn + 1)
        with jax.named_scope("mate"):
            from_mate(first)
            from_mate(second)
        with jax.named_scope("contract"):
            contract(first)
            contract(second)

    @pl.loop(2 * lines - 2, 2 * lines)
    def _(turn):
        @pl.when(jnp.logical_not(at_end) & (turn == 2 * lines - 2))
        def _():
            relay_last()

        block = block_at(turn)
        with jax.named_scope("mate"):
            from_mate(block)
        with jax.named_scope("contract"):
            contract(block)

    for g in range(rows // group):
        rows_out = dot(picks[g], results[g].reshape(owners * group, 2 * num_vec), NN)
        out_ref[g * group : (g + 1) * group] = rows_out.reshape(group, fanout, 2 * num_vec).astype(BF16)

    def all_sent(what, way):
        copy(what, what, send_sem.at[way], core_recv.at[0], mate).wait_send()

    @pl.when(core == 0)
    def _():
        all_sent(peram_hbm.at[:, pl.ds(half, half)], PAIR)

    @pl.when(core == 1)
    def _():
        all_sent(peram_hbm, PAIR)

    all_sent(core_out, CORES)
    all_sent(z_out.at[pl.ds(0, lines - 1)], LINES)
    all_sent(y_out, TOTALS)
    all_sent(gath.at[pl.ds(0, lines), core], ACROSS)
    all_sent(gath.at[:, core], MATE)
    for count in range(1, lines):

        @pl.when(line == count - 1)
        def _():
            all_sent(gath.at[pl.ds(0, count), core], UP)

        @pl.when(line == lines - count)
        def _():
            all_sent(gath.at[pl.ds(0, count), core], DOWN)


def fused_on_device(eigvecs, momenta, peram, graph):
    num_vec, colours, local_sites = eigvecs.shape[1:]
    spaces = lax.axis_size("space")
    wide = 2
    lines = spaces // (2 * wide)
    chips = lines * wide
    rows, fanout = graph.shape
    group = 16
    vectors = jnp.transpose(eigvecs, (0, 2, 1, 3))
    half = num_vec // 2
    dma = pltpu.SemaphoreType.DMA
    return pl.pallas_call(
        functools.partial(fused_kernel, lines, wide),
        out_shape=pltpu.VMEM((rows, fanout, 2 * num_vec), BF16),
        in_specs=[pl.BlockSpec(memory_space=pltpu.HBM)] * 4,
        out_specs=pl.BlockSpec(memory_space=pltpu.VMEM),
        scratch_shapes=[
            pltpu.SMEM(momenta.shape, jnp.int32),
            pltpu.VMEM((2, colours, num_vec, local_sites), BF16),
            pltpu.VMEM((fanout, rows), jnp.int32),
            pltpu.VMEM((momenta.shape[0], local_sites), F32),
            pltpu.VMEM((momenta.shape[0], local_sites), F32),
            pltpu.VMEM((2, 2, num_vec, num_vec), BF16),
            pltpu.VMEM((chips, 2, 2, half, num_vec), BF16),
            pltpu.VMEM((2 * rows, 2 * num_vec), F32),
            pltpu.VMEM((chips, rows, 2 * num_vec), F32),
            pltpu.VMEM((chips, rows, 2 * num_vec), BF16),
            pltpu.VMEM((chips, rows, 2 * num_vec), BF16),
            pltpu.VMEM((lines, wide, rows, 2 * num_vec), BF16),
            pltpu.VMEM((2, lines, wide, rows, 2 * num_vec), BF16),
            pltpu.VMEM((wide, rows, 2 * num_vec), F32),
            pltpu.VMEM((rows, 2 * num_vec), BF16),
            pltpu.VMEM((rows, 2 * num_vec), BF16),
            pltpu.VMEM((2, 2 * rows, 2 * num_vec), BF16),
            pltpu.VMEM((rows // group, spaces, group, 2 * num_vec), BF16),
            pltpu.VMEM((rows // group, group * fanout, spaces * group), BF16),
            dma((4,)),
            dma((8,)),
            dma((2,)),
            dma((chips,)),
            dma((lines + 1, wide, 2)),
            dma((2,)),
            dma((chips, 2, 2)),
            dma((chips,)),
        ],
        compiler_params=pltpu.CompilerParams(
            collective_id=0, has_side_effects=True, vmem_limit_bytes=VMEM_ROOM + (16 << 20)
        ),
    )(momenta, vectors, peram[0], graph.T)


def fits(mesh, eigvecs, momenta, graph):
    num_vec = eigvecs.shape[1]
    spaces = mesh.shape["space"]
    rows = momenta.shape[0] * num_vec // spaces
    return (
        spaces == 16
        and rows % 16 == 0
        and num_vec % (2 * rows) == 0
        and num_vec % 128 == 0
        and spaces * 2 * num_vec * num_vec + 14 * spaces * rows * 2 * num_vec <= VMEM_ROOM
    )


def solution(mesh):
    placed = (
        P(None, None, None, ("groups", "space")),
        P(),
        P(("groups", "space"), None, None, None),
        P(("groups", "space"), None),
    )

    def whole(eigvecs, momenta, peram, graph):
        body = fused_on_device if fits(mesh, eigvecs, momenta, graph) else on_device
        return jax.shard_map(
            body,
            mesh=mesh,
            in_specs=placed,
            out_specs=P(("groups", "space"), None, None),
            check_vma=False,
        )(eigvecs, momenta, peram, graph)

    return whole
```

```python
import functools
import math

import jax
import jax.numpy as jnp
from jax import lax
from jax.experimental import pallas as pl
from jax.experimental.pallas import tpu as pltpu
from jax.sharding import PartitionSpec as P

EXTENT = 128
VMEM_ROOM = 40 << 20
BF16 = jnp.bfloat16
F32 = jnp.float32


def partner(block, axis, bit):
    count = lax.axis_size(axis)
    route = []
    for low in range(count):
        high = low | 1 << bit
        if high != low and high < count:
            route += [(low, high), (high, low)]
    return lax.ppermute(block, axis, route)


def phase_tables(momenta, site_index, extent):
    coord_x = site_index % extent
    coord_y = site_index // extent % extent
    coord_z = site_index // (extent * extent)
    wave_number = (
        momenta[:, 0:1] * coord_x[None, :]
        + momenta[:, 1:2] * coord_y[None, :]
        + momenta[:, 2:3] * coord_z[None, :]
    )
    wave_number = jnp.mod(wave_number, extent)
    phase_angle = wave_number.astype(jnp.float32) * (2.0 * math.pi / extent)
    return (jnp.cos(phase_angle), jnp.sin(phase_angle))


def block_form(peram_pair):
    peram_re = peram_pair[0]
    peram_im = peram_pair[1]
    top_half = jnp.concatenate([peram_re, peram_im], axis=1)
    bottom_half = jnp.concatenate([-peram_im, peram_re], axis=1)
    return jnp.concatenate([top_half, bottom_half], axis=0)


def sink_product(arrived, block):
    return lax.dot_general(
        arrived, block, (((2,), (0,)), ((), ())), preferred_element_type=jnp.float32
    ).astype(jnp.bfloat16)


def adjoint_product(sinks, block):
    return lax.dot_general(
        sinks, block, (((2,), (1,)), ((), ())), preferred_element_type=jnp.float32
    ).astype(jnp.bfloat16)


def on_device(eigvecs, momenta, peram, graph):
    num_vec = eigvecs.shape[1]
    local_sites = eigvecs.shape[3]
    spaces = lax.axis_size("space")
    position = lax.axis_index("space")
    site_index = position * local_sites + jnp.arange(local_sites, dtype=jnp.int32)
    cosine, sine = phase_tables(momenta, site_index, EXTENT)
    total_rows = cosine.shape[0] * num_vec
    rows_here = total_rows // spaces
    right_side = jnp.concatenate(
        [
            jnp.concatenate([eigvecs[0], -eigvecs[1]], axis=1),
            jnp.concatenate([eigvecs[1], eigvecs[0]], axis=1),
        ],
        axis=0,
    ).reshape(2 * num_vec, 6 * local_sites)
    row_index = jnp.arange(rows_here * lax.axis_size("space"), dtype=jnp.int32)
    vector_index = row_index % num_vec
    momentum_index = row_index // num_vec
    vec_re = jnp.take(eigvecs[0], vector_index, axis=0).astype(jnp.float32)
    vec_im = jnp.take(eigvecs[1], vector_index, axis=0).astype(jnp.float32)
    cos_rows = jnp.take(cosine, momentum_index, axis=0)[:, None, :]
    sin_rows = jnp.take(sine, momentum_index, axis=0)[:, None, :]
    left_re = vec_re * cos_rows - vec_im * sin_rows
    left_im = -(vec_re * sin_rows + vec_im * cos_rows)
    left_cat = (
        jnp.concatenate([left_re, left_im], axis=1)
        .astype(jnp.bfloat16)
        .reshape(rows_here * lax.axis_size("space"), 6 * local_sites)
    )
    summed = lax.psum_scatter(
        lax.dot_general(
            left_cat, right_side, (((1,), (1,)), ((), ())), preferred_element_type=jnp.float32
        ),
        "space",
        scatter_dimension=0,
        tiled=True,
    )
    elemental = summed.astype(jnp.bfloat16)
    fanout = graph.shape[1]
    capacity = max(2, 2 * rows_here * fanout // spaces)
    flat_owner = graph.reshape(-1)
    entries = flat_owner.shape[0]
    onehot = (flat_owner[:, None] == jnp.arange(spaces, dtype=jnp.int32)[None, :]).astype(jnp.int32)
    earlier = jnp.cumsum(onehot, axis=0) - onehot
    slot = jnp.sum(earlier * onehot, axis=1)
    source_row = jnp.arange(entries, dtype=jnp.int32) // fanout
    payload = jnp.take(elemental, source_row, axis=0)
    outgoing = (
        jnp.zeros((spaces, capacity, 2 * num_vec), jnp.bfloat16).at[flat_owner, slot].set(payload)
    )
    own_block = block_form(peram[0])
    partner_block = partner(own_block, "space", 0)
    sinks = sink_product(
        lax.all_to_all(outgoing, "space", split_axis=0, concat_axis=0, tiled=True), own_block
    )
    finished = adjoint_product(sinks, partner_block)
    returned = lax.all_to_all(finished, "space", split_axis=0, concat_axis=0, tiled=True)
    collected = returned[flat_owner, slot]
    return collected.reshape(rows_here, fanout, 2 * num_vec)


NT = (((1,), (1,)), ((), ()))
NN = (((1,), (0,)), ((), ()))


def dot(a, b, dims):
    return lax.dot_general(a, b, dims, preferred_element_type=F32)


def fill_phases(mom_ref, cos_ref, sin_ref, first_site):
    count = cos_ref.shape[0]
    shape = (1, cos_ref.shape[1])
    bits = EXTENT.bit_length() - 1
    site = first_site + lax.broadcasted_iota(jnp.int32, shape, 1)
    coord_x = site & (EXTENT - 1)
    coord_y = (site >> bits) & (EXTENT - 1)
    coord_z = site >> (2 * bits)
    for q in range(count):
        wave = (mom_ref[q, 0] * coord_x + mom_ref[q, 1] * coord_y + mom_ref[q, 2] * coord_z) & (EXTENT - 1)
        angle = wave.astype(F32) * (2.0 * math.pi / EXTENT)
        cos_ref[q : q + 1, :] = jnp.cos(angle)
        sin_ref[q : q + 1, :] = jnp.sin(angle)


def fused_kernel(
    lines, wide, mom_hbm, vec_hbm, peram_hbm, owner_hbm, out_ref,
    mom_ref, vec_ref, owner_ref, cos_ref, sin_ref, pair, gath, prod, own, core_out, core_in, z_out, z_in, total, y_out, y_in,
    lhs, results, picks, load_sem, send_sem, pair_recv, core_recv, z_recv, y_recv, gath_recv, mate_recv,
):
    colours, num_vec, local_sites = vec_ref.shape[1:]
    rows = own.shape[1]
    half = num_vec // 2
    me = lax.axis_index("space")
    core = me % 2
    chip = me // 2
    line = chip // wide
    column = chip % wide
    mate = chip * 2 + 1 - core
    other = 1 - column
    across = (line * wide + other) * 2 + core
    above = me + 2 * wide
    below = me - 2 * wide
    has_above = line < lines - 1
    has_below = line > 0

    def copy(src, dst, send, recv, to):
        return pltpu.make_async_remote_copy(
            src_ref=src, dst_ref=dst, send_sem=send, recv_sem=recv,
            device_id={"space": to}, device_id_type=pl.DeviceIdType.MESH,
        )

    barrier = pltpu.get_barrier_semaphore()

    def greet(to):
        pl.semaphore_signal(barrier, inc=1, device_id={"space": to}, device_id_type=pl.DeviceIdType.MESH)

    greet(mate)
    greet(across)

    @pl.when(has_above)
    def _():
        greet(above)

    @pl.when(has_below)
    def _():
        greet(below)

    loads = [
        pltpu.make_async_copy(src, dst, load_sem.at[place])
        for place, (src, dst) in enumerate(
            [(mom_hbm, mom_ref), (peram_hbm, pair.at[core]), (vec_hbm, vec_ref), (owner_hbm, owner_ref)]
        )
    ]
    for load in loads:
        load.start()
    load_mom, load_own, load_vec, load_owner = loads
    UP, ACROSS, MATE, DOWN, CORES, LINES, TOTALS, PAIR = range(8)

    def core_copy(unit):
        return copy(core_out.at[unit], core_in.at[unit], send_sem.at[CORES], core_recv.at[unit], mate)

    def unit_product(unit):
        first = unit * (2 * rows)
        momentum = first // num_vec
        start = pl.multiple_of(first % num_vec, 2 * rows)
        cosine = cos_ref[pl.ds(momentum, 1), :]
        sine = sin_ref[pl.ds(momentum, 1), :]
        left = []
        for colour in range(colours):
            v_re = vec_ref[0, colour, pl.ds(start, 2 * rows), :].astype(F32)
            v_im = vec_ref[1, colour, pl.ds(start, 2 * rows), :].astype(F32)
            left_re = (v_re * cosine - v_im * sine).astype(BF16)
            left_im = (-(v_re * sine + v_im * cosine)).astype(BF16)
            left.append(jnp.concatenate([left_re, left_im], axis=0))
        left = jnp.concatenate(left, axis=1)
        by_re = dot(left, jnp.concatenate([vec_ref[0, colour] for colour in range(colours)], axis=1), NT)
        by_im = dot(left, jnp.concatenate([vec_ref[1, colour] for colour in range(colours)], axis=1), NT)
        prod[:, :num_vec] = by_re[: 2 * rows] - by_im[2 * rows :]
        prod[:, num_vec:] = by_im[: 2 * rows] + by_re[2 * rows :]
        own[unit] = prod[pl.ds(pl.multiple_of(core * rows, rows), rows), :]
        core_out[unit] = prod[pl.ds(pl.multiple_of((1 - core) * rows, rows), rows), :].astype(BF16)

    lower = line < lines // 2
    below_count = line
    above_count = lines - 1 - line
    at_end = (line == 0) | (line == lines - 1)
    toward = jnp.where(lower, 1, -1)

    def line_at(step):
        if step == lines - 1:
            return line
        down = lines - 1 - step
        down = jnp.where(down <= line, down - 1, down)
        up = jnp.where(step >= line, step + 1, step)
        return jnp.where(lower, down, up)

    def column_at(piece):
        return jnp.where(piece == 0, other, column)

    def product_at(step, piece):
        unit = line_at(step) * wide + column_at(piece)
        unit_product(unit)
        core_copy(unit).start()

    share = rows // 2

    def z_copy(way, to_line, col, piece, to):
        span = pl.ds(piece * share, share)
        return copy(
            z_out.at[to_line, col, span], z_in.at[way, to_line, col, span],
            send_sem.at[LINES], z_recv.at[z_place(way, to_line, line + (1 - 2 * way)), col, piece], to,
        )

    def z_place(way, to_line, at):
        return jnp.where(to_line == at, lines, to_line) if way else to_line

    def z_arrived(way, to_line, col, piece):
        span = pl.ds(piece * share, share)
        copy(
            z_out.at[to_line, col, span], z_in.at[way, to_line, col, span],
            send_sem.at[LINES], z_recv.at[z_place(way, to_line, line), col, piece], mate,
        ).wait_recv()

    def chip_sum(to_line, col, span):
        unit = to_line * wide + col
        return own[unit, span] + core_in[unit, span].astype(F32)

    def mate_sent(to_line, col):
        core_copy(to_line * wide + col).wait_recv()

    def spans():
        return [(piece, pl.ds(piece * share, share)) for piece in range(2)]

    def begin(step, piece):
        to_line = line_at(step)
        col = column_at(piece)

        def send(way, to):
            mate_sent(to_line, col)
            for part, span in spans():
                z_out[to_line, col, span] = chip_sum(to_line, col, span).astype(BF16)
                z_copy(way, to_line, col, part, to).start()

        @pl.when(line == 0)
        def _():
            send(0, above)

        @pl.when(line == lines - 1)
        def _():
            send(1, below)

    def pass_on(way, to_line, piece, part, to, wait):
        col = column_at(piece)
        if part == 0:
            mate_sent(to_line, col)
        span = pl.ds(part * share, share)
        z_arrived(way, to_line, col, part)
        before = z_in[way, to_line, col, span].astype(F32)
        z_out[to_line, col, span] = (chip_sum(to_line, col, span) + before).astype(BF16)

        @pl.when(jnp.logical_not(wait))
        def _():
            z_copy(way, to_line, col, part, to).start()

    parts = gath.shape[2]

    def gather_copy(block, part, piece, way, to):
        there = gath.at[block, core, part, pl.ds(piece * (half // 2), half // 2)]
        recv = mate_recv.at[block] if way == MATE else gath_recv.at[block, part, piece]
        return copy(there, there, send_sem.at[way], recv, to)

    def gather_arrived(block, part, piece):
        gather_copy(block, part, piece, ACROSS, across).wait_recv()

    def from_mate(block):
        there = gath.at[block, 1 - core]
        copy(there, there, send_sem.at[MATE], mate_recv.at[block], mate).wait_recv()

    def spread(at, part, piece, onward, way, to):
        block = at * wide + column
        gather_arrived(block, part, piece)

        @pl.when(onward)
        def _():
            gather_copy(block, part, piece, way, to).start()

        @pl.when(jnp.logical_not(held(at, part, piece)))
        def _():
            gather_copy(block, part, piece, ACROSS, across).start()

        gather_copy(block, part, piece, MATE, mate).start()

    def nth_line(turn):
        inner = jnp.where(turn == 2, -1, jnp.where(turn == 3, 2, turn))
        return line + toward * jnp.where(at_end, turn, inner)

    def relay(nth, piece):
        ends = toward * (nth // 2)
        inner = [0, 0, -1, 1, toward, 2 * toward, -toward, 2 * toward][nth]
        part = jnp.where(at_end, nth % 2, [0, 1, 0, 0, 1, 0, 1, 1][nth])
        block = (line + jnp.where(at_end, ends, inner)) * wide + other
        gather_arrived(block, part, piece)
        gather_copy(block, part, piece, MATE, mate).start()

    def arrivals(turn, count):
        tail = 2 * count - 1
        first = (turn == tail + 1) | (turn == tail + 2)
        last_piece = jnp.where(count == lines - 1, 2, 3)
        is_block = (count > 0) & ((turn <= tail) | (turn == tail + last_piece))
        back = jnp.where(turn < tail, (turn + 1) // 2, count)
        ahead = jnp.where(first, lines - 1 - count, lines - (turn + 1) // 2)
        part = jnp.where(turn <= tail, (turn - 1) % 2, jnp.where(first, turn - tail - 1, jnp.where(turn == tail + 3, 1, (turn - 1) % 2)))
        is_sum = (count > 0) & jnp.logical_not(is_block) & (ahead > 0)
        return is_block, is_sum, back, ahead, part

    def held(at, part, piece):
        inner = (at == line + 2 * toward) & (part == 1)
        outer = (at == line + (lines - 1) * toward) & (part == 0)
        return jnp.where(at_end, outer, inner) if piece else jnp.logical_not(at_end) & inner

    def late_sum(turn, piece, count):
        return (count == lines - 2) & (turn == 2 * lines - 3) & (piece == 1)

    def send_late(way, count, to_line, to):
        @pl.when(count == lines - 2)
        def _():
            z_copy(way, to_line, column, 1, to).start()

    def slot(turn, piece):
        is_block, is_sum, back, ahead, part = arrivals(turn, below_count)

        @pl.when(is_block)
        def _():
            spread(line - back, part, piece, has_above, UP, above)

        @pl.when(is_sum)
        def _():
            pass_on(0, line + ahead, part, piece, above, late_sum(turn, piece, below_count))

        is_block_, is_sum_, back_, ahead_, part_ = arrivals(turn, above_count)

        @pl.when(is_block_)
        def _():
            spread(line + back_, part_, piece, has_below, DOWN, below)

        @pl.when(is_sum_)
        def _():
            pass_on(1, line - ahead_, part_, piece, below, late_sum(turn, piece, above_count))

        if turn == 2 * lines - 2 and piece == 1:
            send_late(0, below_count, lines - 1, above)
            send_late(1, above_count, 0, below)

    def line_total(piece, after=None):
        col = column_at(piece)
        mate_sent(line, col)
        for part, span in spans():
            total[col, span] = chip_sum(line, col, span)

            @pl.when(has_below)
            def _():
                z_arrived(0, line, col, part)
                total[col, span] += z_in[0, line, col, span].astype(F32)

            @pl.when(has_above)
            def _():
                z_arrived(1, line, col, part)
                total[col, span] += z_in[1, line, col, span].astype(F32)

            if after is not None:
                after(part, span)

    def y_copy(part, span):
        return copy(y_out.at[span], y_in.at[span], send_sem.at[TOTALS], y_recv.at[part], across)

    def send_across(part, span):
        y_out[span] = total[other, span].astype(BF16)
        y_copy(part, span).start()

    group = results.shape[2]
    fanout = out_ref.shape[1]
    owners = results.shape[1]

    def make_picks():
        spread = lax.broadcasted_iota(jnp.int32, (rows * fanout, fanout), 0) % fanout
        spread = jnp.where(spread == lax.broadcasted_iota(jnp.int32, (rows * fanout, fanout), 1), 1.0, 0.0)
        named = dot(spread.astype(BF16), owner_ref[...].astype(F32).astype(BF16), NN)
        own_row = lax.broadcasted_iota(jnp.int32, named.shape, 0) // fanout
        at_row = own_row == lax.broadcasted_iota(jnp.int32, named.shape, 1)
        named = jnp.sum(jnp.where(at_row, named, 0.0), axis=1, keepdims=True)
        shape = (group * fanout, owners * group)
        of_row = lax.broadcasted_iota(jnp.int32, shape, 0) // fanout
        of_col = lax.broadcasted_iota(jnp.int32, shape, 1)
        same = of_row == of_col % group
        col_owner = (of_col // group).astype(F32)
        for g in range(rows // group):
            chosen = named[g * group * fanout : (g + 1) * group * fanout, :] == col_owner
            picks[g] = jnp.where(same & chosen, 1.0, 0.0).astype(BF16)

    peers = 2 + jnp.where(has_above, 1, 0) + jnp.where(has_below, 1, 0)
    with jax.named_scope("greet"):
        pl.semaphore_wait(barrier, peers)

    def pair_copy(part, rows_from):
        span = pl.ds(rows_from, num_vec - rows_from)
        there = pair.at[core, part, span]
        return copy(there, there, send_sem.at[PAIR], pair_recv.at[part], mate)

    def pair_arrived(part, rows_from):
        span = pl.ds(rows_from, num_vec - rows_from)
        there = pair.at[1 - core, part, span]
        copy(there, there, send_sem.at[PAIR], pair_recv.at[part], mate).wait_recv()

    def each_part(act, first, second):
        @pl.when(core == 0)
        def _():
            for part in range(2):
                act(part, first)

        @pl.when(core == 1)
        def _():
            for part in range(2):
                act(part, second)

    load_own.wait()
    each_part(lambda part, rows_from: pair_copy(part, rows_from).start(), half, 0)
    load_mom.wait()
    fill_phases(mom_ref, cos_ref, sin_ref, me * local_sites)
    def own_lefts():
        mine_rows = pl.ds(pl.multiple_of(core * half, half), half)
        return jnp.concatenate([pair[0, 0, mine_rows, :], pair[0, 1, mine_rows, :]], axis=0)

    def own_block(by_re, by_im):
        gath[chip, core, 0] = (by_re[:half] + by_im[half:]).astype(BF16)
        gath[chip, core, 1] = (by_re[half:] - by_im[:half]).astype(BF16)

    @pl.when(core == 1)
    def _():
        with jax.named_scope("pair"):
            pair_arrived(0, half)
            pair_arrived(1, half)
        with jax.named_scope("block"):
            lefts = own_lefts()
            own_block(dot(lefts, pair[1, 0], NT), dot(lefts, pair[1, 1], NT))

    @pl.when(core == 0)
    def _():
        with jax.named_scope("pair"):
            pair_arrived(0, 0)
        with jax.named_scope("block"):
            lefts = own_lefts()
            by_re = dot(lefts, pair[1, 0], NT)
            pair_arrived(1, 0)
            own_block(by_re, dot(lefts, pair[1, 1], NT))

    def send_own(part):
        for piece in range(2):

            @pl.when(has_above)
            def _():
                gather_copy(chip, part, piece, UP, above).start()

            @pl.when(has_below)
            def _():
                gather_copy(chip, part, piece, DOWN, below).start()

    def send_both(block, part, way, to):
        for piece in range(2):
            gather_copy(block, part, piece, way, to).start()

    send_both(chip, 0, ACROSS, across)
    send_own(0)
    send_both(chip, 1, ACROSS, across)

    @pl.when(jnp.logical_not(at_end))
    def _():
        send_own(1)

    for part in range(parts):
        send_both(chip, part, MATE, mate)

    def named_product(step, piece):
        with jax.named_scope(f"unit{step}{piece}"):
            product_at(step, piece)

    def named_slot(turn, piece):
        with jax.named_scope(f"slot{turn}{piece}"):
            slot(turn, piece)
            relay(turn - 1, piece)

    with jax.named_scope("load"):
        load_vec.wait()
    named_product(0, 0)
    named_product(0, 1)
    begin(0, 0)
    named_product(1, 0)
    begin(0, 1)

    @pl.when(at_end)
    def _():
        send_own(1)

    named_slot(1, 0)
    named_product(1, 1)
    named_slot(1, 1)
    named_product(2, 0)
    begin(1, 0)
    begin(1, 1)
    named_slot(2, 0)
    named_product(2, 1)
    named_slot(2, 1)
    named_product(3, 0)
    begin(2, 0)
    begin(2, 1)
    named_slot(3, 0)
    named_product(3, 1)
    named_slot(3, 1)
    load_owner.wait()
    with jax.named_scope("picks"):
        make_picks()
    for turn in range(4, 7):
        for piece in range(2):
            named_slot(turn, piece)
    def send_held(part, span):
        if part == 0:
            gather_copy(farthest, 1, 0, ACROSS, across).start()

    farthest = nth_line(lines - 1) * wide + column

    @pl.when(at_end)
    def _():
        with jax.named_scope("total0"):
            line_total(0, send_across)

    with jax.named_scope("slot7"):
        for piece in range(2):
            slot(2 * lines - 1, piece)

    @pl.when(at_end)
    def _():
        relay(2 * lines - 2, 0)
        with jax.named_scope("total1"):
            line_total(1)

    @pl.when(jnp.logical_not(at_end))
    def _():
        with jax.named_scope("total0"):
            line_total(0, send_across)
        with jax.named_scope("rel6"):
            for piece in range(2):
                relay(2 * lines - 2, piece)
        inward = (line - toward) * wide + other
        outward = (line + 2 * toward) * wide + other

        @pl.when(lower)
        def _():
            gather_copy(inward, 1, 1, UP, above).start()
            gather_copy(outward, 0, 1, DOWN, below).start()

        @pl.when(jnp.logical_not(lower))
        def _():
            gather_copy(inward, 1, 1, DOWN, below).start()
            gather_copy(outward, 0, 1, UP, above).start()

        with jax.named_scope("total1"):
            line_total(1, send_held)

    with jax.named_scope("across"):
        for part, span in spans():
            y_copy(part, span).wait_recv()
    row = (total[column] + y_in[...].astype(F32)).astype(BF16)
    row_re = row[:, :num_vec]
    row_im = row[:, num_vec:]
    lhs[0, :rows] = jnp.concatenate([row_re, -row_im], axis=1)
    lhs[0, rows:] = jnp.concatenate([row_im, row_re], axis=1)
    lhs[1, :rows] = row
    lhs[1, rows:] = jnp.concatenate([row_im, -row_re], axis=1)

    def put(owner, re, im):
        sixteen = results.shape[2]
        results[:, owner, :, :num_vec] = re.astype(BF16).reshape(rows // sixteen, sixteen, num_vec)
        results[:, owner, :, num_vec:] = im.astype(BF16).reshape(rows // sixteen, sixteen, num_vec)

    def contract(block):
        high = jnp.concatenate([gath[block, 0, 0], gath[block, 1, 0], gath[block, 0, 1], gath[block, 1, 1]], axis=0)
        by = dot(lhs[0], high, NN)
        put(2 * block, by[:rows], by[rows:])
        broad = [jnp.concatenate([gath[block, which, 0], gath[block, which, 1]], axis=1) for which in range(2)]
        by = dot(lhs[1], jnp.concatenate(broad, axis=0), NT)
        put(2 * block + 1, by[:rows], by[rows:])

    def block_at(turn):
        return nth_line(turn // 2) * wide + jnp.where(turn % 2 == 0, column, other)

    def relay_last():
        with jax.named_scope("last"):

            @pl.when(at_end)
            def _():
                relay(2 * lines - 2, 1)

            for piece in range(2):
                relay(2 * lines - 1, piece)

    early = [block_at(turn) for turn in range(2 * lines - 2)]
    with jax.named_scope("mate"):
        for block in early:
            from_mate(block)
    with jax.named_scope("contract"):
        for block in early:
            contract(block)
    relay_last()

    @pl.loop(2 * lines - 2, 2 * lines)
    def _(turn):
        block = block_at(turn)
        with jax.named_scope("mate"):
            from_mate(block)
        with jax.named_scope("contract"):
            contract(block)

    for g in range(rows // group):
        rows_out = dot(picks[g], results[g].reshape(owners * group, 2 * num_vec), NN)
        out_ref[g * group : (g + 1) * group] = rows_out.reshape(group, fanout, 2 * num_vec).astype(BF16)

    def all_sent(what, way):
        copy(what, what, send_sem.at[way], core_recv.at[0], mate).wait_send()

    @pl.when(core == 0)
    def _():
        all_sent(pair.at[0, :, pl.ds(half, half)], PAIR)

    @pl.when(core == 1)
    def _():
        all_sent(pair.at[1], PAIR)

    all_sent(core_out, CORES)
    all_sent(z_out.at[pl.ds(0, lines - 1)], LINES)
    all_sent(y_out, TOTALS)
    all_sent(gath.at[:, core], MATE)

    def pieces_sent(count, way):
        all_sent(results.at[pl.ds(0, half // (4 * group)), pl.ds(0, count)], way)

    pieces_sent(4 * lines - 1, ACROSS)
    for count in range(1, lines):

        @pl.when(line == count - 1)
        def _():
            pieces_sent(4 * count + (1 if count > 1 else 0), UP)

        @pl.when(line == lines - count)
        def _():
            pieces_sent(4 * count + (1 if count > 1 else 0), DOWN)


def fused_on_device(eigvecs, momenta, peram, graph):
    num_vec, colours, local_sites = eigvecs.shape[1:]
    spaces = lax.axis_size("space")
    wide = 2
    lines = spaces // (2 * wide)
    chips = lines * wide
    rows, fanout = graph.shape
    group = 16
    vectors = jnp.transpose(eigvecs, (0, 2, 1, 3))
    half = num_vec // 2
    dma = pltpu.SemaphoreType.DMA
    return pl.pallas_call(
        functools.partial(fused_kernel, lines, wide),
        out_shape=pltpu.VMEM((rows, fanout, 2 * num_vec), BF16),
        in_specs=[pl.BlockSpec(memory_space=pltpu.HBM)] * 4,
        out_specs=pl.BlockSpec(memory_space=pltpu.VMEM),
        scratch_shapes=[
            pltpu.SMEM(momenta.shape, jnp.int32),
            pltpu.VMEM((2, colours, num_vec, local_sites), BF16),
            pltpu.VMEM((fanout, rows), jnp.int32),
            pltpu.VMEM((momenta.shape[0], local_sites), F32),
            pltpu.VMEM((momenta.shape[0], local_sites), F32),
            pltpu.VMEM((2, 2, num_vec, num_vec), BF16),
            pltpu.VMEM((chips, 2, 2, half, num_vec), BF16),
            pltpu.VMEM((2 * rows, 2 * num_vec), F32),
            pltpu.VMEM((chips, rows, 2 * num_vec), F32),
            pltpu.VMEM((chips, rows, 2 * num_vec), BF16),
            pltpu.VMEM((chips, rows, 2 * num_vec), BF16),
            pltpu.VMEM((lines, wide, rows, 2 * num_vec), BF16),
            pltpu.VMEM((2, lines, wide, rows, 2 * num_vec), BF16),
            pltpu.VMEM((wide, rows, 2 * num_vec), F32),
            pltpu.VMEM((rows, 2 * num_vec), BF16),
            pltpu.VMEM((rows, 2 * num_vec), BF16),
            pltpu.VMEM((2, 2 * rows, 2 * num_vec), BF16),
            pltpu.VMEM((rows // group, spaces, group, 2 * num_vec), BF16),
            pltpu.VMEM((rows // group, group * fanout, spaces * group), BF16),
            dma((4,)),
            dma((8,)),
            dma((2,)),
            dma((chips,)),
            dma((lines + 1, wide, 2)),
            dma((2,)),
            dma((chips, 2, 2)),
            dma((chips,)),
        ],
        compiler_params=pltpu.CompilerParams(
            collective_id=0, has_side_effects=True, vmem_limit_bytes=VMEM_ROOM + (16 << 20)
        ),
    )(momenta, vectors, peram[0], graph.T)


def fits(mesh, eigvecs, momenta, graph):
    num_vec = eigvecs.shape[1]
    spaces = mesh.shape["space"]
    rows = momenta.shape[0] * num_vec // spaces
    return (
        spaces == 16
        and rows % 16 == 0
        and num_vec % (2 * rows) == 0
        and num_vec % 128 == 0
        and spaces * 2 * num_vec * num_vec + 14 * spaces * rows * 2 * num_vec <= VMEM_ROOM
    )


def solution(mesh):
    placed = (
        P(None, None, None, ("groups", "space")),
        P(),
        P(("groups", "space"), None, None, None),
        P(("groups", "space"), None),
    )

    def whole(eigvecs, momenta, peram, graph):
        body = fused_on_device if fits(mesh, eigvecs, momenta, graph) else on_device
        return jax.shard_map(
            body,
            mesh=mesh,
            in_specs=placed,
            out_specs=P(("groups", "space"), None, None),
            check_vma=False,
        )(eigvecs, momenta, peram, graph)

    return whole
```

```python
import functools
import math

import jax
import jax.numpy as jnp
from jax import lax
from jax.experimental import pallas as pl
from jax.experimental.pallas import tpu as pltpu
from jax.sharding import PartitionSpec as P

EXTENT = 128
VMEM_ROOM = 40 << 20
BF16 = jnp.bfloat16
F32 = jnp.float32


def partner(block, axis, bit):
    count = lax.axis_size(axis)
    route = []
    for low in range(count):
        high = low | 1 << bit
        if high != low and high < count:
            route += [(low, high), (high, low)]
    return lax.ppermute(block, axis, route)


def phase_tables(momenta, site_index, extent):
    coord_x = site_index % extent
    coord_y = site_index // extent % extent
    coord_z = site_index // (extent * extent)
    wave_number = (
        momenta[:, 0:1] * coord_x[None, :]
        + momenta[:, 1:2] * coord_y[None, :]
        + momenta[:, 2:3] * coord_z[None, :]
    )
    wave_number = jnp.mod(wave_number, extent)
    phase_angle = wave_number.astype(jnp.float32) * (2.0 * math.pi / extent)
    return (jnp.cos(phase_angle), jnp.sin(phase_angle))


def block_form(peram_pair):
    peram_re = peram_pair[0]
    peram_im = peram_pair[1]
    top_half = jnp.concatenate([peram_re, peram_im], axis=1)
    bottom_half = jnp.concatenate([-peram_im, peram_re], axis=1)
    return jnp.concatenate([top_half, bottom_half], axis=0)


def sink_product(arrived, block):
    return lax.dot_general(
        arrived, block, (((2,), (0,)), ((), ())), preferred_element_type=jnp.float32
    ).astype(jnp.bfloat16)


def adjoint_product(sinks, block):
    return lax.dot_general(
        sinks, block, (((2,), (1,)), ((), ())), preferred_element_type=jnp.float32
    ).astype(jnp.bfloat16)


def on_device(eigvecs, momenta, peram, graph):
    num_vec = eigvecs.shape[1]
    local_sites = eigvecs.shape[3]
    spaces = lax.axis_size("space")
    position = lax.axis_index("space")
    site_index = position * local_sites + jnp.arange(local_sites, dtype=jnp.int32)
    cosine, sine = phase_tables(momenta, site_index, EXTENT)
    total_rows = cosine.shape[0] * num_vec
    rows_here = total_rows // spaces
    right_side = jnp.concatenate(
        [
            jnp.concatenate([eigvecs[0], -eigvecs[1]], axis=1),
            jnp.concatenate([eigvecs[1], eigvecs[0]], axis=1),
        ],
        axis=0,
    ).reshape(2 * num_vec, 6 * local_sites)
    row_index = jnp.arange(rows_here * lax.axis_size("space"), dtype=jnp.int32)
    vector_index = row_index % num_vec
    momentum_index = row_index // num_vec
    vec_re = jnp.take(eigvecs[0], vector_index, axis=0).astype(jnp.float32)
    vec_im = jnp.take(eigvecs[1], vector_index, axis=0).astype(jnp.float32)
    cos_rows = jnp.take(cosine, momentum_index, axis=0)[:, None, :]
    sin_rows = jnp.take(sine, momentum_index, axis=0)[:, None, :]
    left_re = vec_re * cos_rows - vec_im * sin_rows
    left_im = -(vec_re * sin_rows + vec_im * cos_rows)
    left_cat = (
        jnp.concatenate([left_re, left_im], axis=1)
        .astype(jnp.bfloat16)
        .reshape(rows_here * lax.axis_size("space"), 6 * local_sites)
    )
    summed = lax.psum_scatter(
        lax.dot_general(
            left_cat, right_side, (((1,), (1,)), ((), ())), preferred_element_type=jnp.float32
        ),
        "space",
        scatter_dimension=0,
        tiled=True,
    )
    elemental = summed.astype(jnp.bfloat16)
    fanout = graph.shape[1]
    capacity = max(2, 2 * rows_here * fanout // spaces)
    flat_owner = graph.reshape(-1)
    entries = flat_owner.shape[0]
    onehot = (flat_owner[:, None] == jnp.arange(spaces, dtype=jnp.int32)[None, :]).astype(jnp.int32)
    earlier = jnp.cumsum(onehot, axis=0) - onehot
    slot = jnp.sum(earlier * onehot, axis=1)
    source_row = jnp.arange(entries, dtype=jnp.int32) // fanout
    payload = jnp.take(elemental, source_row, axis=0)
    outgoing = (
        jnp.zeros((spaces, capacity, 2 * num_vec), jnp.bfloat16).at[flat_owner, slot].set(payload)
    )
    own_block = block_form(peram[0])
    partner_block = partner(own_block, "space", 0)
    sinks = sink_product(
        lax.all_to_all(outgoing, "space", split_axis=0, concat_axis=0, tiled=True), own_block
    )
    finished = adjoint_product(sinks, partner_block)
    returned = lax.all_to_all(finished, "space", split_axis=0, concat_axis=0, tiled=True)
    collected = returned[flat_owner, slot]
    return collected.reshape(rows_here, fanout, 2 * num_vec)


NT = (((1,), (1,)), ((), ()))
NN = (((1,), (0,)), ((), ()))


def dot(a, b, dims):
    return lax.dot_general(a, b, dims, preferred_element_type=F32)


def fill_phases(mom_ref, cos_ref, sin_ref, first_site):
    count = cos_ref.shape[0]
    shape = (1, cos_ref.shape[1])
    bits = EXTENT.bit_length() - 1
    site = first_site + lax.broadcasted_iota(jnp.int32, shape, 1)
    coord_x = site & (EXTENT - 1)
    coord_y = (site >> bits) & (EXTENT - 1)
    coord_z = site >> (2 * bits)
    for q in range(count):
        wave = (mom_ref[q, 0] * coord_x + mom_ref[q, 1] * coord_y + mom_ref[q, 2] * coord_z) & (EXTENT - 1)
        angle = wave.astype(F32) * (2.0 * math.pi / EXTENT)
        cos_ref[q : q + 1, :] = jnp.cos(angle)
        sin_ref[q : q + 1, :] = jnp.sin(angle)


def fused_kernel(
    lines, wide, mom_hbm, vec_hbm, peram_hbm, owner_hbm, results, picks,
    mom_ref, vec_ref, owner_ref, cos_ref, sin_ref, pair, gath, prod, own, core_out, core_in, z_out, z_in, total, y_out, y_in,
    lhs, load_sem, send_sem, pair_recv, core_recv, z_recv, y_recv, gath_recv, mate_recv,
):
    colours, num_vec, local_sites = vec_ref.shape[1:]
    rows = own.shape[1]
    half = num_vec // 2
    me = lax.axis_index("space")
    core = me % 2
    chip = me // 2
    line = chip // wide
    column = chip % wide
    mate = chip * 2 + 1 - core
    other = 1 - column
    across = (line * wide + other) * 2 + core
    above = me + 2 * wide
    below = me - 2 * wide
    has_above = line < lines - 1
    has_below = line > 0

    def copy(src, dst, send, recv, to):
        return pltpu.make_async_remote_copy(
            src_ref=src, dst_ref=dst, send_sem=send, recv_sem=recv,
            device_id={"space": to}, device_id_type=pl.DeviceIdType.MESH,
        )

    barrier = pltpu.get_barrier_semaphore()

    def greet(to):
        pl.semaphore_signal(barrier, inc=1, device_id={"space": to}, device_id_type=pl.DeviceIdType.MESH)

    greet(mate)
    greet(across)

    @pl.when(has_above)
    def _():
        greet(above)

    @pl.when(has_below)
    def _():
        greet(below)

    loads = [
        pltpu.make_async_copy(src, dst, load_sem.at[place])
        for place, (src, dst) in enumerate(
            [(mom_hbm, mom_ref), (peram_hbm, pair.at[core]), (vec_hbm, vec_ref), (owner_hbm, owner_ref)]
        )
    ]
    for load in loads:
        load.start()
    load_mom, load_own, load_vec, load_owner = loads
    UP, ACROSS, MATE, DOWN, CORES, LINES, TOTALS, PAIR = range(8)

    def core_copy(unit):
        return copy(core_out.at[unit], core_in.at[unit], send_sem.at[CORES], core_recv.at[unit], mate)

    def unit_product(unit):
        first = unit * (2 * rows)
        momentum = first // num_vec
        start = pl.multiple_of(first % num_vec, 2 * rows)
        cosine = cos_ref[pl.ds(momentum, 1), :]
        sine = sin_ref[pl.ds(momentum, 1), :]
        left = []
        for colour in range(colours):
            v_re = vec_ref[0, colour, pl.ds(start, 2 * rows), :].astype(F32)
            v_im = vec_ref[1, colour, pl.ds(start, 2 * rows), :].astype(F32)
            left_re = (v_re * cosine - v_im * sine).astype(BF16)
            left_im = (-(v_re * sine + v_im * cosine)).astype(BF16)
            left.append(jnp.concatenate([left_re, left_im], axis=0))
        left = jnp.concatenate(left, axis=1)
        by_re = dot(left, jnp.concatenate([vec_ref[0, colour] for colour in range(colours)], axis=1), NT)
        by_im = dot(left, jnp.concatenate([vec_ref[1, colour] for colour in range(colours)], axis=1), NT)
        prod[:, :num_vec] = by_re[: 2 * rows] - by_im[2 * rows :]
        prod[:, num_vec:] = by_im[: 2 * rows] + by_re[2 * rows :]
        own[unit] = prod[pl.ds(pl.multiple_of(core * rows, rows), rows), :]
        core_out[unit] = prod[pl.ds(pl.multiple_of((1 - core) * rows, rows), rows), :].astype(BF16)

    lower = line < lines // 2
    below_count = line
    above_count = lines - 1 - line
    at_end = (line == 0) | (line == lines - 1)
    toward = jnp.where(lower, 1, -1)

    def line_at(step):
        if step == lines - 1:
            return line
        down = lines - 1 - step
        down = jnp.where(down <= line, down - 1, down)
        up = jnp.where(step >= line, step + 1, step)
        return jnp.where(lower, down, up)

    def column_at(piece):
        return jnp.where(piece == 0, other, column)

    def product_at(step, piece):
        unit = line_at(step) * wide + column_at(piece)
        unit_product(unit)
        core_copy(unit).start()

    share = rows // 2

    def z_copy(way, to_line, col, piece, to):
        span = pl.ds(piece * share, share)
        return copy(
            z_out.at[to_line, col, span], z_in.at[way, to_line, col, span],
            send_sem.at[LINES], z_recv.at[z_place(way, to_line, line + (1 - 2 * way)), col, piece], to,
        )

    def z_place(way, to_line, at):
        return jnp.where(to_line == at, lines, to_line) if way else to_line

    def z_arrived(way, to_line, col, piece):
        span = pl.ds(piece * share, share)
        copy(
            z_out.at[to_line, col, span], z_in.at[way, to_line, col, span],
            send_sem.at[LINES], z_recv.at[z_place(way, to_line, line), col, piece], mate,
        ).wait_recv()

    def chip_sum(to_line, col, span):
        unit = to_line * wide + col
        return own[unit, span] + core_in[unit, span].astype(F32)

    def mate_sent(to_line, col):
        core_copy(to_line * wide + col).wait_recv()

    def spans():
        return [(piece, pl.ds(piece * share, share)) for piece in range(2)]

    def begin(step, piece):
        to_line = line_at(step)
        col = column_at(piece)

        def send(way, to):
            mate_sent(to_line, col)
            for part, span in spans():
                z_out[to_line, col, span] = chip_sum(to_line, col, span).astype(BF16)
                z_copy(way, to_line, col, part, to).start()

        @pl.when(line == 0)
        def _():
            send(0, above)

        @pl.when(line == lines - 1)
        def _():
            send(1, below)

    def pass_on(way, to_line, piece, part, to, wait):
        col = column_at(piece)
        if part == 0:
            mate_sent(to_line, col)
        span = pl.ds(part * share, share)
        z_arrived(way, to_line, col, part)
        before = z_in[way, to_line, col, span].astype(F32)
        z_out[to_line, col, span] = (chip_sum(to_line, col, span) + before).astype(BF16)

        @pl.when(jnp.logical_not(wait))
        def _():
            z_copy(way, to_line, col, part, to).start()

    parts = gath.shape[2]

    def gather_copy(block, part, piece, way, to):
        there = gath.at[block, core, part, pl.ds(piece * (half // 2), half // 2)]
        recv = mate_recv.at[mate_place(block)] if way == MATE else gath_recv.at[block, part, piece]
        return copy(there, there, send_sem.at[way], recv, to)

    def gather_arrived(block, part, piece):
        gather_copy(block, part, piece, ACROSS, across).wait_recv()

    def mate_place(block):
        far = line + toward * jnp.where(at_end, lines - 1, 2)
        return jnp.where(block // wide != far, 0, jnp.where(block % wide == column, 1, 2))

    def from_mate(block):
        there = gath.at[block, 1 - core]
        copy(there, there, send_sem.at[MATE], mate_recv.at[mate_place(block)], mate).wait_recv()

    def early_from_mate():
        there = gath.at[pl.ds(0, wide * (lines - 1)), 1 - core]
        copy(there, there, send_sem.at[MATE], mate_recv.at[0], mate).wait_recv()

    def spread(at, part, piece, onward, way, to):
        block = at * wide + column
        gather_arrived(block, part, piece)

        @pl.when(onward)
        def _():
            gather_copy(block, part, piece, way, to).start()

        @pl.when(jnp.logical_not(held(at, part, piece)))
        def _():
            gather_copy(block, part, piece, ACROSS, across).start()

        gather_copy(block, part, piece, MATE, mate).start()

    def nth_line(turn):
        inner = jnp.where(turn == 2, -1, jnp.where(turn == 3, 2, turn))
        return line + toward * jnp.where(at_end, turn, inner)

    def relay(nth, piece):
        ends = toward * (nth // 2)
        inner = [0, 0, -1, 1, toward, 2 * toward, -toward, 2 * toward][nth]
        part = jnp.where(at_end, nth % 2, [0, 1, 0, 0, 1, 0, 1, 1][nth])
        block = (line + jnp.where(at_end, ends, inner)) * wide + other
        gather_arrived(block, part, piece)
        gather_copy(block, part, piece, MATE, mate).start()

    def arrivals(turn, count):
        tail = 2 * count - 1
        first = (turn == tail + 1) | (turn == tail + 2)
        last_piece = jnp.where(count == lines - 1, 2, 3)
        is_block = (count > 0) & ((turn <= tail) | (turn == tail + last_piece))
        back = jnp.where(turn < tail, (turn + 1) // 2, count)
        ahead = jnp.where(first, lines - 1 - count, lines - (turn + 1) // 2)
        part = jnp.where(turn <= tail, (turn - 1) % 2, jnp.where(first, turn - tail - 1, jnp.where(turn == tail + 3, 1, (turn - 1) % 2)))
        is_sum = (count > 0) & jnp.logical_not(is_block) & (ahead > 0)
        return is_block, is_sum, back, ahead, part

    def held(at, part, piece):
        inner = (at == line + 2 * toward) & (part == 1)
        outer = (at == line + (lines - 1) * toward) & (part == 0)
        return jnp.where(at_end, outer, inner) if piece else jnp.logical_not(at_end) & inner

    def late_sum(turn, piece, count):
        return (count == lines - 2) & (turn == 2 * lines - 3) & (piece == 1)

    def send_late(way, count, to_line, to):
        @pl.when(count == lines - 2)
        def _():
            z_copy(way, to_line, column, 1, to).start()

    def slot(turn, piece):
        is_block, is_sum, back, ahead, part = arrivals(turn, below_count)

        @pl.when(is_block)
        def _():
            spread(line - back, part, piece, has_above, UP, above)

        @pl.when(is_sum)
        def _():
            pass_on(0, line + ahead, part, piece, above, late_sum(turn, piece, below_count))

        is_block_, is_sum_, back_, ahead_, part_ = arrivals(turn, above_count)

        @pl.when(is_block_)
        def _():
            spread(line + back_, part_, piece, has_below, DOWN, below)

        @pl.when(is_sum_)
        def _():
            pass_on(1, line - ahead_, part_, piece, below, late_sum(turn, piece, above_count))

        if turn == 2 * lines - 2 and piece == 1:
            send_late(0, below_count, lines - 1, above)
            send_late(1, above_count, 0, below)

    def line_total(piece, after=None):
        col = column_at(piece)
        mate_sent(line, col)
        for part, span in spans():
            total[col, span] = chip_sum(line, col, span)

            @pl.when(has_below)
            def _():
                z_arrived(0, line, col, part)
                total[col, span] += z_in[0, line, col, span].astype(F32)

            @pl.when(has_above)
            def _():
                z_arrived(1, line, col, part)
                total[col, span] += z_in[1, line, col, span].astype(F32)

            if after is not None:
                after(part, span)

    def y_copy(part, span):
        return copy(y_out.at[span], y_in.at[span], send_sem.at[TOTALS], y_recv.at[part], across)

    def send_across(part, span):
        y_out[span] = total[other, span].astype(BF16)
        y_copy(part, span).start()

    group = results.shape[2]
    fanout = owner_ref.shape[0]
    owners = results.shape[1]

    def make_picks():
        spread = lax.broadcasted_iota(jnp.int32, (rows * fanout, fanout), 0) % fanout
        spread = jnp.where(spread == lax.broadcasted_iota(jnp.int32, (rows * fanout, fanout), 1), 1.0, 0.0)
        named = dot(spread.astype(BF16), owner_ref[...].astype(F32).astype(BF16), NN)
        own_row = lax.broadcasted_iota(jnp.int32, named.shape, 0) // fanout
        at_row = own_row == lax.broadcasted_iota(jnp.int32, named.shape, 1)
        named = jnp.sum(jnp.where(at_row, named, 0.0), axis=1, keepdims=True)
        shape = (group * fanout, owners * group)
        of_row = lax.broadcasted_iota(jnp.int32, shape, 0) // fanout
        of_col = lax.broadcasted_iota(jnp.int32, shape, 1)
        same = of_row == of_col % group
        col_owner = (of_col // group).astype(F32)
        for g in range(rows // group):
            chosen = named[g * group * fanout : (g + 1) * group * fanout, :] == col_owner
            picks[g] = jnp.where(same & chosen, 1.0, 0.0).astype(BF16)

    peers = 2 + jnp.where(has_above, 1, 0) + jnp.where(has_below, 1, 0)
    with jax.named_scope("greet"):
        pl.semaphore_wait(barrier, peers)

    def pair_copy(part, rows_from):
        span = pl.ds(rows_from, num_vec - rows_from)
        there = pair.at[core, part, span]
        return copy(there, there, send_sem.at[PAIR], pair_recv.at[part], mate)

    def pair_arrived(part, rows_from):
        span = pl.ds(rows_from, num_vec - rows_from)
        there = pair.at[1 - core, part, span]
        copy(there, there, send_sem.at[PAIR], pair_recv.at[part], mate).wait_recv()

    def each_part(act, first, second):
        @pl.when(core == 0)
        def _():
            for part in range(2):
                act(part, first)

        @pl.when(core == 1)
        def _():
            for part in range(2):
                act(part, second)

    load_own.wait()
    each_part(lambda part, rows_from: pair_copy(part, rows_from).start(), half, 0)
    load_mom.wait()
    fill_phases(mom_ref, cos_ref, sin_ref, me * local_sites)
    def own_lefts():
        mine_rows = pl.ds(pl.multiple_of(core * half, half), half)
        return jnp.concatenate([pair[0, 0, mine_rows, :], pair[0, 1, mine_rows, :]], axis=0)

    def own_block(by_re, by_im):
        gath[chip, core, 0] = (by_re[:half] + by_im[half:]).astype(BF16)
        gath[chip, core, 1] = (by_re[half:] - by_im[:half]).astype(BF16)

    @pl.when(core == 1)
    def _():
        with jax.named_scope("pair"):
            pair_arrived(0, half)
            pair_arrived(1, half)
        with jax.named_scope("block"):
            lefts = own_lefts()
            own_block(dot(lefts, pair[1, 0], NT), dot(lefts, pair[1, 1], NT))

    @pl.when(core == 0)
    def _():
        with jax.named_scope("pair"):
            pair_arrived(0, 0)
        with jax.named_scope("block"):
            lefts = own_lefts()
            by_re = dot(lefts, pair[1, 0], NT)
            pair_arrived(1, 0)
            own_block(by_re, dot(lefts, pair[1, 1], NT))

    def send_own(part, piece):
        @pl.when(has_above)
        def _():
            gather_copy(chip, part, piece, UP, above).start()

        @pl.when(has_below)
        def _():
            gather_copy(chip, part, piece, DOWN, below).start()

    for piece in range(2):
        send_own(0, piece)
        gather_copy(chip, 0, piece, ACROSS, across).start()
    for piece in range(2):

        @pl.when(jnp.logical_not(at_end))
        def _():
            send_own(1, piece)

        gather_copy(chip, 1, piece, ACROSS, across).start()

    def named_product(step, piece):
        with jax.named_scope(f"unit{step}{piece}"):
            product_at(step, piece)

    def named_slot(turn, piece):
        with jax.named_scope(f"slot{turn}{piece}"):
            slot(turn, piece)
            relay(turn - 1, piece)

    with jax.named_scope("load"):
        load_vec.wait()
    named_product(0, 0)
    named_product(0, 1)
    begin(0, 0)
    named_product(1, 0)
    begin(0, 1)

    for piece in range(2):

        @pl.when(at_end)
        def _():
            send_own(1, piece)

        for part in range(parts):
            gather_copy(chip, part, piece, MATE, mate).start()

    named_slot(1, 0)
    named_product(1, 1)
    named_slot(1, 1)
    named_product(2, 0)
    begin(1, 0)
    begin(1, 1)
    named_slot(2, 0)
    named_product(2, 1)
    named_slot(2, 1)
    named_product(3, 0)
    begin(2, 0)
    begin(2, 1)
    named_slot(3, 0)
    named_product(3, 1)
    named_slot(3, 1)
    load_owner.wait()
    with jax.named_scope("picks"):
        make_picks()
    for turn in range(4, 7):
        for piece in range(2):
            named_slot(turn, piece)
    def send_held(part, span):
        if part == 0:
            gather_copy(farthest, 1, 0, ACROSS, across).start()

    farthest = nth_line(lines - 1) * wide + column

    @pl.when(at_end)
    def _():
        with jax.named_scope("total0"):
            line_total(0, send_across)

    with jax.named_scope("slot7"):
        for piece in range(2):
            slot(2 * lines - 1, piece)

    @pl.when(at_end)
    def _():
        relay(2 * lines - 2, 0)
        with jax.named_scope("total1"):
            line_total(1)

    @pl.when(jnp.logical_not(at_end))
    def _():
        with jax.named_scope("total0"):
            line_total(0, send_across)
        with jax.named_scope("rel6"):
            for piece in range(2):
                relay(2 * lines - 2, piece)
        inward = (line - toward) * wide + other
        outward = (line + 2 * toward) * wide + other

        @pl.when(lower)
        def _():
            gather_copy(inward, 1, 1, UP, above).start()
            gather_copy(outward, 0, 1, DOWN, below).start()

        @pl.when(jnp.logical_not(lower))
        def _():
            gather_copy(inward, 1, 1, DOWN, below).start()
            gather_copy(outward, 0, 1, UP, above).start()

        with jax.named_scope("total1"):
            line_total(1, send_held)

    with jax.named_scope("across"):
        for part, span in spans():
            y_copy(part, span).wait_recv()
    row = (total[column] + y_in[...].astype(F32)).astype(BF16)
    row_re = row[:, :num_vec]
    row_im = row[:, num_vec:]
    lhs[0, :rows] = jnp.concatenate([row_re, -row_im], axis=1)
    lhs[0, rows:] = jnp.concatenate([row_im, row_re], axis=1)
    lhs[1, :rows] = row
    lhs[1, rows:] = jnp.concatenate([row_im, -row_re], axis=1)

    def put(owner, re, im):
        sixteen = results.shape[2]
        results[:, owner, :, :num_vec] = re.astype(BF16).reshape(rows // sixteen, sixteen, num_vec)
        results[:, owner, :, num_vec:] = im.astype(BF16).reshape(rows // sixteen, sixteen, num_vec)

    def contract(block):
        high = jnp.concatenate([gath[block, 0, 0], gath[block, 1, 0], gath[block, 0, 1], gath[block, 1, 1]], axis=0)
        by = dot(lhs[0], high, NN)
        put(2 * block, by[:rows], by[rows:])
        broad = [jnp.concatenate([gath[block, which, 0], gath[block, which, 1]], axis=1) for which in range(2)]
        by = dot(lhs[1], jnp.concatenate(broad, axis=0), NT)
        put(2 * block + 1, by[:rows], by[rows:])

    def block_at(turn):
        return nth_line(turn // 2) * wide + jnp.where(turn % 2 == 0, column, other)

    def relay_last():
        with jax.named_scope("last"):

            @pl.when(at_end)
            def _():
                relay(2 * lines - 2, 1)

            for piece in range(2):
                relay(2 * lines - 1, piece)

    early = [block_at(turn) for turn in range(2 * lines - 2)]
    with jax.named_scope("mate"):
        early_from_mate()
    with jax.named_scope("contract"):
        for block in early:
            contract(block)
    relay_last()

    def contract_at(turn):
        block = block_at(turn)
        with jax.named_scope("mate"):
            from_mate(block)
        with jax.named_scope("contract"):
            contract(block)

    contract_at(2 * lines - 2)

    def all_sent(what, way):
        copy(what, what, send_sem.at[way], core_recv.at[0], mate).wait_send()

    @pl.when(core == 0)
    def _():
        all_sent(pair.at[0, :, pl.ds(half, half)], PAIR)

    @pl.when(core == 1)
    def _():
        all_sent(pair.at[1], PAIR)

    all_sent(core_out, CORES)
    all_sent(z_out.at[pl.ds(0, lines - 1)], LINES)
    all_sent(y_out, TOTALS)

    def pieces_sent(count, way):
        all_sent(results.at[pl.ds(0, half // (4 * group)), pl.ds(0, count)], way)

    pieces_sent(4 * lines - 1, ACROSS)
    for count in range(1, lines):

        @pl.when(line == count - 1)
        def _():
            pieces_sent(4 * count + (1 if count > 1 else 0), UP)

        @pl.when(line == lines - count)
        def _():
            pieces_sent(4 * count + (1 if count > 1 else 0), DOWN)

    contract_at(2 * lines - 1)
    all_sent(gath.at[:, core], MATE)

def pick_kernel(results, picks, out_hbm, out, sems):
    groups, owners, group, width = results.shape
    fanout = out.shape[1]
    copies = []
    for g in range(groups):
        part = slice(g * group, (g + 1) * group)
        picked = dot(picks[g], results[g].reshape(owners * group, width), NN)
        out[part] = picked.reshape(group, fanout, width).astype(BF16)
        copies.append(pltpu.make_async_copy(out.at[part], out_hbm.at[part], sems.at[g]))
        copies[-1].start()
    for each in copies:
        each.wait()


def fused_on_device(eigvecs, momenta, peram, graph):
    num_vec, colours, local_sites = eigvecs.shape[1:]
    spaces = lax.axis_size("space")
    wide = 2
    lines = spaces // (2 * wide)
    chips = lines * wide
    rows, fanout = graph.shape
    group = 16
    vectors = jnp.transpose(eigvecs, (0, 2, 1, 3))
    half = num_vec // 2
    dma = pltpu.SemaphoreType.DMA
    groups = rows // group
    results, picks = pl.pallas_call(
        functools.partial(fused_kernel, lines, wide),
        out_shape=(
            pltpu.VMEM((groups, spaces, group, 2 * num_vec), BF16),
            pltpu.VMEM((groups, group * fanout, spaces * group), BF16),
        ),
        in_specs=[pl.BlockSpec(memory_space=pltpu.HBM)] * 4,
        out_specs=[pl.BlockSpec(memory_space=pltpu.VMEM)] * 2,
        scratch_shapes=[
            pltpu.SMEM(momenta.shape, jnp.int32),
            pltpu.VMEM((2, colours, num_vec, local_sites), BF16),
            pltpu.VMEM((fanout, rows), jnp.int32),
            pltpu.VMEM((momenta.shape[0], local_sites), F32),
            pltpu.VMEM((momenta.shape[0], local_sites), F32),
            pltpu.VMEM((2, 2, num_vec, num_vec), BF16),
            pltpu.VMEM((chips, 2, 2, half, num_vec), BF16),
            pltpu.VMEM((2 * rows, 2 * num_vec), F32),
            pltpu.VMEM((chips, rows, 2 * num_vec), F32),
            pltpu.VMEM((chips, rows, 2 * num_vec), BF16),
            pltpu.VMEM((chips, rows, 2 * num_vec), BF16),
            pltpu.VMEM((lines, wide, rows, 2 * num_vec), BF16),
            pltpu.VMEM((2, lines, wide, rows, 2 * num_vec), BF16),
            pltpu.VMEM((wide, rows, 2 * num_vec), F32),
            pltpu.VMEM((rows, 2 * num_vec), BF16),
            pltpu.VMEM((rows, 2 * num_vec), BF16),
            pltpu.VMEM((2, 2 * rows, 2 * num_vec), BF16),
            dma((4,)),
            dma((8,)),
            dma((2,)),
            dma((chips,)),
            dma((lines + 1, wide, 2)),
            dma((2,)),
            dma((chips, 2, 2)),
            dma((3,)),
        ],
        compiler_params=pltpu.CompilerParams(
            collective_id=0, has_side_effects=True, vmem_limit_bytes=VMEM_ROOM + (16 << 20)
        ),
    )(momenta, vectors, peram[0], graph.T)
    return pl.pallas_call(
        pick_kernel,
        out_shape=jax.ShapeDtypeStruct((rows, fanout, 2 * num_vec), BF16),
        in_specs=[pl.BlockSpec(memory_space=pltpu.VMEM)] * 2,
        out_specs=pl.BlockSpec(memory_space=pltpu.HBM),
        scratch_shapes=[pltpu.VMEM((rows, fanout, 2 * num_vec), BF16), dma((groups,))],
    )(
        pltpu.with_memory_space_constraint(results, pltpu.VMEM),
        pltpu.with_memory_space_constraint(picks, pltpu.VMEM),
    )


def fits(mesh, eigvecs, momenta, graph):
    num_vec = eigvecs.shape[1]
    spaces = mesh.shape["space"]
    rows = momenta.shape[0] * num_vec // spaces
    return (
        spaces == 16
        and rows % 16 == 0
        and num_vec % (2 * rows) == 0
        and num_vec % 128 == 0
        and spaces * 2 * num_vec * num_vec + 14 * spaces * rows * 2 * num_vec <= VMEM_ROOM
    )


def solution(mesh):
    placed = (
        P(None, None, None, ("groups", "space")),
        P(),
        P(("groups", "space"), None, None, None),
        P(("groups", "space"), None),
    )

    def whole(eigvecs, momenta, peram, graph):
        body = fused_on_device if fits(mesh, eigvecs, momenta, graph) else on_device
        return jax.shard_map(
            body,
            mesh=mesh,
            in_specs=placed,
            out_specs=P(("groups", "space"), None, None),
            check_vma=False,
        )(eigvecs, momenta, peram, graph)

    return whole
```

```python
import functools
import math

import jax
import jax.numpy as jnp
from jax import lax
from jax.experimental import pallas as pl
from jax.experimental.pallas import tpu as pltpu
from jax.sharding import PartitionSpec as P

EXTENT = 128
VMEM_ROOM = 40 << 20
BF16 = jnp.bfloat16
F32 = jnp.float32


def partner(block, axis, bit):
    count = lax.axis_size(axis)
    route = []
    for low in range(count):
        high = low | 1 << bit
        if high != low and high < count:
            route += [(low, high), (high, low)]
    return lax.ppermute(block, axis, route)


def phase_tables(momenta, site_index, extent):
    coord_x = site_index % extent
    coord_y = site_index // extent % extent
    coord_z = site_index // (extent * extent)
    wave_number = (
        momenta[:, 0:1] * coord_x[None, :]
        + momenta[:, 1:2] * coord_y[None, :]
        + momenta[:, 2:3] * coord_z[None, :]
    )
    wave_number = jnp.mod(wave_number, extent)
    phase_angle = wave_number.astype(jnp.float32) * (2.0 * math.pi / extent)
    return (jnp.cos(phase_angle), jnp.sin(phase_angle))


def block_form(peram_pair):
    peram_re = peram_pair[0]
    peram_im = peram_pair[1]
    top_half = jnp.concatenate([peram_re, peram_im], axis=1)
    bottom_half = jnp.concatenate([-peram_im, peram_re], axis=1)
    return jnp.concatenate([top_half, bottom_half], axis=0)


def sink_product(arrived, block):
    return lax.dot_general(
        arrived, block, (((2,), (0,)), ((), ())), preferred_element_type=jnp.float32
    ).astype(jnp.bfloat16)


def adjoint_product(sinks, block):
    return lax.dot_general(
        sinks, block, (((2,), (1,)), ((), ())), preferred_element_type=jnp.float32
    ).astype(jnp.bfloat16)


def on_device(eigvecs, momenta, peram, graph):
    num_vec = eigvecs.shape[1]
    local_sites = eigvecs.shape[3]
    spaces = lax.axis_size("space")
    position = lax.axis_index("space")
    site_index = position * local_sites + jnp.arange(local_sites, dtype=jnp.int32)
    cosine, sine = phase_tables(momenta, site_index, EXTENT)
    total_rows = cosine.shape[0] * num_vec
    rows_here = total_rows // spaces
    right_side = jnp.concatenate(
        [
            jnp.concatenate([eigvecs[0], -eigvecs[1]], axis=1),
            jnp.concatenate([eigvecs[1], eigvecs[0]], axis=1),
        ],
        axis=0,
    ).reshape(2 * num_vec, 6 * local_sites)
    row_index = jnp.arange(rows_here * lax.axis_size("space"), dtype=jnp.int32)
    vector_index = row_index % num_vec
    momentum_index = row_index // num_vec
    vec_re = jnp.take(eigvecs[0], vector_index, axis=0).astype(jnp.float32)
    vec_im = jnp.take(eigvecs[1], vector_index, axis=0).astype(jnp.float32)
    cos_rows = jnp.take(cosine, momentum_index, axis=0)[:, None, :]
    sin_rows = jnp.take(sine, momentum_index, axis=0)[:, None, :]
    left_re = vec_re * cos_rows - vec_im * sin_rows
    left_im = -(vec_re * sin_rows + vec_im * cos_rows)
    left_cat = (
        jnp.concatenate([left_re, left_im], axis=1)
        .astype(jnp.bfloat16)
        .reshape(rows_here * lax.axis_size("space"), 6 * local_sites)
    )
    summed = lax.psum_scatter(
        lax.dot_general(
            left_cat, right_side, (((1,), (1,)), ((), ())), preferred_element_type=jnp.float32
        ),
        "space",
        scatter_dimension=0,
        tiled=True,
    )
    elemental = summed.astype(jnp.bfloat16)
    fanout = graph.shape[1]
    capacity = max(2, 2 * rows_here * fanout // spaces)
    flat_owner = graph.reshape(-1)
    entries = flat_owner.shape[0]
    onehot = (flat_owner[:, None] == jnp.arange(spaces, dtype=jnp.int32)[None, :]).astype(jnp.int32)
    earlier = jnp.cumsum(onehot, axis=0) - onehot
    slot = jnp.sum(earlier * onehot, axis=1)
    source_row = jnp.arange(entries, dtype=jnp.int32) // fanout
    payload = jnp.take(elemental, source_row, axis=0)
    outgoing = (
        jnp.zeros((spaces, capacity, 2 * num_vec), jnp.bfloat16).at[flat_owner, slot].set(payload)
    )
    own_block = block_form(peram[0])
    partner_block = partner(own_block, "space", 0)
    sinks = sink_product(
        lax.all_to_all(outgoing, "space", split_axis=0, concat_axis=0, tiled=True), own_block
    )
    finished = adjoint_product(sinks, partner_block)
    returned = lax.all_to_all(finished, "space", split_axis=0, concat_axis=0, tiled=True)
    collected = returned[flat_owner, slot]
    return collected.reshape(rows_here, fanout, 2 * num_vec)


NT = (((1,), (1,)), ((), ()))
NN = (((1,), (0,)), ((), ()))


def dot(a, b, dims):
    return lax.dot_general(a, b, dims, preferred_element_type=F32)


def fill_phases(mom_ref, cos_ref, sin_ref, first_site):
    count = cos_ref.shape[0]
    shape = (1, cos_ref.shape[1])
    bits = EXTENT.bit_length() - 1
    site = first_site + lax.broadcasted_iota(jnp.int32, shape, 1)
    coord_x = site & (EXTENT - 1)
    coord_y = (site >> bits) & (EXTENT - 1)
    coord_z = site >> (2 * bits)
    for q in range(count):
        wave = (mom_ref[q, 0] * coord_x + mom_ref[q, 1] * coord_y + mom_ref[q, 2] * coord_z) & (EXTENT - 1)
        angle = wave.astype(F32) * (2.0 * math.pi / EXTENT)
        cos_ref[q : q + 1, :] = jnp.cos(angle)
        sin_ref[q : q + 1, :] = jnp.sin(angle)


def fused_kernel(
    lines, wide, mom_hbm, vec_hbm, peram_hbm, owner_hbm, results, picks,
    mom_ref, vec_ref, owner_ref, cos_ref, sin_ref, pair, gath, prod, own, core_out, core_in, z_out, z_in, total, y_out, y_in,
    lhs, load_sem, send_sem, pair_recv, core_recv, z_recv, y_recv, gath_recv, mate_recv,
):
    colours, num_vec, local_sites = vec_ref.shape[1:]
    rows = own.shape[1]
    half = num_vec // 2
    me = lax.axis_index("space")
    core = me % 2
    chip = me // 2
    line = chip // wide
    column = chip % wide
    mate = chip * 2 + 1 - core
    other = 1 - column
    across = (line * wide + other) * 2 + core
    above = me + 2 * wide
    below = me - 2 * wide
    has_above = line < lines - 1
    has_below = line > 0

    def copy(src, dst, send, recv, to):
        return pltpu.make_async_remote_copy(
            src_ref=src, dst_ref=dst, send_sem=send, recv_sem=recv,
            device_id={"space": to}, device_id_type=pl.DeviceIdType.MESH,
        )

    barrier = pltpu.get_barrier_semaphore()

    def greet(to):
        pl.semaphore_signal(barrier, inc=1, device_id={"space": to}, device_id_type=pl.DeviceIdType.MESH)

    greet(mate)
    greet(across)

    @pl.when(has_above)
    def _():
        greet(above)

    @pl.when(has_below)
    def _():
        greet(below)

    loads = [
        pltpu.make_async_copy(src, dst, load_sem.at[place])
        for place, (src, dst) in enumerate(
            [(mom_hbm, mom_ref), (peram_hbm, pair.at[core]), (vec_hbm, vec_ref), (owner_hbm, owner_ref)]
        )
    ]
    load_mom, load_own, load_vec, load_owner = loads
    load_own.start()
    load_mom.start()
    UP, ACROSS, MATE, DOWN, CORES, LINES, TOTALS, PAIR = range(8)

    def core_copy(unit):
        return copy(core_out.at[unit], core_in.at[unit], send_sem.at[CORES], core_recv.at[unit], mate)

    def unit_product(unit):
        first = unit * (2 * rows)
        momentum = first // num_vec
        start = pl.multiple_of(first % num_vec, 2 * rows)
        cosine = cos_ref[pl.ds(momentum, 1), :]
        sine = sin_ref[pl.ds(momentum, 1), :]
        left = []
        for colour in range(colours):
            v_re = vec_ref[0, colour, pl.ds(start, 2 * rows), :].astype(F32)
            v_im = vec_ref[1, colour, pl.ds(start, 2 * rows), :].astype(F32)
            left_re = (v_re * cosine - v_im * sine).astype(BF16)
            left_im = (-(v_re * sine + v_im * cosine)).astype(BF16)
            left.append(jnp.concatenate([left_re, left_im], axis=0))
        left = jnp.concatenate(left, axis=1)
        by_re = dot(left, jnp.concatenate([vec_ref[0, colour] for colour in range(colours)], axis=1), NT)
        by_im = dot(left, jnp.concatenate([vec_ref[1, colour] for colour in range(colours)], axis=1), NT)
        prod[:, :num_vec] = by_re[: 2 * rows] - by_im[2 * rows :]
        prod[:, num_vec:] = by_im[: 2 * rows] + by_re[2 * rows :]
        own[unit] = prod[pl.ds(pl.multiple_of(core * rows, rows), rows), :]
        core_out[unit] = prod[pl.ds(pl.multiple_of((1 - core) * rows, rows), rows), :].astype(BF16)

    lower = line < lines // 2
    below_count = line
    above_count = lines - 1 - line
    at_end = (line == 0) | (line == lines - 1)
    toward = jnp.where(lower, 1, -1)

    def line_at(step):
        if step == lines - 1:
            return line
        down = lines - 1 - step
        down = jnp.where(down <= line, down - 1, down)
        up = jnp.where(step >= line, step + 1, step)
        return jnp.where(lower, down, up)

    def column_at(piece):
        return jnp.where(piece == 0, other, column)

    def product_at(step, piece):
        unit = line_at(step) * wide + column_at(piece)
        unit_product(unit)
        core_copy(unit).start()

    share = rows // 2

    def z_copy(way, to_line, col, piece, to):
        span = pl.ds(piece * share, share)
        return copy(
            z_out.at[to_line, col, span], z_in.at[way, to_line, col, span],
            send_sem.at[LINES], z_recv.at[z_place(way, to_line, line + (1 - 2 * way)), col, piece], to,
        )

    def z_place(way, to_line, at):
        return jnp.where(to_line == at, lines, to_line) if way else to_line

    def z_arrived(way, to_line, col, piece):
        span = pl.ds(piece * share, share)
        copy(
            z_out.at[to_line, col, span], z_in.at[way, to_line, col, span],
            send_sem.at[LINES], z_recv.at[z_place(way, to_line, line), col, piece], mate,
        ).wait_recv()

    def chip_sum(to_line, col, span):
        unit = to_line * wide + col
        return own[unit, span] + core_in[unit, span].astype(F32)

    def mate_sent(to_line, col):
        core_copy(to_line * wide + col).wait_recv()

    def spans():
        return [(piece, pl.ds(piece * share, share)) for piece in range(2)]

    def begin(step, piece):
        to_line = line_at(step)
        col = column_at(piece)

        def send(way, to):
            mate_sent(to_line, col)
            for part, span in spans():
                z_out[to_line, col, span] = chip_sum(to_line, col, span).astype(BF16)
                z_copy(way, to_line, col, part, to).start()

        @pl.when(line == 0)
        def _():
            send(0, above)

        @pl.when(line == lines - 1)
        def _():
            send(1, below)

    def pass_on(way, to_line, piece, part, to, wait):
        col = column_at(piece)
        if part == 0:
            mate_sent(to_line, col)
        span = pl.ds(part * share, share)
        z_arrived(way, to_line, col, part)
        before = z_in[way, to_line, col, span].astype(F32)
        z_out[to_line, col, span] = (chip_sum(to_line, col, span) + before).astype(BF16)

        @pl.when(jnp.logical_not(wait))
        def _():
            z_copy(way, to_line, col, part, to).start()

    parts = gath.shape[2]

    def gather_copy(block, part, piece, way, to):
        there = gath.at[block, core, part, pl.ds(piece * (half // 2), half // 2)]
        recv = mate_recv.at[mate_place(block)] if way == MATE else gath_recv.at[block, part, piece]
        return copy(there, there, send_sem.at[way], recv, to)

    def gather_arrived(block, part, piece):
        gather_copy(block, part, piece, ACROSS, across).wait_recv()

    def mate_place(block):
        far = line + toward * jnp.where(at_end, lines - 1, 2)
        return jnp.where(block // wide != far, 0, jnp.where(block % wide == column, 1, 2))

    def from_mate(block):
        there = gath.at[block, 1 - core]
        copy(there, there, send_sem.at[MATE], mate_recv.at[mate_place(block)], mate).wait_recv()

    def early_from_mate():
        there = gath.at[pl.ds(0, wide * (lines - 1)), 1 - core]
        copy(there, there, send_sem.at[MATE], mate_recv.at[0], mate).wait_recv()

    def spread(at, part, piece, onward, way, to):
        block = at * wide + column
        gather_arrived(block, part, piece)

        @pl.when(onward)
        def _():
            gather_copy(block, part, piece, way, to).start()

        @pl.when(jnp.logical_not(held(at, part, piece)))
        def _():
            gather_copy(block, part, piece, ACROSS, across).start()

        gather_copy(block, part, piece, MATE, mate).start()

    def nth_line(turn):
        inner = jnp.where(turn == 2, -1, jnp.where(turn == 3, 2, turn))
        return line + toward * jnp.where(at_end, turn, inner)

    def relay(nth, piece):
        ends = toward * (nth // 2)
        inner = [0, 0, -1, 1, toward, 2 * toward, -toward, 2 * toward][nth]
        part = jnp.where(at_end, nth % 2, [0, 1, 0, 0, 1, 0, 1, 1][nth])
        block = (line + jnp.where(at_end, ends, inner)) * wide + other
        gather_arrived(block, part, piece)
        gather_copy(block, part, piece, MATE, mate).start()

    def arrivals(turn, count):
        tail = 2 * count - 1
        first = (turn == tail + 1) | (turn == tail + 2)
        last_piece = jnp.where(count == lines - 1, 2, 3)
        is_block = (count > 0) & ((turn <= tail) | (turn == tail + last_piece))
        back = jnp.where(turn < tail, (turn + 1) // 2, count)
        ahead = jnp.where(first, lines - 1 - count, lines - (turn + 1) // 2)
        part = jnp.where(turn <= tail, (turn - 1) % 2, jnp.where(first, turn - tail - 1, jnp.where(turn == tail + 3, 1, (turn - 1) % 2)))
        is_sum = (count > 0) & jnp.logical_not(is_block) & (ahead > 0)
        return is_block, is_sum, back, ahead, part

    def held(at, part, piece):
        inner = (at == line + 2 * toward) & (part == 1)
        outer = (at == line + (lines - 1) * toward) & (part == 0)
        return jnp.where(at_end, outer, inner) if piece else jnp.logical_not(at_end) & inner

    def late_sum(turn, piece, count):
        return (count == lines - 2) & (turn == 2 * lines - 3) & (piece == 1)

    def send_late(way, count, to_line, to):
        @pl.when(count == lines - 2)
        def _():
            z_copy(way, to_line, column, 1, to).start()

    def slot(turn, piece):
        is_block, is_sum, back, ahead, part = arrivals(turn, below_count)

        @pl.when(is_block)
        def _():
            spread(line - back, part, piece, has_above, UP, above)

        @pl.when(is_sum)
        def _():
            pass_on(0, line + ahead, part, piece, above, late_sum(turn, piece, below_count))

        is_block_, is_sum_, back_, ahead_, part_ = arrivals(turn, above_count)

        @pl.when(is_block_)
        def _():
            spread(line + back_, part_, piece, has_below, DOWN, below)

        @pl.when(is_sum_)
        def _():
            pass_on(1, line - ahead_, part_, piece, below, late_sum(turn, piece, above_count))

        if turn == 2 * lines - 2 and piece == 1:
            send_late(0, below_count, lines - 1, above)
            send_late(1, above_count, 0, below)

    def line_total(piece, after=None):
        col = column_at(piece)
        mate_sent(line, col)
        for part, span in spans():
            total[col, span] = chip_sum(line, col, span)

            @pl.when(has_below)
            def _():
                z_arrived(0, line, col, part)
                total[col, span] += z_in[0, line, col, span].astype(F32)

            @pl.when(has_above)
            def _():
                z_arrived(1, line, col, part)
                total[col, span] += z_in[1, line, col, span].astype(F32)

            if after is not None:
                after(part, span)

    def y_copy(part, span):
        return copy(y_out.at[span], y_in.at[span], send_sem.at[TOTALS], y_recv.at[part], across)

    def send_across(part, span):
        y_out[span] = total[other, span].astype(BF16)
        y_copy(part, span).start()

    group = results.shape[2]
    fanout = owner_ref.shape[0]
    owners = results.shape[1]

    def make_picks():
        spread = lax.broadcasted_iota(jnp.int32, (rows * fanout, fanout), 0) % fanout
        spread = jnp.where(spread == lax.broadcasted_iota(jnp.int32, (rows * fanout, fanout), 1), 1.0, 0.0)
        named = dot(spread.astype(BF16), owner_ref[...].astype(F32).astype(BF16), NN)
        own_row = lax.broadcasted_iota(jnp.int32, named.shape, 0) // fanout
        at_row = own_row == lax.broadcasted_iota(jnp.int32, named.shape, 1)
        named = jnp.sum(jnp.where(at_row, named, 0.0), axis=1, keepdims=True)
        shape = (group * fanout, owners * group)
        of_row = lax.broadcasted_iota(jnp.int32, shape, 0) // fanout
        of_col = lax.broadcasted_iota(jnp.int32, shape, 1)
        same = of_row == of_col % group
        col_owner = (of_col // group).astype(F32)
        for g in range(rows // group):
            chosen = named[g * group * fanout : (g + 1) * group * fanout, :] == col_owner
            picks[g] = jnp.where(same & chosen, 1.0, 0.0).astype(BF16)

    peers = 2 + jnp.where(has_above, 1, 0) + jnp.where(has_below, 1, 0)
    load_own.wait()
    load_vec.start()
    load_owner.start()
    with jax.named_scope("greet"):
        pl.semaphore_wait(barrier, peers)

    def pair_copy(part, rows_from):
        span = pl.ds(rows_from, num_vec - rows_from)
        there = pair.at[core, part, span]
        return copy(there, there, send_sem.at[PAIR], pair_recv.at[part], mate)

    def pair_arrived(part, rows_from):
        span = pl.ds(rows_from, num_vec - rows_from)
        there = pair.at[1 - core, part, span]
        copy(there, there, send_sem.at[PAIR], pair_recv.at[part], mate).wait_recv()

    def each_part(act, first, second):
        @pl.when(core == 0)
        def _():
            for part in range(2):
                act(part, first)

        @pl.when(core == 1)
        def _():
            for part in range(2):
                act(part, second)

    each_part(lambda part, rows_from: pair_copy(part, rows_from).start(), half, 0)
    load_mom.wait()
    fill_phases(mom_ref, cos_ref, sin_ref, me * local_sites)
    def own_lefts():
        mine_rows = pl.ds(pl.multiple_of(core * half, half), half)
        return jnp.concatenate([pair[0, 0, mine_rows, :], pair[0, 1, mine_rows, :]], axis=0)

    def own_block(by_re, by_im):
        gath[chip, core, 0] = (by_re[:half] + by_im[half:]).astype(BF16)
        gath[chip, core, 1] = (by_re[half:] - by_im[:half]).astype(BF16)

    @pl.when(core == 1)
    def _():
        with jax.named_scope("pair"):
            pair_arrived(0, half)
            pair_arrived(1, half)
        with jax.named_scope("block"):
            lefts = own_lefts()
            own_block(dot(lefts, pair[1, 0], NT), dot(lefts, pair[1, 1], NT))

    @pl.when(core == 0)
    def _():
        with jax.named_scope("pair"):
            pair_arrived(0, 0)
        with jax.named_scope("block"):
            lefts = own_lefts()
            by_re = dot(lefts, pair[1, 0], NT)
            pair_arrived(1, 0)
            own_block(by_re, dot(lefts, pair[1, 1], NT))

    def send_own(part, piece):
        @pl.when(has_above)
        def _():
            gather_copy(chip, part, piece, UP, above).start()

        @pl.when(has_below)
        def _():
            gather_copy(chip, part, piece, DOWN, below).start()

    for piece in range(2):
        send_own(0, piece)
        gather_copy(chip, 0, piece, ACROSS, across).start()
    for piece in range(2):

        @pl.when(jnp.logical_not(at_end))
        def _():
            send_own(1, piece)

        gather_copy(chip, 1, piece, ACROSS, across).start()

    def named_product(step, piece):
        with jax.named_scope(f"unit{step}{piece}"):
            product_at(step, piece)

    def named_slot(turn, piece):
        with jax.named_scope(f"slot{turn}{piece}"):
            slot(turn, piece)
            relay(turn - 1, piece)

    with jax.named_scope("load"):
        load_vec.wait()
    named_product(0, 0)
    named_product(0, 1)
    begin(0, 0)
    named_product(1, 0)
    begin(0, 1)

    for piece in range(2):

        @pl.when(at_end)
        def _():
            send_own(1, piece)

        for part in range(parts):
            gather_copy(chip, part, piece, MATE, mate).start()

    named_slot(1, 0)
    named_product(1, 1)
    named_slot(1, 1)
    named_product(2, 0)
    begin(1, 0)
    begin(1, 1)
    named_slot(2, 0)
    named_product(2, 1)
    named_slot(2, 1)
    named_product(3, 0)
    begin(2, 0)
    begin(2, 1)
    named_slot(3, 0)
    named_product(3, 1)
    named_slot(3, 1)
    load_owner.wait()
    with jax.named_scope("picks"):
        make_picks()
    for turn in range(4, 7):
        for piece in range(2):
            named_slot(turn, piece)
    def send_held(part, span):
        if part == 0:
            gather_copy(farthest, 1, 0, ACROSS, across).start()

    farthest = nth_line(lines - 1) * wide + column

    @pl.when(at_end)
    def _():
        with jax.named_scope("total0"):
            line_total(0, send_across)

    with jax.named_scope("slot7"):
        for piece in range(2):
            slot(2 * lines - 1, piece)

    @pl.when(at_end)
    def _():
        relay(2 * lines - 2, 0)
        with jax.named_scope("total1"):
            line_total(1)

    @pl.when(jnp.logical_not(at_end))
    def _():
        with jax.named_scope("total0"):
            line_total(0, send_across)
        with jax.named_scope("rel6"):
            for piece in range(2):
                relay(2 * lines - 2, piece)
        inward = (line - toward) * wide + other
        outward = (line + 2 * toward) * wide + other

        @pl.when(lower)
        def _():
            gather_copy(inward, 1, 1, UP, above).start()
            gather_copy(outward, 0, 1, DOWN, below).start()

        @pl.when(jnp.logical_not(lower))
        def _():
            gather_copy(inward, 1, 1, DOWN, below).start()
            gather_copy(outward, 0, 1, UP, above).start()

        with jax.named_scope("total1"):
            line_total(1, send_held)

    with jax.named_scope("across"):
        for part, span in spans():
            y_copy(part, span).wait_recv()
    row = (total[column] + y_in[...].astype(F32)).astype(BF16)
    row_re = row[:, :num_vec]
    row_im = row[:, num_vec:]
    lhs[0, :rows] = jnp.concatenate([row_re, -row_im], axis=1)
    lhs[0, rows:] = jnp.concatenate([row_im, row_re], axis=1)
    lhs[1, :rows] = row
    lhs[1, rows:] = jnp.concatenate([row_im, -row_re], axis=1)

    def put(owner, re, im):
        sixteen = results.shape[2]
        results[:, owner, :, :num_vec] = re.astype(BF16).reshape(rows // sixteen, sixteen, num_vec)
        results[:, owner, :, num_vec:] = im.astype(BF16).reshape(rows // sixteen, sixteen, num_vec)

    def contract(block):
        high = jnp.concatenate([gath[block, 0, 0], gath[block, 1, 0], gath[block, 0, 1], gath[block, 1, 1]], axis=0)
        by = dot(lhs[0], high, NN)
        put(2 * block, by[:rows], by[rows:])
        broad = [jnp.concatenate([gath[block, which, 0], gath[block, which, 1]], axis=1) for which in range(2)]
        by = dot(lhs[1], jnp.concatenate(broad, axis=0), NT)
        put(2 * block + 1, by[:rows], by[rows:])

    def block_at(turn):
        return nth_line(turn // 2) * wide + jnp.where(turn % 2 == 0, column, other)

    def relay_last():
        with jax.named_scope("last"):

            @pl.when(at_end)
            def _():
                relay(2 * lines - 2, 1)

            for piece in range(2):
                relay(2 * lines - 1, piece)

    early = [block_at(turn) for turn in range(2 * lines - 2)]
    with jax.named_scope("mate"):
        early_from_mate()
    with jax.named_scope("contract"):
        for block in early:
            contract(block)
    relay_last()

    def contract_at(turn):
        block = block_at(turn)
        with jax.named_scope("mate"):
            from_mate(block)
        with jax.named_scope("contract"):
            contract(block)

    contract_at(2 * lines - 2)

    def all_sent(what, way):
        copy(what, what, send_sem.at[way], core_recv.at[0], mate).wait_send()

    @pl.when(core == 0)
    def _():
        all_sent(pair.at[0, :, pl.ds(half, half)], PAIR)

    @pl.when(core == 1)
    def _():
        all_sent(pair.at[1], PAIR)

    all_sent(core_out, CORES)
    all_sent(z_out.at[pl.ds(0, lines - 1)], LINES)
    all_sent(y_out, TOTALS)

    def pieces_sent(count, way):
        all_sent(results.at[pl.ds(0, half // (4 * group)), pl.ds(0, count)], way)

    pieces_sent(4 * lines - 1, ACROSS)
    for count in range(1, lines):

        @pl.when(line == count - 1)
        def _():
            pieces_sent(4 * count + (1 if count > 1 else 0), UP)

        @pl.when(line == lines - count)
        def _():
            pieces_sent(4 * count + (1 if count > 1 else 0), DOWN)

    contract_at(2 * lines - 1)
    all_sent(gath.at[:, core], MATE)

def pick_kernel(results, picks, out_hbm, out, sems):
    groups, owners, group, width = results.shape
    fanout = out.shape[1]
    copies = []
    for g in range(groups):
        part = slice(g * group, (g + 1) * group)
        picked = dot(picks[g], results[g].reshape(owners * group, width), NN)
        out[part] = picked.reshape(group, fanout, width).astype(BF16)
        copies.append(pltpu.make_async_copy(out.at[part], out_hbm.at[part], sems.at[g]))
        copies[-1].start()
    for each in copies:
        each.wait()


def fused_on_device(eigvecs, momenta, peram, graph):
    num_vec, colours, local_sites = eigvecs.shape[1:]
    spaces = lax.axis_size("space")
    wide = 2
    lines = spaces // (2 * wide)
    chips = lines * wide
    rows, fanout = graph.shape
    group = 16
    vectors = jnp.transpose(eigvecs, (0, 2, 1, 3))
    half = num_vec // 2
    dma = pltpu.SemaphoreType.DMA
    groups = rows // group
    results, picks = pl.pallas_call(
        functools.partial(fused_kernel, lines, wide),
        out_shape=(
            pltpu.VMEM((groups, spaces, group, 2 * num_vec), BF16),
            pltpu.VMEM((groups, group * fanout, spaces * group), BF16),
        ),
        in_specs=[pl.BlockSpec(memory_space=pltpu.HBM)] * 4,
        out_specs=[pl.BlockSpec(memory_space=pltpu.VMEM)] * 2,
        scratch_shapes=[
            pltpu.SMEM(momenta.shape, jnp.int32),
            pltpu.VMEM((2, colours, num_vec, local_sites), BF16),
            pltpu.VMEM((fanout, rows), jnp.int32),
            pltpu.VMEM((momenta.shape[0], local_sites), F32),
            pltpu.VMEM((momenta.shape[0], local_sites), F32),
            pltpu.VMEM((2, 2, num_vec, num_vec), BF16),
            pltpu.VMEM((chips, 2, 2, half, num_vec), BF16),
            pltpu.VMEM((2 * rows, 2 * num_vec), F32),
            pltpu.VMEM((chips, rows, 2 * num_vec), F32),
            pltpu.VMEM((chips, rows, 2 * num_vec), BF16),
            pltpu.VMEM((chips, rows, 2 * num_vec), BF16),
            pltpu.VMEM((lines, wide, rows, 2 * num_vec), BF16),
            pltpu.VMEM((2, lines, wide, rows, 2 * num_vec), BF16),
            pltpu.VMEM((wide, rows, 2 * num_vec), F32),
            pltpu.VMEM((rows, 2 * num_vec), BF16),
            pltpu.VMEM((rows, 2 * num_vec), BF16),
            pltpu.VMEM((2, 2 * rows, 2 * num_vec), BF16),
            dma((4,)),
            dma((8,)),
            dma((2,)),
            dma((chips,)),
            dma((lines + 1, wide, 2)),
            dma((2,)),
            dma((chips, 2, 2)),
            dma((3,)),
        ],
        compiler_params=pltpu.CompilerParams(
            collective_id=0, has_side_effects=True, vmem_limit_bytes=VMEM_ROOM + (16 << 20)
        ),
    )(momenta, vectors, peram[0], graph.T)
    return pl.pallas_call(
        pick_kernel,
        out_shape=jax.ShapeDtypeStruct((rows, fanout, 2 * num_vec), BF16),
        in_specs=[pl.BlockSpec(memory_space=pltpu.VMEM)] * 2,
        out_specs=pl.BlockSpec(memory_space=pltpu.HBM),
        scratch_shapes=[pltpu.VMEM((rows, fanout, 2 * num_vec), BF16), dma((groups,))],
    )(
        pltpu.with_memory_space_constraint(results, pltpu.VMEM),
        pltpu.with_memory_space_constraint(picks, pltpu.VMEM),
    )


def fits(mesh, eigvecs, momenta, graph):
    num_vec = eigvecs.shape[1]
    spaces = mesh.shape["space"]
    rows = momenta.shape[0] * num_vec // spaces
    return (
        spaces == 16
        and rows % 16 == 0
        and num_vec % (2 * rows) == 0
        and num_vec % 128 == 0
        and spaces * 2 * num_vec * num_vec + 14 * spaces * rows * 2 * num_vec <= VMEM_ROOM
    )


def solution(mesh):
    placed = (
        P(None, None, None, ("groups", "space")),
        P(),
        P(("groups", "space"), None, None, None),
        P(("groups", "space"), None),
    )

    def whole(eigvecs, momenta, peram, graph):
        body = fused_on_device if fits(mesh, eigvecs, momenta, graph) else on_device
        return jax.shard_map(
            body,
            mesh=mesh,
            in_specs=placed,
            out_specs=P(("groups", "space"), None, None),
            check_vma=False,
        )(eigvecs, momenta, peram, graph)

    return whole
```

```python
import functools
import math

import jax
import jax.numpy as jnp
from jax import lax
from jax.experimental import pallas as pl
from jax.experimental.pallas import tpu as pltpu
from jax.sharding import PartitionSpec as P

EXTENT = 128
VMEM_ROOM = 40 << 20
BF16 = jnp.bfloat16
F32 = jnp.float32


def partner(block, axis, bit):
    count = lax.axis_size(axis)
    route = []
    for low in range(count):
        high = low | 1 << bit
        if high != low and high < count:
            route += [(low, high), (high, low)]
    return lax.ppermute(block, axis, route)


def phase_tables(momenta, site_index, extent):
    coord_x = site_index % extent
    coord_y = site_index // extent % extent
    coord_z = site_index // (extent * extent)
    wave_number = (
        momenta[:, 0:1] * coord_x[None, :]
        + momenta[:, 1:2] * coord_y[None, :]
        + momenta[:, 2:3] * coord_z[None, :]
    )
    wave_number = jnp.mod(wave_number, extent)
    phase_angle = wave_number.astype(jnp.float32) * (2.0 * math.pi / extent)
    return (jnp.cos(phase_angle), jnp.sin(phase_angle))


def block_form(peram_pair):
    peram_re = peram_pair[0]
    peram_im = peram_pair[1]
    top_half = jnp.concatenate([peram_re, peram_im], axis=1)
    bottom_half = jnp.concatenate([-peram_im, peram_re], axis=1)
    return jnp.concatenate([top_half, bottom_half], axis=0)


def sink_product(arrived, block):
    return lax.dot_general(
        arrived, block, (((2,), (0,)), ((), ())), preferred_element_type=jnp.float32
    ).astype(jnp.bfloat16)


def adjoint_product(sinks, block):
    return lax.dot_general(
        sinks, block, (((2,), (1,)), ((), ())), preferred_element_type=jnp.float32
    ).astype(jnp.bfloat16)


def on_device(eigvecs, momenta, peram, graph):
    num_vec = eigvecs.shape[1]
    local_sites = eigvecs.shape[3]
    spaces = lax.axis_size("space")
    position = lax.axis_index("space")
    site_index = position * local_sites + jnp.arange(local_sites, dtype=jnp.int32)
    cosine, sine = phase_tables(momenta, site_index, EXTENT)
    total_rows = cosine.shape[0] * num_vec
    rows_here = total_rows // spaces
    right_side = jnp.concatenate(
        [
            jnp.concatenate([eigvecs[0], -eigvecs[1]], axis=1),
            jnp.concatenate([eigvecs[1], eigvecs[0]], axis=1),
        ],
        axis=0,
    ).reshape(2 * num_vec, 6 * local_sites)
    row_index = jnp.arange(rows_here * lax.axis_size("space"), dtype=jnp.int32)
    vector_index = row_index % num_vec
    momentum_index = row_index // num_vec
    vec_re = jnp.take(eigvecs[0], vector_index, axis=0).astype(jnp.float32)
    vec_im = jnp.take(eigvecs[1], vector_index, axis=0).astype(jnp.float32)
    cos_rows = jnp.take(cosine, momentum_index, axis=0)[:, None, :]
    sin_rows = jnp.take(sine, momentum_index, axis=0)[:, None, :]
    left_re = vec_re * cos_rows - vec_im * sin_rows
    left_im = -(vec_re * sin_rows + vec_im * cos_rows)
    left_cat = (
        jnp.concatenate([left_re, left_im], axis=1)
        .astype(jnp.bfloat16)
        .reshape(rows_here * lax.axis_size("space"), 6 * local_sites)
    )
    summed = lax.psum_scatter(
        lax.dot_general(
            left_cat, right_side, (((1,), (1,)), ((), ())), preferred_element_type=jnp.float32
        ),
        "space",
        scatter_dimension=0,
        tiled=True,
    )
    elemental = summed.astype(jnp.bfloat16)
    fanout = graph.shape[1]
    capacity = max(2, 2 * rows_here * fanout // spaces)
    flat_owner = graph.reshape(-1)
    entries = flat_owner.shape[0]
    onehot = (flat_owner[:, None] == jnp.arange(spaces, dtype=jnp.int32)[None, :]).astype(jnp.int32)
    earlier = jnp.cumsum(onehot, axis=0) - onehot
    slot = jnp.sum(earlier * onehot, axis=1)
    source_row = jnp.arange(entries, dtype=jnp.int32) // fanout
    payload = jnp.take(elemental, source_row, axis=0)
    outgoing = (
        jnp.zeros((spaces, capacity, 2 * num_vec), jnp.bfloat16).at[flat_owner, slot].set(payload)
    )
    own_block = block_form(peram[0])
    partner_block = partner(own_block, "space", 0)
    sinks = sink_product(
        lax.all_to_all(outgoing, "space", split_axis=0, concat_axis=0, tiled=True), own_block
    )
    finished = adjoint_product(sinks, partner_block)
    returned = lax.all_to_all(finished, "space", split_axis=0, concat_axis=0, tiled=True)
    collected = returned[flat_owner, slot]
    return collected.reshape(rows_here, fanout, 2 * num_vec)


NT = (((1,), (1,)), ((), ()))
NN = (((1,), (0,)), ((), ()))


def dot(a, b, dims):
    return lax.dot_general(a, b, dims, preferred_element_type=F32)


def fill_phases(mom_ref, cos_ref, sin_ref, first_site):
    count = cos_ref.shape[0]
    shape = (1, cos_ref.shape[1])
    bits = EXTENT.bit_length() - 1
    site = first_site + lax.broadcasted_iota(jnp.int32, shape, 1)
    coord_x = site & (EXTENT - 1)
    coord_y = (site >> bits) & (EXTENT - 1)
    coord_z = site >> (2 * bits)
    for q in range(count):
        wave = (mom_ref[q, 0] * coord_x + mom_ref[q, 1] * coord_y + mom_ref[q, 2] * coord_z) & (EXTENT - 1)
        angle = wave.astype(F32) * (2.0 * math.pi / EXTENT)
        cos_ref[q : q + 1, :] = jnp.cos(angle)
        sin_ref[q : q + 1, :] = jnp.sin(angle)


def fused_kernel(
    lines, wide, mom_hbm, vec_hbm, peram_hbm, owner_hbm, results, picks,
    mom_ref, vec_ref, owner_ref, cos_ref, sin_ref, pair, gath, prod, own, core_out, core_in, z_out, z_in, total, y_out, y_in,
    lhs, load_sem, send_sem, pair_recv, core_recv, z_recv, y_recv, gath_recv, mate_recv,
):
    colours, num_vec, local_sites = vec_ref.shape[1:]
    rows = own.shape[1]
    half = num_vec // 2
    me = lax.axis_index("space")
    core = me % 2
    chip = me // 2
    line = chip // wide
    column = chip % wide
    mate = chip * 2 + 1 - core
    other = 1 - column
    across = (line * wide + other) * 2 + core
    above = me + 2 * wide
    below = me - 2 * wide
    has_above = line < lines - 1
    has_below = line > 0

    def copy(src, dst, send, recv, to):
        return pltpu.make_async_remote_copy(
            src_ref=src, dst_ref=dst, send_sem=send, recv_sem=recv,
            device_id={"space": to}, device_id_type=pl.DeviceIdType.MESH,
        )

    barrier = pltpu.get_barrier_semaphore()

    def greet(to):
        pl.semaphore_signal(barrier, inc=1, device_id={"space": to}, device_id_type=pl.DeviceIdType.MESH)

    greet(mate)
    greet(across)

    @pl.when(has_above)
    def _():
        greet(above)

    @pl.when(has_below)
    def _():
        greet(below)

    loads = [
        pltpu.make_async_copy(src, dst, load_sem.at[place])
        for place, (src, dst) in enumerate(
            [(mom_hbm, mom_ref), (peram_hbm, pair.at[core]), (vec_hbm, vec_ref), (owner_hbm, owner_ref)]
        )
    ]
    for load in loads:
        load.start()
    load_mom, load_own, load_vec, load_owner = loads
    UP, ACROSS, MATE, DOWN, CORES, LINES, TOTALS, PAIR = range(8)

    def core_copy(unit):
        return copy(core_out.at[unit], core_in.at[unit], send_sem.at[CORES], core_recv.at[unit], mate)

    def unit_product(unit):
        first = unit * (2 * rows)
        momentum = first // num_vec
        start = pl.multiple_of(first % num_vec, 2 * rows)
        cosine = cos_ref[pl.ds(momentum, 1), :]
        sine = sin_ref[pl.ds(momentum, 1), :]
        left = []
        for colour in range(colours):
            v_re = vec_ref[0, colour, pl.ds(start, 2 * rows), :].astype(F32)
            v_im = vec_ref[1, colour, pl.ds(start, 2 * rows), :].astype(F32)
            left_re = (v_re * cosine - v_im * sine).astype(BF16)
            left_im = (-(v_re * sine + v_im * cosine)).astype(BF16)
            left.append(jnp.concatenate([left_re, left_im], axis=0))
        left = jnp.concatenate(left, axis=1)
        by_re = dot(left, jnp.concatenate([vec_ref[0, colour] for colour in range(colours)], axis=1), NT)
        by_im = dot(left, jnp.concatenate([vec_ref[1, colour] for colour in range(colours)], axis=1), NT)
        prod[:, :num_vec] = by_re[: 2 * rows] - by_im[2 * rows :]
        prod[:, num_vec:] = by_im[: 2 * rows] + by_re[2 * rows :]
        own[unit] = prod[pl.ds(pl.multiple_of(core * rows, rows), rows), :]
        core_out[unit] = prod[pl.ds(pl.multiple_of((1 - core) * rows, rows), rows), :].astype(BF16)

    lower = line < lines // 2
    below_count = line
    above_count = lines - 1 - line
    at_end = (line == 0) | (line == lines - 1)
    toward = jnp.where(lower, 1, -1)

    def line_at(step):
        if step == lines - 1:
            return line
        down = lines - 1 - step
        down = jnp.where(down <= line, down - 1, down)
        up = jnp.where(step >= line, step + 1, step)
        return jnp.where(lower, down, up)

    def column_at(piece):
        return jnp.where(piece == 0, other, column)

    def product_at(step, piece):
        unit = line_at(step) * wide + column_at(piece)
        unit_product(unit)
        core_copy(unit).start()

    share = rows // 2

    def z_copy(way, to_line, col, piece, to):
        span = pl.ds(piece * share, share)
        return copy(
            z_out.at[to_line, col, span], z_in.at[way, to_line, col, span],
            send_sem.at[LINES], z_recv.at[z_place(way, to_line, line + (1 - 2 * way)), col, piece], to,
        )

    def z_place(way, to_line, at):
        return jnp.where(to_line == at, lines, to_line) if way else to_line

    def z_arrived(way, to_line, col, piece):
        span = pl.ds(piece * share, share)
        copy(
            z_out.at[to_line, col, span], z_in.at[way, to_line, col, span],
            send_sem.at[LINES], z_recv.at[z_place(way, to_line, line), col, piece], mate,
        ).wait_recv()

    def chip_sum(to_line, col, span):
        unit = to_line * wide + col
        return own[unit, span] + core_in[unit, span].astype(F32)

    def mate_sent(to_line, col):
        core_copy(to_line * wide + col).wait_recv()

    def spans():
        return [(piece, pl.ds(piece * share, share)) for piece in range(2)]

    def begin(step, piece):
        to_line = line_at(step)
        col = column_at(piece)

        def send(way, to):
            mate_sent(to_line, col)
            for part, span in spans():
                z_out[to_line, col, span] = chip_sum(to_line, col, span).astype(BF16)
                z_copy(way, to_line, col, part, to).start()

        @pl.when(line == 0)
        def _():
            send(0, above)

        @pl.when(line == lines - 1)
        def _():
            send(1, below)

    def pass_on(way, to_line, piece, part, to, wait):
        col = column_at(piece)
        if part == 0:
            mate_sent(to_line, col)
        span = pl.ds(part * share, share)
        z_arrived(way, to_line, col, part)
        before = z_in[way, to_line, col, span].astype(F32)
        z_out[to_line, col, span] = (chip_sum(to_line, col, span) + before).astype(BF16)

        @pl.when(jnp.logical_not(wait))
        def _():
            z_copy(way, to_line, col, part, to).start()

    parts = gath.shape[2]

    def gather_copy(block, part, piece, way, to):
        there = gath.at[block, core, part, pl.ds(piece * (half // 2), half // 2)]
        recv = mate_recv.at[mate_place(block)] if way == MATE else gath_recv.at[block, part, piece]
        return copy(there, there, send_sem.at[way], recv, to)

    def gather_arrived(block, part, piece):
        gather_copy(block, part, piece, ACROSS, across).wait_recv()

    def mate_place(block):
        far = line + toward * jnp.where(at_end, lines - 1, 2)
        return jnp.where(block // wide != far, 0, jnp.where(block % wide == column, 1, 2))

    def from_mate(block):
        there = gath.at[block, 1 - core]
        copy(there, there, send_sem.at[MATE], mate_recv.at[mate_place(block)], mate).wait_recv()

    def early_from_mate():
        there = gath.at[pl.ds(0, wide * (lines - 1)), 1 - core]
        copy(there, there, send_sem.at[MATE], mate_recv.at[0], mate).wait_recv()

    def spread(at, part, piece, onward, way, to):
        block = at * wide + column
        gather_arrived(block, part, piece)

        @pl.when(onward)
        def _():
            gather_copy(block, part, piece, way, to).start()

        @pl.when(jnp.logical_not(held(at, part, piece)))
        def _():
            gather_copy(block, part, piece, ACROSS, across).start()

        gather_copy(block, part, piece, MATE, mate).start()

    def nth_line(turn):
        inner = jnp.where(turn == 2, -1, jnp.where(turn == 3, 2, turn))
        return line + toward * jnp.where(at_end, turn, inner)

    def relay(nth, piece):
        ends = toward * (nth // 2)
        inner = [0, 0, -1, 1, toward, 2 * toward, -toward, 2 * toward][nth]
        part = jnp.where(at_end, nth % 2, [0, 1, 0, 0, 1, 0, 1, 1][nth])
        block = (line + jnp.where(at_end, ends, inner)) * wide + other
        gather_arrived(block, part, piece)
        gather_copy(block, part, piece, MATE, mate).start()

    def arrivals(turn, count):
        tail = 2 * count - 1
        first = (turn == tail + 1) | (turn == tail + 2)
        last_piece = jnp.where(count == lines - 1, 2, 3)
        is_block = (count > 0) & ((turn <= tail) | (turn == tail + last_piece))
        back = jnp.where(turn < tail, (turn + 1) // 2, count)
        ahead = jnp.where(first, lines - 1 - count, lines - (turn + 1) // 2)
        part = jnp.where(turn <= tail, (turn - 1) % 2, jnp.where(first, turn - tail - 1, jnp.where(turn == tail + 3, 1, (turn - 1) % 2)))
        is_sum = (count > 0) & jnp.logical_not(is_block) & (ahead > 0)
        return is_block, is_sum, back, ahead, part

    def held(at, part, piece):
        inner = (at == line + 2 * toward) & (part == 1)
        outer = (at == line + (lines - 1) * toward) & (part == 0)
        return jnp.where(at_end, outer, inner) if piece else jnp.logical_not(at_end) & inner

    def late_sum(turn, piece, count):
        return (count == lines - 2) & (turn == 2 * lines - 3) & (piece == 1)

    def send_late(way, count, to_line, to):
        @pl.when(count == lines - 2)
        def _():
            z_copy(way, to_line, column, 1, to).start()

    def slot(turn, piece):
        is_block, is_sum, back, ahead, part = arrivals(turn, below_count)

        @pl.when(is_block)
        def _():
            spread(line - back, part, piece, has_above, UP, above)

        @pl.when(is_sum)
        def _():
            pass_on(0, line + ahead, part, piece, above, late_sum(turn, piece, below_count))

        is_block_, is_sum_, back_, ahead_, part_ = arrivals(turn, above_count)

        @pl.when(is_block_)
        def _():
            spread(line + back_, part_, piece, has_below, DOWN, below)

        @pl.when(is_sum_)
        def _():
            pass_on(1, line - ahead_, part_, piece, below, late_sum(turn, piece, above_count))

        if turn == 2 * lines - 2 and piece == 1:
            send_late(0, below_count, lines - 1, above)
            send_late(1, above_count, 0, below)

    def line_total(piece, after=None):
        col = column_at(piece)
        mate_sent(line, col)
        for part, span in spans():
            total[col, span] = chip_sum(line, col, span)

            @pl.when(has_below)
            def _():
                z_arrived(0, line, col, part)
                total[col, span] += z_in[0, line, col, span].astype(F32)

            @pl.when(has_above)
            def _():
                z_arrived(1, line, col, part)
                total[col, span] += z_in[1, line, col, span].astype(F32)

            if after is not None:
                after(part, span)

    def y_copy(part, span):
        return copy(y_out.at[span], y_in.at[span], send_sem.at[TOTALS], y_recv.at[part], across)

    def send_across(part, span):
        y_out[span] = total[other, span].astype(BF16)
        y_copy(part, span).start()

    group = results.shape[2]
    fanout = owner_ref.shape[0]
    owners = results.shape[1]

    def make_picks():
        spread = lax.broadcasted_iota(jnp.int32, (rows * fanout, fanout), 0) % fanout
        spread = jnp.where(spread == lax.broadcasted_iota(jnp.int32, (rows * fanout, fanout), 1), 1.0, 0.0)
        named = dot(spread.astype(BF16), owner_ref[...].astype(F32).astype(BF16), NN)
        own_row = lax.broadcasted_iota(jnp.int32, named.shape, 0) // fanout
        at_row = own_row == lax.broadcasted_iota(jnp.int32, named.shape, 1)
        named = jnp.sum(jnp.where(at_row, named, 0.0), axis=1, keepdims=True)
        shape = (group * fanout, owners * group)
        of_row = lax.broadcasted_iota(jnp.int32, shape, 0) // fanout
        of_col = lax.broadcasted_iota(jnp.int32, shape, 1)
        same = of_row == of_col % group
        col_owner = (of_col // group).astype(F32)
        for g in range(rows // group):
            chosen = named[g * group * fanout : (g + 1) * group * fanout, :] == col_owner
            picks[g] = jnp.where(same & chosen, 1.0, 0.0).astype(BF16)

    peers = 2 + jnp.where(has_above, 1, 0) + jnp.where(has_below, 1, 0)
    with jax.named_scope("greet"):
        pl.semaphore_wait(barrier, peers)

    def pair_copy(part, rows_from):
        span = pl.ds(rows_from, num_vec - rows_from)
        there = pair.at[core, part, span]
        return copy(there, there, send_sem.at[PAIR], pair_recv.at[part], mate)

    def pair_arrived(part, rows_from):
        span = pl.ds(rows_from, num_vec - rows_from)
        there = pair.at[1 - core, part, span]
        copy(there, there, send_sem.at[PAIR], pair_recv.at[part], mate).wait_recv()

    def each_part(act, first, second):
        @pl.when(core == 0)
        def _():
            for part in range(2):
                act(part, first)

        @pl.when(core == 1)
        def _():
            for part in range(2):
                act(part, second)

    load_own.wait()
    each_part(lambda part, rows_from: pair_copy(part, rows_from).start(), half, 0)
    load_mom.wait()
    fill_phases(mom_ref, cos_ref, sin_ref, me * local_sites)
    def own_lefts():
        mine_rows = pl.ds(pl.multiple_of(core * half, half), half)
        return jnp.concatenate([pair[0, 0, mine_rows, :], pair[0, 1, mine_rows, :]], axis=0)

    def own_block(by_re, by_im):
        gath[chip, core, 0] = (by_re[:half] + by_im[half:]).astype(BF16)
        gath[chip, core, 1] = (by_re[half:] - by_im[:half]).astype(BF16)

    @pl.when(core == 1)
    def _():
        with jax.named_scope("pair"):
            pair_arrived(0, half)
            pair_arrived(1, half)
        with jax.named_scope("block"):
            lefts = own_lefts()
            own_block(dot(lefts, pair[1, 0], NT), dot(lefts, pair[1, 1], NT))

    @pl.when(core == 0)
    def _():
        with jax.named_scope("pair"):
            pair_arrived(0, 0)
        with jax.named_scope("block"):
            lefts = own_lefts()
            by_re = dot(lefts, pair[1, 0], NT)
            pair_arrived(1, 0)
            own_block(by_re, dot(lefts, pair[1, 1], NT))

    def send_own(part, piece):
        @pl.when(has_above)
        def _():
            gather_copy(chip, part, piece, UP, above).start()

        @pl.when(has_below)
        def _():
            gather_copy(chip, part, piece, DOWN, below).start()

    for piece in range(2):
        send_own(0, piece)
        gather_copy(chip, 0, piece, ACROSS, across).start()
    for piece in range(2):

        @pl.when(jnp.logical_not(at_end))
        def _():
            send_own(1, piece)

        gather_copy(chip, 1, piece, ACROSS, across).start()

    def named_product(step, piece):
        with jax.named_scope(f"unit{step}{piece}"):
            product_at(step, piece)

    def named_slot(turn, piece):
        with jax.named_scope(f"slot{turn}{piece}"):
            slot(turn, piece)
            relay(turn - 1, piece)

    with jax.named_scope("load"):
        load_vec.wait()
    named_product(0, 0)
    named_product(0, 1)
    begin(0, 0)
    named_product(1, 0)
    begin(0, 1)

    for piece in range(2):

        @pl.when(at_end)
        def _():
            send_own(1, piece)

        for part in range(parts):
            gather_copy(chip, part, piece, MATE, mate).start()

    named_slot(1, 0)
    named_product(1, 1)
    named_slot(1, 1)
    named_product(2, 0)
    begin(1, 0)
    begin(1, 1)
    named_slot(2, 0)
    named_product(2, 1)
    named_slot(2, 1)
    named_product(3, 0)
    begin(2, 0)
    begin(2, 1)
    named_slot(3, 0)
    named_product(3, 1)
    named_slot(3, 1)
    load_owner.wait()
    with jax.named_scope("picks"):
        make_picks()
    for turn in range(4, 7):
        for piece in range(2):
            named_slot(turn, piece)
    def send_held(part, span):
        if part == 0:
            gather_copy(farthest, 1, 0, ACROSS, across).start()

    farthest = nth_line(lines - 1) * wide + column

    @pl.when(at_end)
    def _():
        with jax.named_scope("total0"):
            line_total(0, send_across)

    with jax.named_scope("slot7"):
        for piece in range(2):
            slot(2 * lines - 1, piece)

    @pl.when(at_end)
    def _():
        relay(2 * lines - 2, 0)
        with jax.named_scope("total1"):
            line_total(1)

    @pl.when(jnp.logical_not(at_end))
    def _():
        with jax.named_scope("total0"):
            line_total(0, send_across)
        with jax.named_scope("rel6"):
            for piece in range(2):
                relay(2 * lines - 2, piece)
        inward = (line - toward) * wide + other
        outward = (line + 2 * toward) * wide + other

        @pl.when(lower)
        def _():
            gather_copy(inward, 1, 1, UP, above).start()
            gather_copy(outward, 0, 1, DOWN, below).start()

        @pl.when(jnp.logical_not(lower))
        def _():
            gather_copy(inward, 1, 1, DOWN, below).start()
            gather_copy(outward, 0, 1, UP, above).start()

        with jax.named_scope("total1"):
            line_total(1, send_held)

    with jax.named_scope("across"):
        for part, span in spans():
            y_copy(part, span).wait_recv()
    row = (total[column] + y_in[...].astype(F32)).astype(BF16)
    row_re = row[:, :num_vec]
    row_im = row[:, num_vec:]
    lhs[0, :rows] = jnp.concatenate([row_re, -row_im], axis=1)
    lhs[0, rows:] = jnp.concatenate([row_im, row_re], axis=1)
    lhs[1, :rows] = row
    lhs[1, rows:] = jnp.concatenate([row_im, -row_re], axis=1)

    def put(owner, re, im):
        sixteen = results.shape[2]
        results[:, owner, :, :num_vec] = re.astype(BF16).reshape(rows // sixteen, sixteen, num_vec)
        results[:, owner, :, num_vec:] = im.astype(BF16).reshape(rows // sixteen, sixteen, num_vec)

    def contract(block):
        high = jnp.concatenate([gath[block, 0, 0], gath[block, 1, 0], gath[block, 0, 1], gath[block, 1, 1]], axis=0)
        by = dot(lhs[0], high, NN)
        put(2 * block, by[:rows], by[rows:])
        broad = [jnp.concatenate([gath[block, which, 0], gath[block, which, 1]], axis=1) for which in range(2)]
        by = dot(lhs[1], jnp.concatenate(broad, axis=0), NT)
        put(2 * block + 1, by[:rows], by[rows:])

    def block_at(turn):
        return nth_line(turn // 2) * wide + jnp.where(turn % 2 == 0, column, other)

    def relay_last():
        with jax.named_scope("last"):

            relay(2 * lines - 1, 0)

            @pl.when(at_end)
            def _():
                relay(2 * lines - 2, 1)

            relay(2 * lines - 1, 1)

    early = [block_at(turn) for turn in range(2 * lines - 2)]
    with jax.named_scope("mate"):
        early_from_mate()
    with jax.named_scope("contract"):
        for block in early:
            contract(block)
    relay_last()

    def contract_at(turn):
        block = block_at(turn)
        with jax.named_scope("mate"):
            from_mate(block)
        with jax.named_scope("contract"):
            contract(block)

    contract_at(2 * lines - 2)

    def all_sent(what, way):
        copy(what, what, send_sem.at[way], core_recv.at[0], mate).wait_send()

    @pl.when(core == 0)
    def _():
        all_sent(pair.at[0, :, pl.ds(half, half)], PAIR)

    @pl.when(core == 1)
    def _():
        all_sent(pair.at[1], PAIR)

    all_sent(core_out, CORES)
    all_sent(z_out.at[pl.ds(0, lines - 1)], LINES)
    all_sent(y_out, TOTALS)

    def pieces_sent(count, way):
        all_sent(results.at[pl.ds(0, half // (4 * group)), pl.ds(0, count)], way)

    pieces_sent(4 * lines - 1, ACROSS)
    for count in range(1, lines):

        @pl.when(line == count - 1)
        def _():
            pieces_sent(4 * count + (1 if count > 1 else 0), UP)

        @pl.when(line == lines - count)
        def _():
            pieces_sent(4 * count + (1 if count > 1 else 0), DOWN)

    contract_at(2 * lines - 1)
    all_sent(gath.at[:, core], MATE)

def pick_kernel(results, picks, out_hbm, out, sems):
    groups, owners, group, width = results.shape
    fanout = out.shape[1]
    copies = []
    for g in range(groups):
        part = slice(g * group, (g + 1) * group)
        picked = dot(picks[g], results[g].reshape(owners * group, width), NN)
        out[part] = picked.reshape(group, fanout, width).astype(BF16)
        copies.append(pltpu.make_async_copy(out.at[part], out_hbm.at[part], sems.at[g]))
        copies[-1].start()
    for each in copies:
        each.wait()


def fused_on_device(eigvecs, momenta, peram, graph):
    num_vec, colours, local_sites = eigvecs.shape[1:]
    spaces = lax.axis_size("space")
    wide = 2
    lines = spaces // (2 * wide)
    chips = lines * wide
    rows, fanout = graph.shape
    group = 16
    vectors = jnp.transpose(eigvecs, (0, 2, 1, 3))
    half = num_vec // 2
    dma = pltpu.SemaphoreType.DMA
    groups = rows // group
    results, picks = pl.pallas_call(
        functools.partial(fused_kernel, lines, wide),
        out_shape=(
            pltpu.VMEM((groups, spaces, group, 2 * num_vec), BF16),
            pltpu.VMEM((groups, group * fanout, spaces * group), BF16),
        ),
        in_specs=[pl.BlockSpec(memory_space=pltpu.HBM)] * 4,
        out_specs=[pl.BlockSpec(memory_space=pltpu.VMEM)] * 2,
        scratch_shapes=[
            pltpu.SMEM(momenta.shape, jnp.int32),
            pltpu.VMEM((2, colours, num_vec, local_sites), BF16),
            pltpu.VMEM((fanout, rows), jnp.int32),
            pltpu.VMEM((momenta.shape[0], local_sites), F32),
            pltpu.VMEM((momenta.shape[0], local_sites), F32),
            pltpu.VMEM((2, 2, num_vec, num_vec), BF16),
            pltpu.VMEM((chips, 2, 2, half, num_vec), BF16),
            pltpu.VMEM((2 * rows, 2 * num_vec), F32),
            pltpu.VMEM((chips, rows, 2 * num_vec), F32),
            pltpu.VMEM((chips, rows, 2 * num_vec), BF16),
            pltpu.VMEM((chips, rows, 2 * num_vec), BF16),
            pltpu.VMEM((lines, wide, rows, 2 * num_vec), BF16),
            pltpu.VMEM((2, lines, wide, rows, 2 * num_vec), BF16),
            pltpu.VMEM((wide, rows, 2 * num_vec), F32),
            pltpu.VMEM((rows, 2 * num_vec), BF16),
            pltpu.VMEM((rows, 2 * num_vec), BF16),
            pltpu.VMEM((2, 2 * rows, 2 * num_vec), BF16),
            dma((4,)),
            dma((8,)),
            dma((2,)),
            dma((chips,)),
            dma((lines + 1, wide, 2)),
            dma((2,)),
            dma((chips, 2, 2)),
            dma((3,)),
        ],
        compiler_params=pltpu.CompilerParams(
            collective_id=0, has_side_effects=True, vmem_limit_bytes=VMEM_ROOM + (16 << 20)
        ),
    )(momenta, vectors, peram[0], graph.T)
    return pl.pallas_call(
        pick_kernel,
        out_shape=jax.ShapeDtypeStruct((rows, fanout, 2 * num_vec), BF16),
        in_specs=[pl.BlockSpec(memory_space=pltpu.VMEM)] * 2,
        out_specs=pl.BlockSpec(memory_space=pltpu.HBM),
        scratch_shapes=[pltpu.VMEM((rows, fanout, 2 * num_vec), BF16), dma((groups,))],
    )(
        pltpu.with_memory_space_constraint(results, pltpu.VMEM),
        pltpu.with_memory_space_constraint(picks, pltpu.VMEM),
    )


def fits(mesh, eigvecs, momenta, graph):
    num_vec = eigvecs.shape[1]
    spaces = mesh.shape["space"]
    rows = momenta.shape[0] * num_vec // spaces
    return (
        spaces == 16
        and rows % 16 == 0
        and num_vec % (2 * rows) == 0
        and num_vec % 128 == 0
        and spaces * 2 * num_vec * num_vec + 14 * spaces * rows * 2 * num_vec <= VMEM_ROOM
    )


def solution(mesh):
    placed = (
        P(None, None, None, ("groups", "space")),
        P(),
        P(("groups", "space"), None, None, None),
        P(("groups", "space"), None),
    )

    def whole(eigvecs, momenta, peram, graph):
        body = fused_on_device if fits(mesh, eigvecs, momenta, graph) else on_device
        return jax.shard_map(
            body,
            mesh=mesh,
            in_specs=placed,
            out_specs=P(("groups", "space"), None, None),
            check_vma=False,
        )(eigvecs, momenta, peram, graph)

    return whole
```
